128 devices in a mesh: lat: 8 (over x, core), lev: 16 (over y, z).
Axes of the slice: x: 4, y: 4, z: 4, core: 2. Of those that a mesh axis runs over, the one named last changes fastest.
Arguments:
- spectral: float32 [2, 128, 256, 256], P(None, 'lev', 'lat'), may hold values from -6 to 6
- background: bfloat16 [384, 768, 128], P('lat', 'lev'), may hold values from -6 to 6
- columns: int32 [128, 2048], P(('lat', 'lev')), may hold values from 0 to 2303
- counts: int32 [128], P(('lat', 'lev')), may hold values from 1 to 2048, 131072 in all
- radiances: bfloat16 [128, 2048, 512], P(('lat', 'lev')), may hold values from -6 to 6
- used_pairs: int32 [128, 2048], P(('lat', 'lev')), may hold values from 1 to 256
- channel_weight: float32 [512], replicated, may hold values from 0.25 to 4
- weight_in: bfloat16 [128, 1024], replicated, may hold values from -0.5 to 0.5
- weight_mid: bfloat16 [1024, 1024], replicated, may hold values from -0.1875 to 0.1875
- weight_out: bfloat16 [1024, 512], replicated, may hold values from -0.1875 to 0.1875
Outputs:
- spectral_grad: float32 [2, 128, 256, 256], P(None, 'lev', 'lat')
- grid_grad: float32 [384, 768, 128], P('lat', 'lev')
The draws below stay inside these ranges and needn't reach their ends.
Inputs may be any that keep to these rules, and one draw needn't show every extreme that they name: Entry [o, s] is the column of owner o's slot s inside o's region of 48 x 48 columns, numbered latitude-major; slots at or past counts[o] are unused. The counts sum to 131072, and the largest is exactly 2048. Block [o, s] uses channels 0 to 2 x used_pairs[o, s] - 1.
All inputs are finite; a program needn't handle non-finite values. No bound on the sum of `counts` on one device may be relied on, other than what follows from the above.
Results may differ from the reference program's by a relative error of at most 0.008.
Values may be sent and summed in bfloat16 or wider, within the bound.
No kernel may reach another device: no remote copies, remote signals or barrier semaphores. Data moves between devices by JAX's collectives and lax.ppermute only.
A program may use at most 128 MiB of HBM per device.

```python
import math
import jax
import jax.numpy as jnp
import numpy as np
from jax import lax

LEV = 128
M = 256
N = 256
NLAT = 384
NLON = 768
H1 = 1024
H2 = 1024
CHAN = 512
BLK_DEV = 1024
CAP = 2048
TOTAL = 131072
CLAT = 48
CLON = 48
N_LEV = 16
DEVICES = 128


def with_ends(array, rng, low, top_value):
    longest = array.shape.index(max(array.shape))
    spots = []
    for shift in (0, 1):
        where = [jax.random.randint(jax.random.fold_in(rng, axis), (), 0, length) for axis, length in enumerate(array.shape)]
        where[longest] = (where[longest] + shift) % array.shape[longest]
        spots.append(tuple(where))
    return array.at[spots[0]].set(low).at[spots[1]].set(top_value)


def shard_levels(rng, extent, shards, low, top_value):
    gain, own = 1.0, jax.random.fold_in(rng, 6)
    for axis_at, blocks in shards:
        steps = jnp.exp(jax.random.uniform(jax.random.fold_in(own, axis_at), (blocks,), jnp.float32, low / len(shards), top_value / len(shards)))
        gain = gain * jnp.repeat(steps, extent[axis_at] // blocks).reshape([-1 if axis == axis_at else 1 for axis in range(len(extent))])
    return gain


def split_up(count, total, bound, lean):
    portions = [(1 << 20) // math.isqrt(standing ** lean) + 1 for standing in range(2, count + 1)]
    rest, given = total - bound - (count - 1), [1] * (count - 1)
    while rest > 0:
        free = [i for i in range(count - 1) if given[i] < bound]
        pool, left = sum([portions[i] for i in free]), rest
        for i in free:
            addition = min(bound - given[i], max(1, left * portions[i] // pool), rest)
            given[i] = given[i] + addition
            rest = rest - addition
    return np.array([bound] + given)


def uneven(rng, count, total, reach, skew):
    if count == 2:
        one = jax.random.randint(rng, (), max(1, total - reach), min(reach, total - 1) + 1)
        return jnp.stack([one, total - one])
    tallies = jnp.asarray(split_up(count, total, reach, skew), jnp.int32)
    pairs = (count - 1) // 2
    source_of, sink = tallies[1:1 + 2 * pairs:2], tallies[2:2 + 2 * pairs:2]
    margin = jnp.minimum(source_of - 1, reach - sink)
    moved = jax.random.randint(jax.random.fold_in(rng, 1), (pairs,), 0, 1 << 20) % (margin + 1)
    tallies = tallies.at[1:1 + 2 * pairs:2].set(source_of - moved).at[2:2 + 2 * pairs:2].set(sink + moved)
    return tallies[jax.random.permutation(jax.random.fold_in(rng, 2), count)]


def scatter_about(rng, shape, deviation, reach, shards=(), held_as=jnp.bfloat16):
    values = deviation * jax.random.normal(rng, shape, jnp.float32)
    if shards:
        values = values * shard_levels(rng, shape, shards, -0.22, 0.18)
    return jnp.clip(values, -reach, reach).astype(held_as)


def setup_inputs(seed: int = 0) -> dict:
    keys = jax.random.split(jax.random.key(seed), 11)
    return {
        "spectral": scatter_about(keys[0], (2, LEV, M, N), 1.0, 6.0, ((1, 16), (2, 8)), jnp.float32),
        "background": scatter_about(keys[1], (NLAT, NLON, LEV), 1.0, 6.0, ((0, 8), (1, 16))),
        "columns": with_ends(jax.random.randint(keys[2], (DEVICES, CAP), 0, CLAT * CLON), jax.random.fold_in(keys[2], 1), 0, (CLAT * CLON) - 1).astype(jnp.int32),
        "counts": uneven(keys[3], DEVICES, TOTAL, CAP, 2).astype(jnp.int32),
        "radiances": scatter_about(keys[4], (DEVICES, CAP, CHAN), 1.0, 6.0, ((0, 128),)),
        "used_pairs": with_ends(jax.random.randint(keys[5], (DEVICES, CAP), 1, CHAN // 2 + 1), jax.random.fold_in(keys[5], 1), 1, (CHAN // 2 + 1) - 1).astype(jnp.int32),
        "channel_weight": jnp.clip(jnp.exp(jax.random.uniform(keys[6], (CHAN,), jnp.float32, math.log(0.25), math.log(4.0))), 0.25, 4.0),
        "weight_in": scatter_about(keys[7], (LEV, H1), LEV ** -0.5, 0.5),
        "weight_mid": scatter_about(keys[8], (H1, H2), H1 ** -0.5, 0.1875),
        "weight_out": scatter_about(keys[9], (H2, CHAN), H2 ** -0.5, 0.1875),
    }


RESCALE_TOP = 2.0 ** 60
RESCALE_BY = 2.0 ** (-60)
RESCALE_LOG = 60.0 * math.log(2.0)
HALF_LOG = 0.5 * math.log(0.5)

def legendre_table(orders, lat_total, degree_total):
    m_float = orders.astype(jnp.float32)
    lat_ids = jnp.arange(lat_total, dtype=jnp.float32)
    latitude = (0.5 - (lat_ids + 0.5) / lat_total) * jnp.pi
    sin_lat = jnp.sin(latitude)
    cos_lat = jnp.cos(latitude)
    order_ids = jnp.arange(1, degree_total, dtype=jnp.float32)
    log_steps = 0.5 * jnp.log((2.0 * order_ids + 1.0) / (2.0 * order_ids))
    log_norm = lax.optimization_barrier(jnp.sum(jnp.where(order_ids[None, :] <= m_float[:, None], log_steps[None, :], 0.0), axis=1))
    log_start = HALF_LOG + log_norm[:, None] + m_float[:, None] * jnp.log(cos_lat)[None, :]

    def advance(recur_state, degree):
        previous, earlier, shifts = recur_state
        n_float = degree.astype(jnp.float32)
        on_diagonal = (n_float == m_float)[:, None]
        next_diag = (n_float == m_float + 1.0)[:, None]
        beyond = (n_float > m_float + 1.0)[:, None]
        factor_a = jnp.sqrt(jnp.maximum(4.0 * n_float * n_float - 1.0, 1.0) / jnp.maximum(n_float * n_float - m_float * m_float, 1.0))
        lower = n_float - 1.0
        factor_b = jnp.sqrt(jnp.maximum(lower * lower - m_float * m_float, 0.0) / jnp.maximum(4.0 * lower * lower - 1.0, 1.0))
        current = jnp.where(beyond, factor_a[:, None] * (sin_lat[None, :] * previous - factor_b[:, None] * earlier), 0.0)
        current = jnp.where(next_diag, jnp.sqrt(2.0 * m_float + 3.0)[:, None] * sin_lat[None, :] * previous, current)
        current = jnp.where(on_diagonal, 1.0, current)
        oversized = jnp.abs(current) > RESCALE_TOP
        current = jnp.where(oversized, current * RESCALE_BY, current)
        previous = jnp.where(oversized, previous * RESCALE_BY, previous)
        shifts = shifts + oversized.astype(jnp.float32)
        values = current * jnp.exp(log_start + shifts * RESCALE_LOG)
        return ((current, previous, shifts), values)
    zeros = jnp.zeros((orders.shape[0], lat_total), jnp.float32)
    _, legendre = lax.scan(advance, (zeros, zeros, zeros), jnp.arange(degree_total, dtype=jnp.int32))
    return legendre

def wave_table(wave_total, lon_total):
    wave_ids = jnp.arange(wave_total, dtype=jnp.int32)
    lon_ids = jnp.arange(lon_total, dtype=jnp.int32)
    phase = (wave_ids[:, None] * lon_ids[None, :] % lon_total).astype(jnp.float32) * (2.0 * math.pi / lon_total)
    weights = jnp.where(wave_ids == 0, 1.0, 2.0).astype(jnp.float32) / wave_total
    return jnp.stack([weights[:, None] * jnp.cos(phase), -weights[:, None] * jnp.sin(phase)])

def silu_slope(inputs):
    sigmoid_v = jax.nn.sigmoid(inputs)
    return sigmoid_v * (1.0 + inputs * (1.0 - sigmoid_v))

def radiance_pass(profiles, observed, pair_counts, usable, channel_weight, weight_in, weight_mid, weight_out):
    pre_first = jnp.dot(profiles, weight_in, preferred_element_type=jnp.float32)
    act_first = jax.nn.silu(pre_first).astype(jnp.bfloat16)
    pre_second = jnp.dot(act_first, weight_mid, preferred_element_type=jnp.float32)
    act_second = jax.nn.silu(pre_second).astype(jnp.bfloat16)
    evolved = jnp.dot(act_second, weight_out, preferred_element_type=jnp.float32)
    channel_ids = jnp.arange(weight_out.shape[1], dtype=jnp.float32)
    active = (channel_ids[None, :] < 2.0 * pair_counts[:, None]) & usable[:, None]
    misfit = jnp.where(active, channel_weight[None, :] * (evolved - observed.astype(jnp.float32)), 0.0).astype(jnp.bfloat16)
    back_second = (jnp.dot(misfit, weight_out.T, preferred_element_type=jnp.float32) * silu_slope(pre_second)).astype(jnp.bfloat16)
    back_first = (jnp.dot(back_second, weight_mid.T, preferred_element_type=jnp.float32) * silu_slope(pre_first)).astype(jnp.bfloat16)
    return jnp.dot(back_first, weight_in.T, preferred_element_type=jnp.float32).astype(jnp.bfloat16)

def reference(spectral, background, columns, counts, radiances, used_pairs, channel_weight, weight_in, weight_mid, weight_out):
    highest = lax.Precision.HIGHEST
    legendre = legendre_table(jnp.arange(M, dtype=jnp.int32), NLAT, N)
    fourier = jnp.einsum('nmj,clmn->clmj', legendre, spectral, precision=highest)
    dft_table = wave_table(M, NLON)
    increment = jnp.einsum('clmj,cmx->jxl', fourier, dft_table, precision=highest)
    grid_state = (background.astype(jnp.float32) + increment).astype(jnp.bfloat16)
    start_ranks = (jnp.cumsum(counts) - counts).astype(jnp.int32)
    block_rank = jnp.arange(TOTAL, dtype=jnp.int32)
    covers = start_ranks[None, :] <= block_rank[:, None]
    owner_ids = (lax.optimization_barrier(jnp.sum(covers.astype(jnp.int32), axis=1)) - 1).astype(jnp.int32)
    slot_ids = (block_rank - start_ranks[owner_ids]).astype(jnp.int32)
    local_cols = columns[owner_ids, slot_ids]
    lat_ids = owner_ids // N_LEV * CLAT + local_cols // CLON
    lon_ids = owner_ids % N_LEV * CLON + local_cols % CLON
    flat_cells = (lat_ids * NLON + lon_ids).astype(jnp.int32)
    profiles = grid_state.reshape(NLAT * NLON, LEV)[flat_cells]
    observed = radiances[owner_ids, slot_ids]
    pair_counts = used_pairs[owner_ids, slot_ids].astype(jnp.float32)
    batches = TOTAL // BLK_DEV

    def one_batch(batch_rows):
        return radiance_pass(batch_rows[0], batch_rows[1], batch_rows[2], jnp.ones((BLK_DEV,), jnp.bool_), channel_weight, weight_in, weight_mid, weight_out)
    block_grad = lax.map(one_batch, (profiles.reshape(batches, BLK_DEV, LEV), observed.reshape(batches, BLK_DEV, CHAN), pair_counts.reshape(batches, BLK_DEV)))
    grid_grad = jnp.zeros((NLAT * NLON, LEV), jnp.float32).at[flat_cells].add(block_grad.reshape(TOTAL, LEV).astype(jnp.float32))
    grid_grad = grid_grad.reshape(NLAT, NLON, LEV)
    coeff_grad = jnp.einsum('jxl,cmx->clmj', grid_grad, dft_table, precision=highest)
    spectral_grad = jnp.einsum('nmj,clmj->clmn', legendre, coeff_grad, precision=highest)
    return (spectral_grad, grid_grad)
```

```python
import math

import jax
import jax.numpy as jnp
import numpy as np
from jax import lax
from jax.experimental import pallas as pl
from jax.experimental.pallas import tpu as pltpu
from jax.sharding import PartitionSpec as P

LEV = 128
M = 256
N = 256
NLAT = 384
NLON = 768
HALF = NLAT // 2
LANES = 128
N_LAT = 8
N_LEV = 16
ML = M // N_LAT
LL = LEV // N_LEV
CLAT = NLAT // N_LAT
CLON = NLON // N_LEV
CELLS = CLAT * CLON
CAP = 2048
CHAN = 512
JL = CLAT * LL
KM = 2 * M
ROWS = 2 * LL * ML

RESCALE_TOP = 2.0**30
RESCALE_BY = 2.0 ** (-60)
RESCALE_LOG = 60.0 * math.log(2.0)
HALF_LOG = 0.5 * math.log(0.5)

bf16 = jnp.bfloat16
f32 = jnp.float32


def params(**kwargs):
    return pltpu.CompilerParams(vmem_limit_bytes=56 << 20, **kwargs)


def dot_nt(a, b):
    return lax.dot_general(a, b, (((1,), (1,)), ((), ())), preferred_element_type=f32)


def dot_tn(a, b):
    return lax.dot_general(a, b, (((0,), (0,)), ((), ())), preferred_element_type=f32)


def dot_nn(a, b):
    return jnp.dot(a, b, preferred_element_type=f32)


def geometry():
    lat = (0.5 - (np.arange(256, dtype=np.float64) + 0.5) / NLAT) * np.pi
    valid = np.arange(256) < HALF
    sin_lat = np.where(valid, np.sin(lat), 0.0)
    log_cos = np.where(valid, np.log(np.cos(np.where(valid, lat, 0.0))), 0.0)
    rows = np.zeros((8, 256), np.float32)
    rows[0], rows[1], rows[2] = sin_lat, log_cos, valid
    k = np.arange(1, M, dtype=np.float64)
    steps = 0.5 * np.log((2.0 * k + 1.0) / (2.0 * k))
    log_norm = np.concatenate([[0.0], np.cumsum(steps)]) + HALF_LOG
    return rows, np.repeat(log_norm[:, None], LANES, axis=1).astype(np.float32)


def wave_table():
    m = np.arange(M)
    phase = (np.arange(NLON)[:, None] * m[None, :] % NLON) * (2.0 * np.pi / NLON)
    weight = np.where(m == 0, 1.0, 2.0) / M
    pair = np.stack([weight * np.cos(phase), -weight * np.sin(phase)])
    table = pair.reshape(2, NLON, N_LAT, ML).transpose(1, 2, 0, 3).reshape(NLON, KM)
    return jnp.asarray(table, f32).astype(bf16)


M_STEP = 4


def legendre_kernel(lat_ref, geo_ref, norm_ref, spec_ref, p_ref, four_ref, table, waves):
    step = pl.program_id(0)
    groups = range(ML // 8)

    @pl.when(step == 0)
    def _():
        m0 = lat_ref[0] * ML
        sub = lax.broadcasted_iota(jnp.int32, (8, LANES), 0)
        mf = [(sub + (m0 + 8 * g)).astype(f32) for g in groups]
        m2 = [v * v for v in mf]
        zero = jnp.zeros((8, LANES), f32)
        x = [jnp.broadcast_to(geo_ref[0:1, h * LANES : (h + 1) * LANES], (8, LANES)) for h in (0, 1)]
        log_cos = [
            jnp.broadcast_to(geo_ref[1:2, h * LANES : (h + 1) * LANES], (8, LANES)) for h in (0, 1)
        ]
        valid = [
            jnp.broadcast_to(geo_ref[2:3, h * LANES : (h + 1) * LANES], (8, LANES)) for h in (0, 1)
        ]
        logs = [
            [norm_ref[pl.ds(m0 + 8 * g, 8), :] + mf[g] * log_cos[h] for h in (0, 1)] for g in groups
        ]

        def block(i, carry):
            prev, earlier, logs, eps_prev, nf = carry
            big = [
                [jnp.maximum(jnp.abs(prev[g][h]), jnp.abs(earlier[g][h])) > RESCALE_TOP for h in (0, 1)]
                for g in groups
            ]
            shrink = [[jnp.where(big[g][h], RESCALE_BY, 1.0) for h in (0, 1)] for g in groups]
            prev = [[prev[g][h] * shrink[g][h] for h in (0, 1)] for g in groups]
            earlier = [[earlier[g][h] * shrink[g][h] for h in (0, 1)] for g in groups]
            logs = [
                [jnp.where(big[g][h], logs[g][h] + RESCALE_LOG, logs[g][h]) for h in (0, 1)]
                for g in groups
            ]
            scale = [[jnp.exp(logs[g][h]) * valid[h] for h in (0, 1)] for g in groups]
            for k in range(8):
                n2 = nf * nf
                inv = 1.0 / jnp.maximum(4.0 * n2 - 1.0, 1.0)
                at = pl.multiple_of((i * 8 + k) * ML, ML)
                new = []
                eps = []
                for g in groups:
                    t = n2 - m2[g]
                    q = jnp.maximum(t, 1.0) * inv
                    a = lax.rsqrt(q)
                    eps.append(jnp.where(t > 0.0, q * a, 0.0))
                    diag = nf == mf[g]
                    row = []
                    for h in (0, 1):
                        cur = (x[h] * prev[g][h] - eps_prev[g] * earlier[g][h]) * a
                        cur = jnp.where(diag, 1.0, cur)
                        table[h, pl.ds(at + 8 * g, 8), :] = cur * scale[g][h]
                        row.append(cur)
                    new.append(row)
                prev, earlier, eps_prev = new, prev, eps
                nf = nf + 1.0
            return prev, earlier, logs, eps_prev, nf

        empty = [[zero, zero] for _ in groups]
        lax.fori_loop(0, N // 8, block, (empty, empty, logs, [zero for _ in groups], zero))

    lane = lax.broadcasted_iota(jnp.int32, (1, N), 1)
    alternate = jnp.where(lane % 2 == 0, 1.0, -1.0)
    for k in range(M_STEP):
        m = step * M_STEP + k
        p_m = jnp.concatenate(
            [table[h, pl.ds(m, N, stride=ML), :].astype(bf16) for h in (0, 1)], axis=1
        )
        p_ref[k] = p_m
        s = jnp.concatenate([spec_ref[h, pl.ds(m, 2 * LL, stride=ML), :] for h in (0, 1)], axis=1)
        signed = s * (alternate if k % 2 == 0 else -alternate)
        out = dot_nn(jnp.concatenate([s, signed], axis=0).astype(bf16), p_m)
        for hemi in (0, 1):
            for c in (0, 1):
                first = (hemi * 2 + c) * LL
                for h in (0, 1):
                    waves[hemi, h, pl.ds(c * ML + m, LL, stride=2 * ML), :] = out[
                        first : first + LL, h * LANES : (h + 1) * LANES
                    ]

    @pl.when(step == pl.num_programs(0) - 1)
    def _():
        row = lax.broadcasted_iota(jnp.int32, (HALF, 256), 0)
        col = lax.broadcasted_iota(jnp.int32, (HALF, 256), 1)
        for hemi in (0, 1):
            pick = jnp.where(col == (row if hemi == 0 else HALF - 1 - row), 1.0, 0.0).astype(bf16)
            values = jnp.concatenate([waves[hemi, h].astype(bf16) for h in (0, 1)], axis=1)
            four_ref[hemi * HALF : (hemi + 1) * HALF, :] = dot_nt(pick, values).astype(bf16)


def legendre_transform(lat_index, spectral):
    geo, norm = geometry()
    spec = spectral.reshape(ROWS, 2, LANES).transpose(1, 0, 2)
    whole = lambda shape: pl.BlockSpec(shape, lambda i, *_: (0,) * len(shape))
    return pl.pallas_call(
        legendre_kernel,
        grid_spec=pltpu.PrefetchScalarGridSpec(
            num_scalar_prefetch=1,
            grid=(ML // M_STEP,),
            in_specs=[whole((8, 256)), whole((M, LANES)), whole((2, ROWS, LANES))],
            out_specs=[
                pl.BlockSpec((M_STEP, N, 256), lambda i, *_: (i, 0, 0)),
                whole((NLAT, ROWS)),
            ],
            scratch_shapes=[
                pltpu.VMEM((2, N * ML, LANES), f32),
                pltpu.VMEM((2, 2, ROWS, LANES), f32),
            ],
        ),
        out_shape=[
            jax.ShapeDtypeStruct((ML, N, 256), bf16),
            jax.ShapeDtypeStruct((NLAT, ROWS), bf16),
        ],
        compiler_params=params(),
        name="legendre",
    )(lat_index, jnp.asarray(geo), jnp.asarray(norm), spec)


def adjoint_kernel(p_ref, rows_ref, out_ref, folded):
    step = pl.program_id(0)

    @pl.when(step == 0)
    def _():
        j = lax.broadcasted_iota(jnp.int32, (NLAT, 256), 0)
        col = lax.broadcasted_iota(jnp.int32, (NLAT, 256), 1)
        north = jnp.where(col == j, 1.0, 0.0)
        south = jnp.where((j >= HALF) & (col == NLAT - 1 - j), 1.0, 0.0)
        north = jnp.where(col < HALF, north, 0.0)
        for part, pick in ((0, north + south), (1, north - south)):
            value = dot_tn(rows_ref[...], pick.astype(bf16))
            for h in (0, 1):
                folded[part, h] = value[:, h * LANES : (h + 1) * LANES]

    lane = lax.broadcasted_iota(jnp.int32, (2 * LL, N), 1)
    for k in range(M_STEP):
        m = step * M_STEP + k
        pieces = []
        for part in (0, 1):
            for c in (0, 1):
                pieces.append(
                    jnp.concatenate(
                        [
                            folded[part, h, pl.ds(c * ML + m, LL, stride=2 * ML), :]
                            for h in (0, 1)
                        ],
                        axis=1,
                    )
                )
        value = dot_nt(jnp.concatenate(pieces, axis=0).astype(bf16), p_ref[k])
        picked = jnp.where(lane % 2 == k % 2, value[: 2 * LL], value[2 * LL :])
        for h in (0, 1):
            out_ref[h, pl.ds(m, 2 * LL, stride=ML), :] = picked[:, h * LANES : (h + 1) * LANES]


def legendre_adjoint(table, rows):
    whole = lambda shape: pl.BlockSpec(shape, lambda i: (0,) * len(shape))
    out = pl.pallas_call(
        adjoint_kernel,
        grid=(ML // M_STEP,),
        in_specs=[pl.BlockSpec((M_STEP, N, 256), lambda i: (i, 0, 0)), whole((NLAT, ROWS))],
        out_specs=whole((2, ROWS, LANES)),
        scratch_shapes=[pltpu.VMEM((2, 2, ROWS, LANES), f32)],
        out_shape=jax.ShapeDtypeStruct((2, ROWS, LANES), f32),
        compiler_params=params(),
        name="legendre_adjoint",
    )(table, rows)
    return out.transpose(1, 0, 2).reshape(2, LL, ML, N)


def waves_kernel(rows_ref, table_ref, out_ref, held):
    for pair in range(N_LAT // 2):
        for l in range(LL):
            pieces = [
                rows_ref[(2 * pair + k) * CLAT : (2 * pair + k + 1) * CLAT, l * 64 : (l + 1) * 64]
                for k in (0, 1)
            ]
            held[pair, pl.ds(l, CLAT, stride=LL), :] = jnp.concatenate(pieces, axis=1).astype(f32)
    waves = jnp.concatenate([held[k].astype(bf16) for k in range(N_LAT // 2)], axis=1)
    out_ref[...] = dot_nt(table_ref[...], waves).astype(bf16)


def waves_to_grid(rows, table):
    return pl.pallas_call(
        waves_kernel,
        out_shape=jax.ShapeDtypeStruct((NLON, JL), bf16),
        scratch_shapes=[pltpu.VMEM((N_LAT // 2, JL, LANES), f32)],
        compiler_params=params(),
        name="waves",
    )(rows, table)


def waves_adjoint_kernel(grid_ref, table_ref, out_ref, held):
    value = dot_tn(grid_ref[...], table_ref[...])
    for k in range(N_LAT // 2):
        held[k] = value[:, k * LANES : (k + 1) * LANES]
    for pair in range(N_LAT // 2):
        for lp in range(LL // 2):
            two = [held[pair, pl.ds(2 * lp + k, CLAT, stride=LL), :] for k in (0, 1)]
            for k in (0, 1):
                piece = jnp.concatenate([v[:, k * 64 : (k + 1) * 64] for v in two], axis=1)
                first = (2 * pair + k) * CLAT
                out_ref[first : first + CLAT, lp * LANES : (lp + 1) * LANES] = piece.astype(bf16)


def grid_to_waves(grid, table):
    return pl.pallas_call(
        waves_adjoint_kernel,
        out_shape=jax.ShapeDtypeStruct((NLAT, ROWS), bf16),
        scratch_shapes=[pltpu.VMEM((N_LAT // 2, JL, LANES), f32)],
        compiler_params=params(),
        name="waves_adjoint",
    )(grid, table)


SUM_TILE = 256


def sums_kernel(count_ref, columns_ref, pairs_ref, obs_ref, sum_ref, seen_ref, masked):
    step = pl.program_id(0)
    count = count_ref[0]

    @pl.when(step == 0)
    def _():
        def fill(i, _):
            r = pl.ds(pl.multiple_of(i * 256, 256), 256)
            channel = lax.broadcasted_iota(jnp.int32, (256, CHAN), 1)
            active = channel < 2 * pairs_ref[r, :]
            masked[r, 0:CHAN] = jnp.where(active, obs_ref[r, :].astype(f32), 0.0).astype(bf16)
            masked[r, CHAN : 2 * CHAN] = jnp.where(active, 1.0, 0.0).astype(bf16)
            return 0

        lax.fori_loop(0, CAP // 256, fill, 0)

    cell = lax.broadcasted_iota(jnp.int32, (SUM_TILE, CAP), 0) + step * SUM_TILE
    slot = lax.broadcasted_iota(jnp.int32, (1, CAP), 1)
    column = jnp.where(slot < count, columns_ref[...], -1)
    hit = jnp.where(cell == column, 1.0, 0.0).astype(bf16)
    sum_ref[...] = dot_nn(hit, masked[:, 0:CHAN])
    seen_ref[...] = dot_nn(hit, masked[:, CHAN : 2 * CHAN])


def column_sums(counts, columns, pairs, obs):
    whole = lambda shape: pl.BlockSpec(shape, lambda i, *_: (0,) * len(shape))
    part = pl.BlockSpec((SUM_TILE, CHAN), lambda i, *_: (i, 0))
    return pl.pallas_call(
        sums_kernel,
        grid_spec=pltpu.PrefetchScalarGridSpec(
            num_scalar_prefetch=1,
            grid=(CELLS // SUM_TILE,),
            in_specs=[whole((1, CAP)), whole((CAP, 1)), whole((CAP, CHAN))],
            out_specs=[part, part],
            scratch_shapes=[pltpu.VMEM((CAP, 2 * CHAN), bf16)],
        ),
        out_shape=[jax.ShapeDtypeStruct((CELLS, CHAN), f32)] * 2,
        compiler_params=params(),
        name="column_sums",
    )(counts, columns, pairs, obs)


J_STEP = 16
TILE = 256
X_ROWS = 16


def silu_and_slope(v):
    half = 0.5 * v
    sig = 0.5 * jnp.tanh(half) + 0.5
    act = v * sig
    return act, sig + act - act * sig


def swap_blocks(v):
    lane = lax.broadcasted_iota(jnp.int32, v[0].shape, 1)
    v = list(v)
    for bit in range(4):
        gap = 1 << bit
        upper = (lane & (8 * gap)) != 0
        for s in range(N_LEV):
            if s & gap:
                continue
            a, b = v[s], v[s + gap]
            v[s] = jnp.where(upper, pltpu.roll(b, 8 * gap, 1), a)
            v[s + gap] = jnp.where(upper, b, pltpu.roll(a, LANES - 8 * gap, 1))
    return v


def network_kernel(
    inc_ref, back_ref, sum_ref, seen_ref, chan_ref, w_in, w_mid, w_out, grad_ref, send_ref, state, grads
):
    for part in range(CLON // X_ROWS):
        x0 = part * X_ROWS
        v = [inc_ref[s * CLON + x0 : s * CLON + x0 + X_ROWS, :].astype(f32) for s in range(N_LEV)]
        v = swap_blocks(v)
        for j in range(J_STEP):
            total = back_ref[j, x0 : x0 + X_ROWS, :].astype(f32) + v[j]
            state[j * CLON + x0 : j * CLON + x0 + X_ROWS, :] = total.astype(bf16)
    for i in range(J_STEP * CLON // TILE):
        r = slice(i * TILE, (i + 1) * TILE)
        act1, slope1 = silu_and_slope(dot_nn(state[r, :], w_in[...]))
        act2, slope2 = silu_and_slope(dot_nn(act1.astype(bf16), w_mid[...]))
        evolved = dot_nn(act2.astype(bf16), w_out[...])
        misfit = (chan_ref[...] * (seen_ref[r, :] * evolved - sum_ref[r, :])).astype(bf16)
        back2 = (dot_nt(misfit, w_out[...]) * slope2).astype(bf16)
        back1 = (dot_nt(back2, w_mid[...]) * slope1).astype(bf16)
        grads[r, :] = dot_nt(back1, w_in[...])
    for j in range(J_STEP):
        grad_ref[j] = grads[j * CLON : (j + 1) * CLON, :]
    for part in range(CLON // X_ROWS):
        x0 = part * X_ROWS
        v = [grads[j * CLON + x0 : j * CLON + x0 + X_ROWS, :] for j in range(J_STEP)]
        v = swap_blocks(v)
        for s in range(N_LEV):
            send_ref[s * CLON + x0 : s * CLON + x0 + X_ROWS, :] = v[s].astype(bf16)


def network(inc, background, sums, seen, channel_weight, w_in, w_mid, w_out):
    whole = lambda shape: pl.BlockSpec(shape, lambda i: (0,) * len(shape))
    cells = J_STEP * CLON
    return pl.pallas_call(
        network_kernel,
        grid=(CLAT // J_STEP,),
        in_specs=[
            pl.BlockSpec((NLON, LANES), lambda i: (0, i)),
            pl.BlockSpec((J_STEP, CLON, LEV), lambda i: (i, 0, 0)),
            pl.BlockSpec((cells, CHAN), lambda i: (i, 0)),
            pl.BlockSpec((cells, CHAN), lambda i: (i, 0)),
            whole((1, CHAN)),
            whole(w_in.shape),
            whole(w_mid.shape),
            whole(w_out.shape),
        ],
        out_specs=[
            pl.BlockSpec((J_STEP, CLON, LEV), lambda i: (i, 0, 0)),
            pl.BlockSpec((NLON, LANES), lambda i: (0, i)),
        ],
        out_shape=[
            jax.ShapeDtypeStruct((CLAT, CLON, LEV), f32),
            jax.ShapeDtypeStruct((NLON, JL), bf16),
        ],
        scratch_shapes=[pltpu.VMEM((cells, LEV), bf16), pltpu.VMEM((cells, LEV), f32)],
        compiler_params=params(),
        name="network",
    )(inc, background, sums, seen, channel_weight, w_in, w_mid, w_out)


def exchange(rows, axis):
    return lax.all_to_all(rows, axis, split_axis=0, concat_axis=0, tiled=True)


def per_device(
    spectral,
    background,
    columns,
    counts,
    radiances,
    used_pairs,
    channel_weight,
    weight_in,
    weight_mid,
    weight_out,
):
    table = wave_table()
    lat_index = lax.axis_index("lat").astype(jnp.int32).reshape(1)
    legendre, fourier = legendre_transform(lat_index, spectral)
    fourier = exchange(fourier, "lat")
    sums, seen = column_sums(counts, columns, used_pairs.reshape(CAP, 1), radiances[0])
    increment = exchange(waves_to_grid(fourier, table), "lev")
    grid_grad, send = network(
        increment,
        background,
        sums,
        seen,
        channel_weight.reshape(1, CHAN),
        weight_in,
        weight_mid,
        weight_out,
    )
    coeff = exchange(grid_to_waves(exchange(send, "lev"), table), "lat")
    return (legendre_adjoint(legendre, coeff), grid_grad)


def solution(mesh):
    in_specs = (
        P(None, "lev", "lat", None),
        P("lat", "lev", None),
        P(("lat", "lev"), None),
        P(("lat", "lev")),
        P(("lat", "lev"), None, None),
        P(("lat", "lev"), None),
        P(),
        P(),
        P(),
        P(),
    )
    out_specs = (P(None, "lev", "lat", None), P("lat", "lev", None))
    return jax.shard_map(
        per_device, mesh=mesh, in_specs=in_specs, out_specs=out_specs, check_vma=False
    )
```

```python
import functools
import math

import jax
import jax.numpy as jnp
import numpy as np
from jax import lax
from jax.experimental import pallas as pl
from jax.experimental.pallas import tpu as pltpu
from jax.sharding import PartitionSpec as P

LEV = 128
M = 256
N = 256
NLAT = 384
NLON = 768
HALF = NLAT // 2
LANES = 128
N_LAT = 8
N_LEV = 16
ML = M // N_LAT
LL = LEV // N_LEV
CLAT = NLAT // N_LAT
CLON = NLON // N_LEV
CELLS = CLAT * CLON
CAP = 2048
CHAN = 512
JL = CLAT * LL
KM = 2 * M
ROWS = 2 * LL * ML

RESCALE_TOP = 2.0**30
RESCALE_BY = 2.0 ** (-60)
RESCALE_LOG = 60.0 * math.log(2.0)
HALF_LOG = 0.5 * math.log(0.5)

bf16 = jnp.bfloat16
f32 = jnp.float32


def params(mib):
    return pltpu.CompilerParams(vmem_limit_bytes=mib << 20)


def on_chip(array):
    return pltpu.with_memory_space_constraint(array, pltpu.VMEM)


def in_hbm(array):
    return pltpu.with_memory_space_constraint(array, pltpu.HBM)


VMEM_SPEC = pl.BlockSpec(memory_space=pltpu.VMEM)


def dot_nt(a, b):
    return lax.dot_general(a, b, (((1,), (1,)), ((), ())), preferred_element_type=f32)


def dot_tn(a, b):
    return lax.dot_general(a, b, (((0,), (0,)), ((), ())), preferred_element_type=f32)


def dot_nn(a, b):
    return jnp.dot(a, b, preferred_element_type=f32)


def geometry():
    lat = (0.5 - (np.arange(256, dtype=np.float64) + 0.5) / NLAT) * np.pi
    valid = np.arange(256) < HALF
    sin_lat = np.where(valid, np.sin(lat), 0.0)
    log_cos = np.where(valid, np.log(np.cos(np.where(valid, lat, 0.0))), 0.0)
    rows = np.zeros((8, 256), np.float32)
    rows[0], rows[1], rows[2] = sin_lat, log_cos, valid
    k = np.arange(1, M, dtype=np.float64)
    steps = 0.5 * np.log((2.0 * k + 1.0) / (2.0 * k))
    log_norm = np.concatenate([[0.0], np.cumsum(steps)]) + HALF_LOG
    return rows, np.repeat(log_norm[:, None], LANES, axis=1).astype(np.float32)


def wave_table():
    m = np.arange(M)
    phase = (np.arange(NLON)[:, None] * m[None, :] % NLON) * (2.0 * np.pi / NLON)
    weight = np.where(m == 0, 1.0, 2.0) / M
    pair = np.stack([weight * np.cos(phase), -weight * np.sin(phase)])
    table = pair.reshape(2, NLON, N_LAT, ML).transpose(1, 2, 0, 3).reshape(NLON, KM)
    return jnp.asarray(table, f32).astype(bf16)


M_STEP = 8
ADJOINT_STEP = 16


def legendre_kernel(lat_ref, geo_ref, norm_ref, spec_ref, p_ref, four_ref, table, waves, halves):
    step = pl.program_id(0)
    groups = range(ML // 8)

    @pl.when(step == 0)
    def _():
        for h in (0, 1):
            halves[h] = spec_ref[:, h * LANES : (h + 1) * LANES]
        m0 = lat_ref[0] * ML
        sub = lax.broadcasted_iota(jnp.int32, (8, LANES), 0)
        mf = [(sub + (m0 + 8 * g)).astype(f32) for g in groups]
        m2 = [v * v for v in mf]
        zero = jnp.zeros((8, LANES), f32)
        x = [jnp.broadcast_to(geo_ref[0:1, h * LANES : (h + 1) * LANES], (8, LANES)) for h in (0, 1)]
        log_cos = [
            jnp.broadcast_to(geo_ref[1:2, h * LANES : (h + 1) * LANES], (8, LANES)) for h in (0, 1)
        ]
        valid = [
            jnp.broadcast_to(geo_ref[2:3, h * LANES : (h + 1) * LANES], (8, LANES)) for h in (0, 1)
        ]
        logs = [
            [norm_ref[pl.ds(m0 + 8 * g, 8), :] + mf[g] * log_cos[h] for h in (0, 1)] for g in groups
        ]

        def block(i, carry):
            prev, earlier, logs, eps_prev, nf = carry
            big = [
                [jnp.maximum(jnp.abs(prev[g][h]), jnp.abs(earlier[g][h])) > RESCALE_TOP for h in (0, 1)]
                for g in groups
            ]
            shrink = [[jnp.where(big[g][h], RESCALE_BY, 1.0) for h in (0, 1)] for g in groups]
            prev = [[prev[g][h] * shrink[g][h] for h in (0, 1)] for g in groups]
            earlier = [[earlier[g][h] * shrink[g][h] for h in (0, 1)] for g in groups]
            logs = [
                [jnp.where(big[g][h], logs[g][h] + RESCALE_LOG, logs[g][h]) for h in (0, 1)]
                for g in groups
            ]
            scale = [[jnp.exp(logs[g][h]) * valid[h] for h in (0, 1)] for g in groups]
            for k in range(8):
                n2 = nf * nf
                inv = 1.0 / jnp.maximum(4.0 * n2 - 1.0, 1.0)
                at = pl.multiple_of((i * 8 + k) * ML, ML)
                new = []
                eps = []
                for g in groups:
                    t = n2 - m2[g]
                    q = jnp.maximum(t, 1.0) * inv
                    a = lax.rsqrt(q)
                    eps.append(jnp.where(t > 0.0, q * a, 0.0))
                    diag = nf == mf[g]
                    row = []
                    for h in (0, 1):
                        cur = (x[h] * prev[g][h] - eps_prev[g] * earlier[g][h]) * a
                        cur = jnp.where(diag, 1.0, cur)
                        table[h, pl.ds(at + 8 * g, 8), :] = cur * scale[g][h]
                        row.append(cur)
                    new.append(row)
                prev, earlier, eps_prev = new, prev, eps
                nf = nf + 1.0
            return prev, earlier, logs, eps_prev, nf

        empty = [[zero, zero] for _ in groups]
        lax.fori_loop(0, N // 8, block, (empty, empty, logs, [zero for _ in groups], zero))

    lane = lax.broadcasted_iota(jnp.int32, (1, N), 1)
    alternate = jnp.where(lane % 2 == 0, 1.0, -1.0)
    for k in range(M_STEP):
        m = step * M_STEP + k
        p_m = jnp.concatenate(
            [table[h, pl.ds(m, N, stride=ML), :].astype(bf16) for h in (0, 1)], axis=1
        )
        p_ref[k] = p_m
        s = jnp.concatenate([halves[h, pl.ds(m, 2 * LL, stride=ML), :] for h in (0, 1)], axis=1)
        s = jnp.concatenate([s, s * (alternate if k % 2 == 0 else -alternate)], axis=0)
        high = s.astype(bf16)
        low = (s - high.astype(f32)).astype(bf16)
        out = dot_nn(jnp.concatenate([high, low], axis=0), p_m)
        out = out[: 4 * LL] + out[4 * LL :]
        for hemi in (0, 1):
            for c in (0, 1):
                first = (hemi * 2 + c) * LL
                for h in (0, 1):
                    waves[hemi, h, pl.ds(c * ML + m, LL, stride=2 * ML), :] = out[
                        first : first + LL, h * LANES : (h + 1) * LANES
                    ]

    @pl.when(step == pl.num_programs(0) - 1)
    def _():
        row = lax.broadcasted_iota(jnp.int32, (HALF, 256), 0)
        col = lax.broadcasted_iota(jnp.int32, (HALF, 256), 1)
        for hemi in (0, 1):
            pick = jnp.where(col == (row if hemi == 0 else HALF - 1 - row), 1.0, 0.0).astype(bf16)
            values = jnp.concatenate([waves[hemi, h].astype(bf16) for h in (0, 1)], axis=1)
            four_ref[hemi * HALF : (hemi + 1) * HALF, :] = dot_nt(pick, values).astype(bf16)


def legendre_transform(lat_index, spectral):
    geo, norm = geometry()
    whole = lambda shape: pl.BlockSpec(shape, lambda i, *_: (0,) * len(shape))
    return pl.pallas_call(
        legendre_kernel,
        grid_spec=pltpu.PrefetchScalarGridSpec(
            num_scalar_prefetch=1,
            grid=(ML // M_STEP,),
            in_specs=[whole((8, 256)), whole((M, LANES)), whole((ROWS, N))],
            out_specs=[
                pl.BlockSpec((M_STEP, N, 256), lambda i, *_: (i, 0, 0)),
                whole((NLAT, ROWS)),
            ],
            scratch_shapes=[
                pltpu.VMEM((2, N * ML, LANES), f32),
                pltpu.VMEM((2, 2, ROWS, LANES), f32),
                pltpu.VMEM((2, ROWS, LANES), f32),
            ],
        ),
        out_shape=[
            pltpu.HBM((ML, N, 256), bf16),
            pltpu.HBM((NLAT, ROWS), bf16),
        ],
        compiler_params=params(18),
        name="legendre",
    )(lat_index, in_hbm(jnp.asarray(geo)), in_hbm(jnp.asarray(norm)), in_hbm(spectral.reshape(ROWS, N)))


def adjoint_kernel(p_ref, rows_ref, out_ref, folded, held):
    step = pl.program_id(0)

    @pl.when(step == 0)
    def _():
        j = lax.broadcasted_iota(jnp.int32, (NLAT, 256), 0)
        col = lax.broadcasted_iota(jnp.int32, (NLAT, 256), 1)
        north = jnp.where(col == j, 1.0, 0.0)
        south = jnp.where((j >= HALF) & (col == NLAT - 1 - j), 1.0, 0.0)
        north = jnp.where(col < HALF, north, 0.0)
        for part, pick in ((0, north + south), (1, north - south)):
            value = dot_tn(rows_ref[...], pick.astype(bf16))
            for h in (0, 1):
                folded[part, h] = value[:, h * LANES : (h + 1) * LANES]

    lane = lax.broadcasted_iota(jnp.int32, (2 * LL, N), 1)
    for k in range(ADJOINT_STEP):
        m = step * ADJOINT_STEP + k
        pieces = []
        for part in (0, 1):
            for c in (0, 1):
                pieces.append(
                    jnp.concatenate(
                        [
                            folded[part, h, pl.ds(c * ML + m, LL, stride=2 * ML), :]
                            for h in (0, 1)
                        ],
                        axis=1,
                    )
                )
        value = dot_nt(jnp.concatenate(pieces, axis=0).astype(bf16), p_ref[m])
        picked = jnp.where(lane % 2 == k % 2, value[: 2 * LL], value[2 * LL :])
        for h in (0, 1):
            held[h, pl.ds(m, 2 * LL, stride=ML), :] = picked[:, h * LANES : (h + 1) * LANES]

    @pl.when(step == pl.num_programs(0) - 1)
    def _():
        for h in (0, 1):
            out_ref[:, h * LANES : (h + 1) * LANES] = held[h]


def legendre_adjoint(table, rows):
    whole = lambda shape: pl.BlockSpec(shape, lambda i: (0,) * len(shape))
    out = pl.pallas_call(
        adjoint_kernel,
        grid=(ML // ADJOINT_STEP,),
        in_specs=[
            VMEM_SPEC,
            VMEM_SPEC,
        ],
        out_specs=whole((ROWS, N)),
        scratch_shapes=[
            pltpu.VMEM((2, 2, ROWS, LANES), f32),
            pltpu.VMEM((2, ROWS, LANES), f32),
        ],
        out_shape=jax.ShapeDtypeStruct((ROWS, N), f32),
        compiler_params=params(12),
        name="legendre_adjoint",
    )(on_chip(table), rows)
    return out.reshape(2, LL, ML, N)


def waves_kernel(rows_ref, table_ref, after_ref, out_ref, held):
    del after_ref
    for pair in range(N_LAT // 2):
        for l in range(LL):
            pieces = [
                rows_ref[(2 * pair + k) * CLAT : (2 * pair + k + 1) * CLAT, l * 64 : (l + 1) * 64]
                for k in (0, 1)
            ]
            held[pair, pl.ds(l, CLAT, stride=LL), :] = jnp.concatenate(pieces, axis=1).astype(f32)
    waves = jnp.concatenate([held[k].astype(bf16) for k in range(N_LAT // 2)], axis=1)
    out_ref[...] = dot_nt(table_ref[...], waves).astype(bf16)


def waves_to_grid(rows, table, after):
    return pl.pallas_call(
        waves_kernel,
        in_specs=[VMEM_SPEC, VMEM_SPEC, pl.BlockSpec(memory_space=pl.ANY)],
        out_shape=pltpu.HBM((NLON, JL), bf16),
        scratch_shapes=[pltpu.VMEM((N_LAT // 2, JL, LANES), f32)],
        compiler_params=params(12),
        name="waves",
    )(rows, table, in_hbm(after))


def waves_adjoint_kernel(grid_ref, table_ref, out_ref, held):
    value = dot_tn(grid_ref[...], table_ref[...])
    for k in range(N_LAT // 2):
        held[k] = value[:, k * LANES : (k + 1) * LANES]
    for pair in range(N_LAT // 2):
        for lp in range(LL // 2):
            two = [held[pair, pl.ds(2 * lp + k, CLAT, stride=LL), :] for k in (0, 1)]
            for k in (0, 1):
                piece = jnp.concatenate([v[:, k * 64 : (k + 1) * 64] for v in two], axis=1)
                first = (2 * pair + k) * CLAT
                out_ref[first : first + CLAT, lp * LANES : (lp + 1) * LANES] = piece.astype(bf16)


def grid_to_waves(grid, table):
    return pl.pallas_call(
        waves_adjoint_kernel,
        in_specs=[VMEM_SPEC, VMEM_SPEC],
        out_shape=pltpu.HBM((NLAT, ROWS), bf16),
        scratch_shapes=[pltpu.VMEM((N_LAT // 2, JL, LANES), f32)],
        compiler_params=params(12),
        name="waves_adjoint",
    )(grid, table)


GROUP = 256
GROUPS = CELLS // GROUP
TILE = 240
SUM_TILE = 2 * TILE
ROW_TILES = -(-(CAP + 7 * GROUPS) // SUM_TILE)
MAX_ROWS = ROW_TILES * SUM_TILE


def assign_rows(count, columns):
    slot = lax.broadcasted_iota(jnp.int32, (1, CAP), 1)
    valid = slot < count
    group = jnp.where(valid, lax.shift_right_logical(columns, 8), -1)
    inner = lax.broadcasted_iota(jnp.int32, (GROUP, CAP), 0) == (columns & (GROUP - 1))
    inner = jnp.where(inner, 1.0, 0.0).astype(bf16)
    in_group = lax.broadcasted_iota(jnp.int32, (16, CAP), 0) == group
    seen = dot_nt(jnp.where(in_group, 1.0, 0.0).astype(bf16), inner)
    used = jnp.where(seen > 0.5, 1.0, 0.0)
    before = lax.broadcasted_iota(jnp.int32, (GROUP, GROUP), 0) < lax.broadcasted_iota(
        jnp.int32, (GROUP, GROUP), 1
    )
    rank = dot_nn(used.astype(bf16), jnp.where(before, 1.0, 0.0).astype(bf16))
    padded = jnp.floor((jnp.sum(used, axis=1, keepdims=True) + 7.0) * 0.125) * 8.0
    padded = jnp.broadcast_to(padded, (16, LANES))
    sub = lax.broadcasted_iota(jnp.int32, (16, LANES), 0)
    first = jnp.zeros((16, LANES), f32)
    for g in range(GROUPS):
        first = first + jnp.where(sub > g, padded[g : g + 1, :], 0.0)
    of_slot = dot_nn(rank.astype(bf16), inner) + first[:, 0:1]
    row = jnp.sum(jnp.where(in_group, of_slot, 0.0), axis=0, keepdims=True)
    row = jnp.where(valid, row, -1.0).astype(jnp.int32)
    return row, jnp.where(used > 0.5, rank, -1.0), first


def sum_rows(step, total, row_of_slot, masked, sum_ref):
    @pl.when(step * SUM_TILE < total)
    def _():
        row = lax.broadcasted_iota(jnp.int32, (SUM_TILE, CAP), 0) + step * SUM_TILE
        hit = jnp.where(row == row_of_slot, 1.0, 0.0).astype(bf16)
        sum_ref[...] = dot_nn(hit, masked[...])


def active_channels(pairs_ref, value, masked):
    channel = lax.broadcasted_iota(jnp.int32, (LANES, LANES), 1)
    for i in range(CAP // LANES):
        r = slice(i * LANES, (i + 1) * LANES)
        used = jnp.transpose(jnp.broadcast_to(2 * pairs_ref[:, r], (LANES, LANES)))
        for c in range(CHAN // LANES):
            lanes = slice(c * LANES, (c + 1) * LANES)
            masked[r, lanes] = jnp.where(
                channel + c * LANES < used, value(r, lanes), 0.0
            ).astype(bf16)


def sums_kernel(
    count_ref,
    columns_ref,
    pairs_ref,
    obs_ref,
    after_ref,
    sum_ref,
    row_ref,
    rank_ref,
    first_ref,
    masked,
    total_ref,
):
    del after_ref
    step = pl.program_id(0)

    @pl.when(step == 0)
    def _():
        row, rank, first = assign_rows(count_ref[0], columns_ref[...])
        row_ref[...] = row
        rank_ref[...] = rank
        first_ref[...] = first.astype(jnp.int32)
        total_ref[0] = jnp.max(first).astype(jnp.int32)
        active_channels(pairs_ref, lambda r, lanes: obs_ref[r, lanes].astype(f32), masked)

    sum_rows(step, total_ref[0], row_ref[...], masked, sum_ref)


def seen_kernel(first_ref, pairs_ref, row_ref, after_ref, sum_ref, masked):
    del after_ref
    step = pl.program_id(0)

    @pl.when(step == 0)
    def _():
        active_channels(pairs_ref, lambda r, lanes: 1.0, masked)

    sum_rows(step, first_ref[GROUPS, 0], row_ref[...], masked, sum_ref)


ROW_COST = pl.CostEstimate(
    flops=2 * MAX_ROWS * CAP * CHAN, transcendentals=0, bytes_accessed=MAX_ROWS * CHAN * 4
)


def row_sums(counts, columns, pairs, obs, after):
    whole = lambda shape: pl.BlockSpec(shape, lambda i, *_: (0,) * len(shape))
    return pl.pallas_call(
        sums_kernel,
        grid_spec=pltpu.PrefetchScalarGridSpec(
            num_scalar_prefetch=1,
            grid=(ROW_TILES,),
            in_specs=[
                whole((1, CAP)),
                whole((1, CAP)),
                whole((CAP, CHAN)),
                pl.BlockSpec(memory_space=pl.ANY),
            ],
            out_specs=[
                pl.BlockSpec((SUM_TILE, CHAN), lambda i, *_: (i, 0)),
                whole((1, CAP)),
                whole((16, GROUP)),
                whole((16, LANES)),
            ],
            scratch_shapes=[pltpu.VMEM((CAP, CHAN), bf16), pltpu.SMEM((1,), jnp.int32)],
        ),
        out_shape=[
            pltpu.HBM((MAX_ROWS, CHAN), f32),
            pltpu.HBM((1, CAP), jnp.int32),
            pltpu.HBM((16, GROUP), f32),
            pltpu.HBM((16, LANES), jnp.int32),
        ],
        compiler_params=params(24),
        cost_estimate=ROW_COST,
        name="row_sums",
    )(counts, in_hbm(columns), in_hbm(pairs), in_hbm(obs), in_hbm(after))


def row_seen(first, pairs, row, after):
    whole = lambda shape: pl.BlockSpec(shape, lambda i: (0,) * len(shape))
    return pl.pallas_call(
        seen_kernel,
        grid=(ROW_TILES,),
        in_specs=[
            pl.BlockSpec(memory_space=pltpu.SMEM),
            whole((1, CAP)),
            whole((1, CAP)),
            pl.BlockSpec(memory_space=pl.ANY),
        ],
        out_specs=pl.BlockSpec((SUM_TILE, CHAN), lambda i: (i, 0)),
        scratch_shapes=[pltpu.VMEM((CAP, CHAN), bf16)],
        out_shape=pltpu.HBM((MAX_ROWS, CHAN), f32),
        compiler_params=params(24),
        cost_estimate=ROW_COST,
        name="row_seen",
    )(first, in_hbm(pairs), in_hbm(row), in_hbm(after))


J_STEP = 16
X_ROWS = 16


def silu_and_slope(v):
    half = 0.5 * v
    sig = 0.5 * jnp.tanh(half) + 0.5
    act = v * sig
    return act, sig + act - act * sig


def swap_blocks(v):
    lane = lax.broadcasted_iota(jnp.int32, v[0].shape, 1)
    v = list(v)
    for bit in range(4):
        gap = 1 << bit
        upper = (lane & (8 * gap)) != 0
        for s in range(N_LEV):
            if s & gap:
                continue
            a, b = v[s], v[s + gap]
            v[s] = jnp.where(upper, pltpu.roll(b, 8 * gap, 1), a)
            v[s + gap] = jnp.where(upper, b, pltpu.roll(a, LANES - 8 * gap, 1))
    return v


def network_kernel(
    first_ref,
    inc_ref,
    back_ref,
    rank_ref,
    sum_hbm,
    seen_hbm,
    chan_ref,
    w_in,
    w_mid,
    w_out,
    grad_ref,
    send_ref,
    state,
    packed,
    packed_grad,
    w_twice,
    sum_buf,
    seen_buf,
    sems,
):
    total = first_ref[GROUPS, 0]
    tiles = (total + (TILE - 1)) // TILE

    def fetches(t, slot):
        r = pl.ds(pl.multiple_of(t * TILE, 8), TILE)
        return (
            pltpu.make_async_copy(sum_hbm.at[r, :], sum_buf.at[slot], sems.at[0, slot]),
            pltpu.make_async_copy(seen_hbm.at[r, :], seen_buf.at[slot], sems.at[1, slot]),
        )

    for fetch in fetches(0, 0):
        fetch.start()
    w_twice[:LEV] = w_in[...]
    w_twice[LEV:] = w_in[...]

    def to_state(jc, _):
        lanes = pl.ds(pl.multiple_of(jc * LANES, LANES), LANES)
        for part in range(CLON // X_ROWS):
            x0 = part * X_ROWS
            v = [
                inc_ref[s * CLON + x0 : s * CLON + x0 + X_ROWS, lanes].astype(f32)
                for s in range(N_LEV)
            ]
            v = swap_blocks(v)
            for j in range(J_STEP):
                r = pl.ds(pl.multiple_of((jc * J_STEP + j) * CLON + x0, 16), X_ROWS)
                grid_state = back_ref[r, :].astype(f32) + v[j]
                high = grid_state.astype(bf16)
                state[r, :LEV] = high
                state[r, LEV:] = (grid_state - high.astype(f32)).astype(bf16)
        return 0

    lax.fori_loop(0, CLAT // J_STEP, to_state, 0)

    def group_rows(g):
        first = pl.ds(pl.multiple_of(first_ref[g, 0], 8), GROUP)
        row = lax.broadcasted_iota(jnp.int32, (GROUP, GROUP), 0).astype(f32)
        pick = jnp.where(row == rank_ref[g : g + 1, :], 1.0, 0.0).astype(bf16)
        return first, slice(g * GROUP, (g + 1) * GROUP), pick

    for g in range(GROUPS):
        rows, cells, pick = group_rows(g)
        packed[rows, :] = dot_nn(pick, state[cells, :])
    packed[pl.ds(pl.multiple_of(total, 8), TILE), :] = jnp.zeros((TILE, 2 * LEV), f32)

    def one_tile(t, _):
        slot = lax.rem(t, 2)
        for fetch in fetches(t, slot):
            fetch.wait()

        @pl.when(t + 1 < tiles)
        def _():
            for fetch in fetches(t + 1, 1 - slot):
                fetch.start()

        r = pl.ds(pl.multiple_of(t * TILE, 8), TILE)
        act1, slope1 = silu_and_slope(dot_nn(packed[r, :].astype(bf16), w_twice[...]))
        act2, slope2 = silu_and_slope(dot_nn(act1.astype(bf16), w_mid[...]))
        evolved = dot_nn(act2.astype(bf16), w_out[...])
        misfit = (chan_ref[...] * (seen_buf[slot] * evolved - sum_buf[slot])).astype(bf16)
        back2 = (dot_nt(misfit, w_out[...]) * slope2).astype(bf16)
        back1 = (dot_nt(back2, w_mid[...]) * slope1).astype(bf16)
        packed_grad[r, :] = dot_nt(back1, w_in[...])
        return 0

    lax.fori_loop(0, tiles, one_tile, 0)
    packed_grad[pl.ds(pl.multiple_of(tiles * TILE, 8), GROUP), :] = jnp.zeros((GROUP, LEV), f32)
    for g in range(GROUPS):
        rows, cells, pick = group_rows(g)
        value = packed_grad[rows, :]
        high = value.astype(bf16)
        low = (value - high.astype(f32)).astype(bf16)
        value = dot_tn(pick, jnp.concatenate([high, low], axis=1))
        grad_ref[cells, :] = value[:, :LEV] + value[:, LEV:]

    def to_send(jc, _):
        lanes = pl.ds(pl.multiple_of(jc * LANES, LANES), LANES)
        for part in range(CLON // X_ROWS):
            x0 = part * X_ROWS
            v = [
                grad_ref[pl.ds(pl.multiple_of((jc * J_STEP + j) * CLON + x0, 16), X_ROWS), :]
                for j in range(J_STEP)
            ]
            v = swap_blocks(v)
            for s in range(N_LEV):
                send_ref[s * CLON + x0 : s * CLON + x0 + X_ROWS, lanes] = v[s].astype(bf16)
        return 0

    lax.fori_loop(0, CLAT // J_STEP, to_send, 0)


def network(first, inc, background, rank, sums, seen, channel_weight, w_in, w_mid, w_out):
    anywhere = pl.BlockSpec(memory_space=pl.ANY)
    grad, send = pl.pallas_call(
        network_kernel,
        in_specs=[pl.BlockSpec(memory_space=pltpu.SMEM), VMEM_SPEC, VMEM_SPEC, VMEM_SPEC]
        + [anywhere] * 2
        + [VMEM_SPEC] * 4,
        out_specs=[VMEM_SPEC, VMEM_SPEC],
        out_shape=[
            jax.ShapeDtypeStruct((CELLS, LEV), f32),
            pltpu.HBM((NLON, JL), bf16),
        ],
        scratch_shapes=[
            pltpu.VMEM((CELLS, 2 * LEV), bf16),
            pltpu.VMEM((MAX_ROWS + GROUP, 2 * LEV), f32),
            pltpu.VMEM((MAX_ROWS + GROUP, LEV), f32),
            pltpu.VMEM((2 * LEV, w_in.shape[1]), bf16),
            pltpu.VMEM((2, TILE, CHAN), f32),
            pltpu.VMEM((2, TILE, CHAN), f32),
            pltpu.SemaphoreType.DMA((2, 2)),
        ],
        compiler_params=params(30),
        name="network",
    )(
        first,
        inc,
        in_hbm(background),
        in_hbm(rank),
        in_hbm(sums),
        in_hbm(seen),
        channel_weight,
        in_hbm(w_in),
        on_chip(w_mid),
        in_hbm(w_out),
    )
    return grad.reshape(CLAT, CLON, LEV), send


def exchange(rows, axis):
    return on_chip(lax.all_to_all(rows, axis, split_axis=0, concat_axis=0, tiled=True))


def per_device(
    spectral,
    background,
    columns,
    counts,
    radiances,
    used_pairs,
    channel_weight,
    weight_in,
    weight_mid,
    weight_out,
):
    table = on_chip(wave_table())
    lat_index = lax.axis_index("lat").astype(jnp.int32).reshape(1)
    legendre, fourier = legendre_transform(lat_index, spectral)
    sums, row, rank, first = row_sums(counts, columns, used_pairs, radiances[0], fourier)
    waves = waves_to_grid(exchange(fourier, "lat"), table, first)
    seen = row_seen(first, used_pairs, row, waves)
    increment = exchange(waves, "lev")
    grid_grad, send = network(
        first,
        increment,
        background.reshape(CELLS, LEV),
        rank,
        sums,
        seen,
        channel_weight.reshape(1, CHAN),
        weight_in,
        weight_mid,
        weight_out,
    )
    coeff = exchange(grid_to_waves(exchange(send, "lev"), table), "lat")
    return (legendre_adjoint(legendre, coeff), grid_grad)


def solution(mesh):
    in_specs = (
        P(None, "lev", "lat", None),
        P("lat", "lev", None),
        P(("lat", "lev"), None),
        P(("lat", "lev")),
        P(("lat", "lev"), None, None),
        P(("lat", "lev"), None),
        P(),
        P(),
        P(),
        P(),
    )
    out_specs = (P(None, "lev", "lat", None), P("lat", "lev", None))
    return jax.shard_map(
        per_device, mesh=mesh, in_specs=in_specs, out_specs=out_specs, check_vma=False
    )
```

```python
import functools
import math

import jax
import jax.numpy as jnp
import numpy as np
from jax import lax
from jax.experimental import pallas as pl
from jax.experimental.pallas import tpu as pltpu
from jax.sharding import PartitionSpec as P

LEV = 128
M = 256
N = 256
NLAT = 384
NLON = 768
HALF = NLAT // 2
LANES = 128
N_LAT = 8
N_LEV = 16
ML = M // N_LAT
LL = LEV // N_LEV
CLAT = NLAT // N_LAT
CLON = NLON // N_LEV
CELLS = CLAT * CLON
CAP = 2048
CHAN = 512
JL = CLAT * LL
KM = 2 * M
M_PITCH = ML + 8
L_PITCH = 2 * ML + 8
ROWS = 2 * LL * ML

RESCALE_TOP = 2.0**30
RESCALE_BY = 2.0 ** (-60)
RESCALE_LOG = 60.0 * math.log(2.0)
HALF_LOG = 0.5 * math.log(0.5)

bf16 = jnp.bfloat16
f32 = jnp.float32


def params(mib):
    return pltpu.CompilerParams(vmem_limit_bytes=mib << 20)


def on_chip(array):
    return pltpu.with_memory_space_constraint(array, pltpu.VMEM)


def in_hbm(array):
    return pltpu.with_memory_space_constraint(array, pltpu.HBM)


VMEM_SPEC = pl.BlockSpec(memory_space=pltpu.VMEM)


def dot_nt(a, b):
    return lax.dot_general(a, b, (((1,), (1,)), ((), ())), preferred_element_type=f32)


def dot_tn(a, b):
    return lax.dot_general(a, b, (((0,), (0,)), ((), ())), preferred_element_type=f32)


def dot_nn(a, b):
    return jnp.dot(a, b, preferred_element_type=f32)


def geometry():
    lat = (0.5 - (np.arange(256, dtype=np.float64) + 0.5) / NLAT) * np.pi
    valid = np.arange(256) < HALF
    sin_lat = np.where(valid, np.sin(lat), 0.0)
    log_cos = np.where(valid, np.log(np.cos(np.where(valid, lat, 0.0))), 0.0)
    rows = np.zeros((8, 256), np.float32)
    rows[0], rows[1], rows[2] = sin_lat, log_cos, valid
    k = np.arange(1, M, dtype=np.float64)
    steps = 0.5 * np.log((2.0 * k + 1.0) / (2.0 * k))
    log_norm = np.concatenate([[0.0], np.cumsum(steps)]) + HALF_LOG
    return rows, np.repeat(log_norm[:, None], LANES, axis=1).astype(np.float32)


def wave_table():
    m = np.arange(M)
    phase = (np.arange(NLON)[:, None] * m[None, :] % NLON) * (2.0 * np.pi / NLON)
    weight = np.where(m == 0, 1.0, 2.0) / M
    pair = np.stack([weight * np.cos(phase), -weight * np.sin(phase)])
    table = pair.reshape(2, NLON, N_LAT, ML).transpose(1, 2, 0, 3).reshape(NLON, KM)
    return jnp.asarray(table, f32).astype(bf16)


M_STEP = 8
ADJOINT_STEP = 16


def legendre_kernel(lat_ref, geo_ref, norm_ref, spec_ref, p_ref, four_ref, table, waves, halves):
    step = pl.program_id(0)
    groups = range(ML // 8)

    @pl.when(step == 0)
    def _():
        for h in (0, 1):
            for k in range(2 * LL):
                halves[h, k * M_PITCH : k * M_PITCH + ML, :] = spec_ref[
                    k * ML : (k + 1) * ML, h * LANES : (h + 1) * LANES
                ]
        m0 = lat_ref[0] * ML
        sub = lax.broadcasted_iota(jnp.int32, (8, LANES), 0)
        mf = [(sub + (m0 + 8 * g)).astype(f32) for g in groups]
        m2 = [v * v for v in mf]
        zero = jnp.zeros((8, LANES), f32)
        x = [jnp.broadcast_to(geo_ref[0:1, h * LANES : (h + 1) * LANES], (8, LANES)) for h in (0, 1)]
        log_cos = [
            jnp.broadcast_to(geo_ref[1:2, h * LANES : (h + 1) * LANES], (8, LANES)) for h in (0, 1)
        ]
        valid = [
            jnp.broadcast_to(geo_ref[2:3, h * LANES : (h + 1) * LANES], (8, LANES)) for h in (0, 1)
        ]
        logs = [
            [norm_ref[pl.ds(m0 + 8 * g, 8), :] + mf[g] * log_cos[h] for h in (0, 1)] for g in groups
        ]

        def block(i, carry):
            prev, earlier, logs, eps_prev, nf = carry
            big = [
                [jnp.maximum(jnp.abs(prev[g][h]), jnp.abs(earlier[g][h])) > RESCALE_TOP for h in (0, 1)]
                for g in groups
            ]
            shrink = [[jnp.where(big[g][h], RESCALE_BY, 1.0) for h in (0, 1)] for g in groups]
            prev = [[prev[g][h] * shrink[g][h] for h in (0, 1)] for g in groups]
            earlier = [[earlier[g][h] * shrink[g][h] for h in (0, 1)] for g in groups]
            logs = [
                [jnp.where(big[g][h], logs[g][h] + RESCALE_LOG, logs[g][h]) for h in (0, 1)]
                for g in groups
            ]
            scale = [[jnp.exp(logs[g][h]) * valid[h] for h in (0, 1)] for g in groups]
            for k in range(8):
                n2 = nf * nf
                inv = 1.0 / jnp.maximum(4.0 * n2 - 1.0, 1.0)
                at = pl.multiple_of((i * 8 + k) * M_PITCH, 8)
                new = []
                eps = []
                for g in groups:
                    t = n2 - m2[g]
                    q = jnp.maximum(t, 1.0) * inv
                    a = lax.rsqrt(q)
                    eps.append(jnp.where(t > 0.0, q * a, 0.0))
                    diag = nf == mf[g]
                    row = []
                    for h in (0, 1):
                        cur = (x[h] * prev[g][h] - eps_prev[g] * earlier[g][h]) * a
                        cur = jnp.where(diag, 1.0, cur)
                        table[h, pl.ds(at + 8 * g, 8), :] = cur * scale[g][h]
                        row.append(cur)
                    new.append(row)
                prev, earlier, eps_prev = new, prev, eps
                nf = nf + 1.0
            return prev, earlier, logs, eps_prev, nf

        empty = [[zero, zero] for _ in groups]
        lax.fori_loop(0, N // 8, block, (empty, empty, logs, [zero for _ in groups], zero))

    lane = lax.broadcasted_iota(jnp.int32, (1, N), 1)
    alternate = jnp.where(lane % 2 == 0, 1.0, -1.0)
    for k in range(M_STEP):
        m = step * M_STEP + k
        p_m = jnp.concatenate(
            [table[h, pl.ds(m, N, stride=M_PITCH), :].astype(bf16) for h in (0, 1)], axis=1
        )
        p_ref[k] = p_m
        s = jnp.concatenate([halves[h, pl.ds(m, 2 * LL, stride=M_PITCH), :] for h in (0, 1)], axis=1)
        s = jnp.concatenate([s, s * (alternate if k % 2 == 0 else -alternate)], axis=0)
        high = s.astype(bf16)
        low = (s - high.astype(f32)).astype(bf16)
        out = dot_nn(jnp.concatenate([high, low], axis=0), p_m)
        out = out[: 4 * LL] + out[4 * LL :]
        for hemi in (0, 1):
            for c in (0, 1):
                first = (hemi * 2 + c) * LL
                for h in (0, 1):
                    waves[hemi, h, pl.ds(c * ML + m, LL, stride=L_PITCH), :] = out[
                        first : first + LL, h * LANES : (h + 1) * LANES
                    ]

    @pl.when(step == pl.num_programs(0) - 1)
    def _():
        row = lax.broadcasted_iota(jnp.int32, (HALF, 256), 0)
        col = lax.broadcasted_iota(jnp.int32, (HALF, 256), 1)
        for hemi in (0, 1):
            pick = jnp.where(col == (row if hemi == 0 else HALF - 1 - row), 1.0, 0.0).astype(bf16)
            values = jnp.concatenate(
                [
                    jnp.concatenate(
                        [
                            waves[hemi, h, l * L_PITCH : l * L_PITCH + 2 * ML, :].astype(bf16)
                            for h in (0, 1)
                        ],
                        axis=1,
                    )
                    for l in range(LL)
                ],
                axis=0,
            )
            four_ref[hemi * HALF : (hemi + 1) * HALF, :] = dot_nt(pick, values).astype(bf16)


def legendre_transform(lat_index, spectral):
    geo, norm = geometry()
    whole = lambda shape: pl.BlockSpec(shape, lambda i, *_: (0,) * len(shape))
    return pl.pallas_call(
        legendre_kernel,
        grid_spec=pltpu.PrefetchScalarGridSpec(
            num_scalar_prefetch=1,
            grid=(ML // M_STEP,),
            in_specs=[whole((8, 256)), whole((M, LANES)), whole((ROWS, N))],
            out_specs=[
                pl.BlockSpec((M_STEP, N, 256), lambda i, *_: (i, 0, 0)),
                VMEM_SPEC,
            ],
            scratch_shapes=[
                pltpu.VMEM((2, N * M_PITCH, LANES), f32),
                pltpu.VMEM((2, 2, LL * L_PITCH, LANES), f32),
                pltpu.VMEM((2, 2 * LL * M_PITCH, LANES), f32),
            ],
        ),
        out_shape=[
            pltpu.HBM((ML, N, 256), bf16),
            pltpu.VMEM((NLAT, ROWS), bf16),
        ],
        compiler_params=params(18),
        name="legendre",
    )(lat_index, in_hbm(jnp.asarray(geo)), in_hbm(jnp.asarray(norm)), in_hbm(spectral.reshape(ROWS, N)))


def adjoint_kernel(p_ref, rows_ref, out_ref, folded, held):
    step = pl.program_id(0)

    @pl.when(step == 0)
    def _():
        j = lax.broadcasted_iota(jnp.int32, (NLAT, 256), 0)
        col = lax.broadcasted_iota(jnp.int32, (NLAT, 256), 1)
        north = jnp.where(col == j, 1.0, 0.0)
        south = jnp.where((j >= HALF) & (col == NLAT - 1 - j), 1.0, 0.0)
        north = jnp.where(col < HALF, north, 0.0)
        for part, pick in ((0, north + south), (1, north - south)):
            value = dot_tn(rows_ref[...], pick.astype(bf16))
            for h in (0, 1):
                for l in range(LL):
                    folded[part, h, l * L_PITCH : l * L_PITCH + 2 * ML, :] = value[
                        l * 2 * ML : (l + 1) * 2 * ML, h * LANES : (h + 1) * LANES
                    ]

    lane = lax.broadcasted_iota(jnp.int32, (2 * LL, N), 1)
    for k in range(ADJOINT_STEP):
        m = step * ADJOINT_STEP + k
        pieces = []
        for part in (0, 1):
            for c in (0, 1):
                pieces.append(
                    jnp.concatenate(
                        [
                            folded[part, h, pl.ds(c * ML + m, LL, stride=L_PITCH), :]
                            for h in (0, 1)
                        ],
                        axis=1,
                    )
                )
        value = dot_nt(jnp.concatenate(pieces, axis=0).astype(bf16), p_ref[m])
        picked = jnp.where(lane % 2 == k % 2, value[: 2 * LL], value[2 * LL :])
        for h in (0, 1):
            held[h, pl.ds(m, 2 * LL, stride=M_PITCH), :] = picked[:, h * LANES : (h + 1) * LANES]

    @pl.when(step == pl.num_programs(0) - 1)
    def _():
        for h in (0, 1):
            for k in range(2 * LL):
                out_ref[k * ML : (k + 1) * ML, h * LANES : (h + 1) * LANES] = held[
                    h, k * M_PITCH : k * M_PITCH + ML, :
                ]


def legendre_adjoint(table, rows):
    whole = lambda shape: pl.BlockSpec(shape, lambda i: (0,) * len(shape))
    out = pl.pallas_call(
        adjoint_kernel,
        grid=(ML // ADJOINT_STEP,),
        in_specs=[
            VMEM_SPEC,
            VMEM_SPEC,
        ],
        out_specs=whole((ROWS, N)),
        scratch_shapes=[
            pltpu.VMEM((2, 2, LL * L_PITCH, LANES), f32),
            pltpu.VMEM((2, 2 * LL * M_PITCH, LANES), f32),
        ],
        out_shape=jax.ShapeDtypeStruct((ROWS, N), f32),
        compiler_params=params(12),
        name="legendre_adjoint",
    )(on_chip(table), rows)
    return out.reshape(2, LL, ML, N)


def waves_kernel(rows_ref, table_ref, after_ref, out_ref, token_ref, held):
    del after_ref
    token_ref[...] = jnp.zeros_like(token_ref)
    for pair in range(N_LAT // 2):
        for l in range(LL):
            pieces = [
                rows_ref[(2 * pair + k) * CLAT : (2 * pair + k + 1) * CLAT, l * 64 : (l + 1) * 64]
                for k in (0, 1)
            ]
            held[pair, pl.ds(l, CLAT, stride=LL), :] = jnp.concatenate(pieces, axis=1).astype(f32)
    waves = jnp.concatenate([held[k].astype(bf16) for k in range(N_LAT // 2)], axis=1)
    out_ref[...] = dot_nt(table_ref[...], waves).astype(bf16)


def waves_to_grid(rows, table, after):
    return pl.pallas_call(
        waves_kernel,
        in_specs=[VMEM_SPEC, VMEM_SPEC, pl.BlockSpec(memory_space=pl.ANY)],
        out_shape=[pltpu.VMEM((NLON, JL), bf16), pltpu.HBM((8, LANES), f32)],
        out_specs=[VMEM_SPEC, VMEM_SPEC],
        scratch_shapes=[pltpu.VMEM((N_LAT // 2, JL, LANES), f32)],
        compiler_params=params(12),
        name="waves",
    )(rows, table, in_hbm(after))


def waves_adjoint_kernel(grid_ref, table_ref, out_ref, held):
    value = dot_tn(grid_ref[...], table_ref[...])
    for k in range(N_LAT // 2):
        held[k] = value[:, k * LANES : (k + 1) * LANES]
    for pair in range(N_LAT // 2):
        for lp in range(LL // 2):
            two = [held[pair, pl.ds(2 * lp + k, CLAT, stride=LL), :] for k in (0, 1)]
            for k in (0, 1):
                piece = jnp.concatenate([v[:, k * 64 : (k + 1) * 64] for v in two], axis=1)
                first = (2 * pair + k) * CLAT
                out_ref[first : first + CLAT, lp * LANES : (lp + 1) * LANES] = piece.astype(bf16)


def grid_to_waves(grid, table):
    return pl.pallas_call(
        waves_adjoint_kernel,
        in_specs=[VMEM_SPEC, VMEM_SPEC],
        out_shape=pltpu.VMEM((NLAT, ROWS), bf16),
        out_specs=VMEM_SPEC,
        scratch_shapes=[pltpu.VMEM((N_LAT // 2, JL, LANES), f32)],
        compiler_params=params(12),
        name="waves_adjoint",
    )(grid, table)


GROUP = 256
GROUPS = CELLS // GROUP
TILE = 240
SUM_TILE = 2 * TILE
ROW_TILES = -(-(CAP + 7 * GROUPS) // SUM_TILE)
MAX_ROWS = ROW_TILES * SUM_TILE


def assign_rows(count, columns):
    slot = lax.broadcasted_iota(jnp.int32, (1, CAP), 1)
    valid = slot < count
    group = jnp.where(valid, lax.shift_right_logical(columns, 8), -1)
    inner = lax.broadcasted_iota(jnp.int32, (GROUP, CAP), 0) == (columns & (GROUP - 1))
    inner = jnp.where(inner, 1.0, 0.0).astype(bf16)
    in_group = lax.broadcasted_iota(jnp.int32, (16, CAP), 0) == group
    seen = dot_nt(jnp.where(in_group, 1.0, 0.0).astype(bf16), inner)
    used = jnp.where(seen > 0.5, 1.0, 0.0)
    before = lax.broadcasted_iota(jnp.int32, (GROUP, GROUP), 0) < lax.broadcasted_iota(
        jnp.int32, (GROUP, GROUP), 1
    )
    rank = dot_nn(used.astype(bf16), jnp.where(before, 1.0, 0.0).astype(bf16))
    padded = jnp.floor((jnp.sum(used, axis=1, keepdims=True) + 7.0) * 0.125) * 8.0
    padded = jnp.broadcast_to(padded, (16, LANES))
    sub = lax.broadcasted_iota(jnp.int32, (16, LANES), 0)
    first = jnp.zeros((16, LANES), f32)
    for g in range(GROUPS):
        first = first + jnp.where(sub > g, padded[g : g + 1, :], 0.0)
    of_slot = dot_nn(rank.astype(bf16), inner) + first[:, 0:1]
    row = jnp.sum(jnp.where(in_group, of_slot, 0.0), axis=0, keepdims=True)
    row = jnp.where(valid, row, -1.0).astype(jnp.int32)
    return row, jnp.where(used > 0.5, rank, -1.0), first


def sum_rows(step, total, row_of_slot, masked, sum_ref):
    @pl.when(step * SUM_TILE < total)
    def _():
        row = lax.broadcasted_iota(jnp.int32, (SUM_TILE, CAP), 0) + step * SUM_TILE
        hit = jnp.where(row == row_of_slot, 1.0, 0.0).astype(bf16)
        sum_ref[...] = dot_nn(hit, masked[...])


def active_channels(pairs_ref, value, masked):
    channel = lax.broadcasted_iota(jnp.int32, (LANES, LANES), 1)
    for i in range(CAP // LANES):
        r = slice(i * LANES, (i + 1) * LANES)
        used = jnp.transpose(jnp.broadcast_to(2 * pairs_ref[:, r], (LANES, LANES)))
        for c in range(CHAN // LANES):
            lanes = slice(c * LANES, (c + 1) * LANES)
            masked[r, lanes] = jnp.where(
                channel + c * LANES < used, value(r, lanes), 0.0
            ).astype(bf16)


def sums_kernel(
    count_ref,
    columns_ref,
    pairs_ref,
    obs_ref,
    after_ref,
    sum_ref,
    row_ref,
    rank_ref,
    first_ref,
    masked,
    total_ref,
):
    del after_ref
    step = pl.program_id(0)

    @pl.when(step == 0)
    def _():
        row, rank, first = assign_rows(count_ref[0], columns_ref[...])
        row_ref[...] = row
        rank_ref[...] = rank
        first_ref[...] = first.astype(jnp.int32)
        total_ref[0] = jnp.max(first).astype(jnp.int32)
        active_channels(pairs_ref, lambda r, lanes: obs_ref[r, lanes].astype(f32), masked)

    sum_rows(step, total_ref[0], row_ref[...], masked, sum_ref)


def seen_kernel(first_ref, pairs_ref, row_ref, after_ref, sum_ref, masked):
    del after_ref
    step = pl.program_id(0)

    @pl.when(step == 0)
    def _():
        active_channels(pairs_ref, lambda r, lanes: 1.0, masked)

    sum_rows(step, first_ref[GROUPS, 0], row_ref[...], masked, sum_ref)


ROW_COST = pl.CostEstimate(
    flops=2 * MAX_ROWS * CAP * CHAN, transcendentals=0, bytes_accessed=MAX_ROWS * CHAN * 4
)


def row_sums(counts, columns, pairs, obs, after):
    whole = lambda shape: pl.BlockSpec(shape, lambda i, *_: (0,) * len(shape))
    return pl.pallas_call(
        sums_kernel,
        grid_spec=pltpu.PrefetchScalarGridSpec(
            num_scalar_prefetch=1,
            grid=(ROW_TILES,),
            in_specs=[
                whole((1, CAP)),
                whole((1, CAP)),
                whole((CAP, CHAN)),
                pl.BlockSpec(memory_space=pl.ANY),
            ],
            out_specs=[
                pl.BlockSpec((SUM_TILE, CHAN), lambda i, *_: (i, 0)),
                whole((1, CAP)),
                whole((16, GROUP)),
                whole((16, LANES)),
            ],
            scratch_shapes=[pltpu.VMEM((CAP, CHAN), bf16), pltpu.SMEM((1,), jnp.int32)],
        ),
        out_shape=[
            pltpu.HBM((MAX_ROWS, CHAN), f32),
            pltpu.HBM((1, CAP), jnp.int32),
            pltpu.HBM((16, GROUP), f32),
            pltpu.HBM((16, LANES), jnp.int32),
        ],
        compiler_params=params(24),
        cost_estimate=ROW_COST,
        name="row_sums",
    )(counts, in_hbm(columns), in_hbm(pairs), in_hbm(obs), in_hbm(after))


def row_seen(first, pairs, row, after):
    whole = lambda shape: pl.BlockSpec(shape, lambda i: (0,) * len(shape))
    return pl.pallas_call(
        seen_kernel,
        grid=(ROW_TILES,),
        in_specs=[
            pl.BlockSpec(memory_space=pltpu.SMEM),
            whole((1, CAP)),
            whole((1, CAP)),
            pl.BlockSpec(memory_space=pl.ANY),
        ],
        out_specs=pl.BlockSpec((SUM_TILE, CHAN), lambda i: (i, 0)),
        scratch_shapes=[pltpu.VMEM((CAP, CHAN), bf16)],
        out_shape=pltpu.HBM((MAX_ROWS, CHAN), f32),
        compiler_params=params(24),
        cost_estimate=ROW_COST,
        name="row_seen",
    )(in_hbm(first), in_hbm(pairs), in_hbm(row), in_hbm(after))


J_STEP = 16
X_ROWS = 16
PART = J_STEP * CLON


def silu_and_slope(v):
    half = 0.5 * v
    sig = 0.5 * jnp.tanh(half) + 0.5
    act = v * sig
    return act, sig + act - act * sig


def swap_blocks(v):
    lane = lax.broadcasted_iota(jnp.int32, v[0].shape, 1)
    v = list(v)
    for bit in range(4):
        gap = 1 << bit
        upper = (lane & (8 * gap)) != 0
        for s in range(N_LEV):
            if s & gap:
                continue
            a, b = v[s], v[s + gap]
            v[s] = jnp.where(upper, pltpu.roll(b, 8 * gap, 1), a)
            v[s + gap] = jnp.where(upper, b, pltpu.roll(a, LANES - 8 * gap, 1))
    return v


def network_kernel(
    first_ref,
    inc_ref,
    back_hbm,
    rank_ref,
    sum_hbm,
    seen_hbm,
    chan_ref,
    w_in_hbm,
    w_mid,
    w_out_hbm,
    grad_hbm,
    send_ref,
    state,
    packed,
    packed_grad,
    w_twice,
    w_last,
    back_buf,
    grads,
    sum_buf,
    seen_buf,
    sems,
    part_sems,
):
    total = first_ref[GROUPS, 0]
    tiles = (total + (TILE - 1)) // TILE

    def fetches(t, slot):
        r = pl.ds(pl.multiple_of(t * TILE, 8), TILE)
        return (
            pltpu.make_async_copy(sum_hbm.at[r, :], sum_buf.at[slot], sems.at[0, slot]),
            pltpu.make_async_copy(seen_hbm.at[r, :], seen_buf.at[slot], sems.at[1, slot]),
        )

    def part_copy(k, src, dst, jc):
        r = pl.ds(pl.multiple_of(jc * PART, PART), PART)
        return pltpu.make_async_copy(src.at[r, :], dst.at[r, :], part_sems.at[k, jc])

    for jc in range(CLAT // J_STEP):
        part_copy(0, back_hbm, back_buf, jc).start()
    weights = [
        pltpu.make_async_copy(w_in_hbm, w_twice.at[pl.ds(0, LEV), :], part_sems.at[2, 0]),
        pltpu.make_async_copy(w_in_hbm, w_twice.at[pl.ds(LEV, LEV), :], part_sems.at[2, 1]),
        pltpu.make_async_copy(w_out_hbm, w_last, part_sems.at[2, 2]),
    ]
    for fetch in weights:
        fetch.start()
    for fetch in fetches(0, 0):
        fetch.start()

    def to_state(jc, _):
        part_copy(0, back_hbm, back_buf, jc).wait()
        lanes = pl.ds(pl.multiple_of(jc * LANES, LANES), LANES)
        for part in range(CLON // X_ROWS):
            x0 = part * X_ROWS
            v = [
                inc_ref[s * CLON + x0 : s * CLON + x0 + X_ROWS, lanes].astype(f32)
                for s in range(N_LEV)
            ]
            v = swap_blocks(v)
            for j in range(J_STEP):
                r = pl.ds(pl.multiple_of((jc * J_STEP + j) * CLON + x0, 16), X_ROWS)
                grid_state = back_buf[r, :].astype(f32) + v[j]
                high = grid_state.astype(bf16)
                state[r, :LEV] = high
                state[r, LEV:] = (grid_state - high.astype(f32)).astype(bf16)
        return 0

    lax.fori_loop(0, CLAT // J_STEP, to_state, 0)

    def group_rows(g):
        first = pl.ds(pl.multiple_of(first_ref[g, 0], 8), GROUP)
        row = lax.broadcasted_iota(jnp.int32, (GROUP, GROUP), 0).astype(f32)
        pick = jnp.where(row == rank_ref[g : g + 1, :], 1.0, 0.0).astype(bf16)
        return first, slice(g * GROUP, (g + 1) * GROUP), pick

    for g in range(GROUPS):
        rows, cells, pick = group_rows(g)
        packed[rows, :] = dot_nn(pick, state[cells, :])
    packed[pl.ds(pl.multiple_of(total, 8), TILE), :] = jnp.zeros((TILE, 2 * LEV), f32)

    for fetch in weights:
        fetch.wait()

    def one_tile(t, _):
        slot = lax.rem(t, 2)
        for fetch in fetches(t, slot):
            fetch.wait()

        @pl.when(t + 1 < tiles)
        def _():
            for fetch in fetches(t + 1, 1 - slot):
                fetch.start()

        r = pl.ds(pl.multiple_of(t * TILE, 8), TILE)
        act1, slope1 = silu_and_slope(dot_nn(packed[r, :].astype(bf16), w_twice[...]))
        act2, slope2 = silu_and_slope(dot_nn(act1.astype(bf16), w_mid[...]))
        evolved = dot_nn(act2.astype(bf16), w_last[...])
        misfit = (chan_ref[...] * (seen_buf[slot] * evolved - sum_buf[slot])).astype(bf16)
        back2 = (dot_nt(misfit, w_last[...]) * slope2).astype(bf16)
        back1 = (dot_nt(back2, w_mid[...]) * slope1).astype(bf16)
        packed_grad[r, :] = dot_nt(back1, w_twice[:LEV])
        return 0

    lax.fori_loop(0, tiles, one_tile, 0)
    packed_grad[pl.ds(pl.multiple_of(tiles * TILE, 8), GROUP), :] = jnp.zeros((GROUP, LEV), f32)
    for g in range(GROUPS):
        rows, cells, pick = group_rows(g)
        value = packed_grad[rows, :]
        high = value.astype(bf16)
        low = (value - high.astype(f32)).astype(bf16)
        value = dot_tn(pick, jnp.concatenate([high, low], axis=1))
        grads[cells, :] = value[:, :LEV] + value[:, LEV:]
        if (g + 1) * GROUP % PART == 0:
            part_copy(1, grads, grad_hbm, g * GROUP // PART).start()

    def to_send(jc, _):
        lanes = pl.ds(pl.multiple_of(jc * LANES, LANES), LANES)
        for part in range(CLON // X_ROWS):
            x0 = part * X_ROWS
            v = [
                grads[pl.ds(pl.multiple_of((jc * J_STEP + j) * CLON + x0, 16), X_ROWS), :]
                for j in range(J_STEP)
            ]
            v = swap_blocks(v)
            for s in range(N_LEV):
                send_ref[s * CLON + x0 : s * CLON + x0 + X_ROWS, lanes] = v[s].astype(bf16)
        return 0

    lax.fori_loop(0, CLAT // J_STEP, to_send, 0)
    for jc in range(CLAT // J_STEP):
        part_copy(1, grads, grad_hbm, jc).wait()


def network(first, inc, background, rank, sums, seen, channel_weight, w_in, w_mid, w_out):
    anywhere = pl.BlockSpec(memory_space=pl.ANY)
    grad, send = pl.pallas_call(
        network_kernel,
        in_specs=[
            pl.BlockSpec(memory_space=pltpu.SMEM),
            VMEM_SPEC,
            anywhere,
            VMEM_SPEC,
            anywhere,
            anywhere,
            VMEM_SPEC,
            anywhere,
            VMEM_SPEC,
            anywhere,
        ],
        out_specs=[anywhere, VMEM_SPEC],
        out_shape=[
            pltpu.HBM((CELLS, LEV), f32),
            pltpu.VMEM((NLON, JL), bf16),
        ],
        scratch_shapes=[
            pltpu.VMEM((CELLS, 2 * LEV), bf16),
            pltpu.VMEM((MAX_ROWS + GROUP, 2 * LEV), f32),
            pltpu.VMEM((MAX_ROWS + GROUP, LEV), f32),
            pltpu.VMEM((2 * LEV, w_in.shape[1]), bf16),
            pltpu.VMEM(w_out.shape, bf16),
            pltpu.VMEM((CELLS, LEV), bf16),
            pltpu.VMEM((CELLS, LEV), f32),
            pltpu.VMEM((2, TILE, CHAN), f32),
            pltpu.VMEM((2, TILE, CHAN), f32),
            pltpu.SemaphoreType.DMA((2, 2)),
            pltpu.SemaphoreType.DMA((3, 3)),
        ],
        compiler_params=params(30),
        name="network",
    )(
        in_hbm(first),
        inc,
        in_hbm(background),
        in_hbm(rank),
        in_hbm(sums),
        in_hbm(seen),
        channel_weight,
        in_hbm(w_in),
        on_chip(w_mid),
        in_hbm(w_out),
    )
    return grad.reshape(CLAT, CLON, LEV), send


def exchange(rows, axis):
    return on_chip(lax.all_to_all(rows, axis, split_axis=0, concat_axis=0, tiled=True))


def per_device(
    spectral,
    background,
    columns,
    counts,
    radiances,
    used_pairs,
    channel_weight,
    weight_in,
    weight_mid,
    weight_out,
):
    table = on_chip(wave_table())
    lat_index = lax.axis_index("lat").astype(jnp.int32).reshape(1)
    legendre, fourier = legendre_transform(lat_index, spectral)
    sums, row, rank, first = row_sums(counts, columns, used_pairs, radiances[0], legendre)
    waves, token = waves_to_grid(exchange(fourier, "lat"), table, first)
    seen = row_seen(first, used_pairs, row, token)
    increment = exchange(waves, "lev")
    grid_grad, send = network(
        first,
        increment,
        background.reshape(CELLS, LEV),
        rank,
        sums,
        seen,
        channel_weight.reshape(1, CHAN),
        weight_in,
        weight_mid,
        weight_out,
    )
    coeff = exchange(grid_to_waves(exchange(send, "lev"), table), "lat")
    return (legendre_adjoint(legendre, coeff), grid_grad)


def solution(mesh):
    in_specs = (
        P(None, "lev", "lat", None),
        P("lat", "lev", None),
        P(("lat", "lev"), None),
        P(("lat", "lev")),
        P(("lat", "lev"), None, None),
        P(("lat", "lev"), None),
        P(),
        P(),
        P(),
        P(),
    )
    out_specs = (P(None, "lev", "lat", None), P("lat", "lev", None))
    return jax.shard_map(
        per_device, mesh=mesh, in_specs=in_specs, out_specs=out_specs, check_vma=False
    )
```

```python
import functools
import math

import jax
import jax.numpy as jnp
import numpy as np
from jax import lax
from jax.experimental import pallas as pl
from jax.experimental.pallas import tpu as pltpu
from jax.sharding import PartitionSpec as P

LEV = 128
M = 256
N = 256
NLAT = 384
NLON = 768
HALF = NLAT // 2
LANES = 128
N_LAT = 8
N_LEV = 16
ML = M // N_LAT
LL = LEV // N_LEV
CLAT = NLAT // N_LAT
CLON = NLON // N_LEV
CELLS = CLAT * CLON
CAP = 2048
CHAN = 512
JL = CLAT * LL
KM = 2 * M
M_PITCH = ML + 8
L_PITCH = 2 * ML + 8
ROWS = 2 * LL * ML

RESCALE_TOP = 2.0**30
RESCALE_BY = 2.0 ** (-60)
RESCALE_LOG = 60.0 * math.log(2.0)
HALF_LOG = 0.5 * math.log(0.5)

bf16 = jnp.bfloat16
f32 = jnp.float32


def params(mib):
    return pltpu.CompilerParams(vmem_limit_bytes=mib << 20)


def on_chip(array):
    return pltpu.with_memory_space_constraint(array, pltpu.VMEM)


def in_hbm(array):
    return pltpu.with_memory_space_constraint(array, pltpu.HBM)


VMEM_SPEC = pl.BlockSpec(memory_space=pltpu.VMEM)


def dot_nt(a, b):
    return lax.dot_general(a, b, (((1,), (1,)), ((), ())), preferred_element_type=f32)


def dot_tn(a, b):
    return lax.dot_general(a, b, (((0,), (0,)), ((), ())), preferred_element_type=f32)


def dot_nn(a, b):
    return jnp.dot(a, b, preferred_element_type=f32)


def geometry():
    lat = (0.5 - (np.arange(256, dtype=np.float64) + 0.5) / NLAT) * np.pi
    valid = np.arange(256) < HALF
    sin_lat = np.where(valid, np.sin(lat), 0.0)
    log_cos = np.where(valid, np.log(np.cos(np.where(valid, lat, 0.0))), 0.0)
    rows = np.zeros((8, 256), np.float32)
    rows[0], rows[1], rows[2] = sin_lat, log_cos, valid
    k = np.arange(1, M, dtype=np.float64)
    steps = 0.5 * np.log((2.0 * k + 1.0) / (2.0 * k))
    log_norm = np.concatenate([[0.0], np.cumsum(steps)]) + HALF_LOG
    return rows, np.repeat(log_norm[:, None], LANES, axis=1).astype(np.float32)


def wave_table():
    m = np.arange(M)
    phase = (np.arange(NLON)[:, None] * m[None, :] % NLON) * (2.0 * np.pi / NLON)
    weight = np.where(m == 0, 1.0, 2.0) / M
    pair = np.stack([weight * np.cos(phase), -weight * np.sin(phase)])
    table = pair.reshape(2, NLON, N_LAT, ML).transpose(1, 2, 0, 3).reshape(NLON, KM)
    return jnp.asarray(table, f32).astype(bf16)


M_STEP = 8
ADJOINT_STEP = 32


def legendre_kernel(
    lat_ref, geo_ref, norm_ref, spec_ref, p_hbm, four_ref, table, waves, halves, p_buf, sems
):
    groups = range(ML // 8)

    for h in (0, 1):
        for k in range(2 * LL):
            halves[h, k * M_PITCH : k * M_PITCH + ML, :] = spec_ref[
                k * ML : (k + 1) * ML, h * LANES : (h + 1) * LANES
            ]
    m0 = lat_ref[0] * ML
    sub = lax.broadcasted_iota(jnp.int32, (8, LANES), 0)
    mf = [(sub + (m0 + 8 * g)).astype(f32) for g in groups]
    m2 = [v * v for v in mf]
    zero = jnp.zeros((8, LANES), f32)
    x = [jnp.broadcast_to(geo_ref[0:1, h * LANES : (h + 1) * LANES], (8, LANES)) for h in (0, 1)]
    log_cos = [
        jnp.broadcast_to(geo_ref[1:2, h * LANES : (h + 1) * LANES], (8, LANES)) for h in (0, 1)
    ]
    valid = [
        jnp.broadcast_to(geo_ref[2:3, h * LANES : (h + 1) * LANES], (8, LANES)) for h in (0, 1)
    ]
    logs = [
        [norm_ref[pl.ds(m0 + 8 * g, 8), :] + mf[g] * log_cos[h] for h in (0, 1)] for g in groups
    ]

    def block(i, carry):
        prev, earlier, logs, eps_prev, nf = carry
        big = [
            [jnp.maximum(jnp.abs(prev[g][h]), jnp.abs(earlier[g][h])) > RESCALE_TOP for h in (0, 1)]
            for g in groups
        ]
        shrink = [[jnp.where(big[g][h], RESCALE_BY, 1.0) for h in (0, 1)] for g in groups]
        prev = [[prev[g][h] * shrink[g][h] for h in (0, 1)] for g in groups]
        earlier = [[earlier[g][h] * shrink[g][h] for h in (0, 1)] for g in groups]
        logs = [
            [jnp.where(big[g][h], logs[g][h] + RESCALE_LOG, logs[g][h]) for h in (0, 1)]
            for g in groups
        ]
        scale = [[jnp.exp(logs[g][h]) * valid[h] for h in (0, 1)] for g in groups]
        for k in range(8):
            n2 = nf * nf
            inv = 1.0 / jnp.maximum(4.0 * n2 - 1.0, 1.0)
            at = pl.multiple_of((i * 8 + k) * M_PITCH, 8)
            new = []
            eps = []
            for g in groups:
                t = n2 - m2[g]
                q = jnp.maximum(t, 1.0) * inv
                a = lax.rsqrt(q)
                eps.append(jnp.where(t > 0.0, q * a, 0.0))
                diag = nf == mf[g]
                row = []
                for h in (0, 1):
                    cur = (x[h] * prev[g][h] - eps_prev[g] * earlier[g][h]) * a
                    cur = jnp.where(diag, 1.0, cur)
                    table[h, pl.ds(at + 8 * g, 8), :] = cur * scale[g][h]
                    row.append(cur)
                new.append(row)
            prev, earlier, eps_prev = new, prev, eps
            nf = nf + 1.0
        return prev, earlier, logs, eps_prev, nf

    empty = [[zero, zero] for _ in groups]
    lax.fori_loop(0, N // 8, block, (empty, empty, logs, [zero for _ in groups], zero))

    lane = lax.broadcasted_iota(jnp.int32, (1, N), 1)
    alternate = jnp.where(lane % 2 == 0, 1.0, -1.0)
    def store(step):
        slot = lax.rem(step, 2)
        m = pl.ds(step * M_STEP, M_STEP)
        return pltpu.make_async_copy(p_buf.at[slot], p_hbm.at[m], sems.at[slot])

    def transform(step, _):
        slot = lax.rem(step, 2)

        @pl.when(step >= 2)
        def _():
            store(step - 2).wait()

        for k in range(M_STEP):
            m = step * M_STEP + k
            p_m = jnp.concatenate(
                [table[h, pl.ds(m, N, stride=M_PITCH), :].astype(bf16) for h in (0, 1)], axis=1
            )
            p_buf[slot, k] = p_m
            s = jnp.concatenate([halves[h, pl.ds(m, 2 * LL, stride=M_PITCH), :] for h in (0, 1)], axis=1)
            s = jnp.concatenate([s, s * (alternate if k % 2 == 0 else -alternate)], axis=0)
            high = s.astype(bf16)
            low = (s - high.astype(f32)).astype(bf16)
            out = dot_nn(jnp.concatenate([high, low], axis=0), p_m)
            out = out[: 4 * LL] + out[4 * LL :]
            for hemi in (0, 1):
                for c in (0, 1):
                    first = (hemi * 2 + c) * LL
                    for h in (0, 1):
                        waves[hemi, h, pl.ds(c * ML + m, LL, stride=L_PITCH), :] = out[
                            first : first + LL, h * LANES : (h + 1) * LANES
                        ]
        store(step).start()
        return 0

    steps = ML // M_STEP
    lax.fori_loop(0, steps, transform, 0)
    row = lax.broadcasted_iota(jnp.int32, (HALF, 256), 0)
    col = lax.broadcasted_iota(jnp.int32, (HALF, 256), 1)
    for hemi in (0, 1):
        pick = jnp.where(col == (row if hemi == 0 else HALF - 1 - row), 1.0, 0.0).astype(bf16)
        values = jnp.concatenate(
            [
                jnp.concatenate(
                    [
                        waves[hemi, h, l * L_PITCH : l * L_PITCH + 2 * ML, :].astype(bf16)
                        for h in (0, 1)
                    ],
                    axis=1,
                )
                for l in range(LL)
            ],
            axis=0,
        )
        four_ref[hemi * HALF : (hemi + 1) * HALF, :] = dot_nt(pick, values).astype(bf16)
    store(steps - 2).wait()
    store(steps - 1).wait()


def legendre_transform(lat_index, spectral):
    geo, norm = geometry()
    return pl.pallas_call(
        legendre_kernel,
        in_specs=[pl.BlockSpec(memory_space=pltpu.SMEM), VMEM_SPEC, VMEM_SPEC, VMEM_SPEC],
        out_specs=[pl.BlockSpec(memory_space=pl.ANY), VMEM_SPEC],
        scratch_shapes=[
            pltpu.VMEM((2, N * M_PITCH, LANES), f32),
            pltpu.VMEM((2, 2, LL * L_PITCH, LANES), f32),
            pltpu.VMEM((2, 2 * LL * M_PITCH, LANES), f32),
            pltpu.VMEM((2, M_STEP, N, 256), bf16),
            pltpu.SemaphoreType.DMA((2,)),
        ],
        out_shape=[
            pltpu.HBM((ML, N, 256), bf16),
            pltpu.VMEM((NLAT, ROWS), bf16),
        ],
        compiler_params=params(24),
        name="legendre",
    )(lat_index, in_hbm(jnp.asarray(geo)), in_hbm(jnp.asarray(norm)), in_hbm(spectral.reshape(ROWS, N)))


def adjoint_kernel(p_ref, rows_ref, out_ref, folded, held):
    step = pl.program_id(0)

    @pl.when(step == 0)
    def _():
        j = lax.broadcasted_iota(jnp.int32, (NLAT, 256), 0)
        col = lax.broadcasted_iota(jnp.int32, (NLAT, 256), 1)
        north = jnp.where(col == j, 1.0, 0.0)
        south = jnp.where((j >= HALF) & (col == NLAT - 1 - j), 1.0, 0.0)
        north = jnp.where(col < HALF, north, 0.0)
        for part, pick in ((0, north + south), (1, north - south)):
            value = dot_tn(rows_ref[...], pick.astype(bf16))
            for h in (0, 1):
                for l in range(LL):
                    folded[part, h, l * L_PITCH : l * L_PITCH + 2 * ML, :] = value[
                        l * 2 * ML : (l + 1) * 2 * ML, h * LANES : (h + 1) * LANES
                    ]

    lane = lax.broadcasted_iota(jnp.int32, (2 * LL, N), 1)
    for k in range(ADJOINT_STEP):
        m = step * ADJOINT_STEP + k
        pieces = []
        for part in (0, 1):
            for c in (0, 1):
                pieces.append(
                    jnp.concatenate(
                        [
                            folded[part, h, pl.ds(c * ML + m, LL, stride=L_PITCH), :]
                            for h in (0, 1)
                        ],
                        axis=1,
                    )
                )
        value = dot_nt(jnp.concatenate(pieces, axis=0).astype(bf16), p_ref[m])
        picked = jnp.where(lane % 2 == k % 2, value[: 2 * LL], value[2 * LL :])
        for h in (0, 1):
            held[h, pl.ds(m, 2 * LL, stride=M_PITCH), :] = picked[:, h * LANES : (h + 1) * LANES]

    @pl.when(step == pl.num_programs(0) - 1)
    def _():
        for h in (0, 1):
            for k in range(2 * LL):
                out_ref[k * ML : (k + 1) * ML, h * LANES : (h + 1) * LANES] = held[
                    h, k * M_PITCH : k * M_PITCH + ML, :
                ]


def legendre_adjoint(table, rows):
    whole = lambda shape: pl.BlockSpec(shape, lambda i: (0,) * len(shape))
    out = pl.pallas_call(
        adjoint_kernel,
        grid=(ML // ADJOINT_STEP,),
        in_specs=[
            VMEM_SPEC,
            VMEM_SPEC,
        ],
        out_specs=whole((ROWS, N)),
        scratch_shapes=[
            pltpu.VMEM((2, 2, LL * L_PITCH, LANES), f32),
            pltpu.VMEM((2, 2 * LL * M_PITCH, LANES), f32),
        ],
        out_shape=jax.ShapeDtypeStruct((ROWS, N), f32),
        compiler_params=params(12),
        name="legendre_adjoint",
    )(on_chip(table), rows)
    return out.reshape(2, LL, ML, N)


def waves_kernel(rows_ref, table_ref, after_ref, out_ref, token_ref, held):
    del after_ref
    token_ref[...] = jnp.zeros_like(token_ref)
    for pair in range(N_LAT // 2):
        for l in range(LL):
            pieces = [
                rows_ref[(2 * pair + k) * CLAT : (2 * pair + k + 1) * CLAT, l * 64 : (l + 1) * 64]
                for k in (0, 1)
            ]
            held[pair, pl.ds(l, CLAT, stride=LL), :] = jnp.concatenate(pieces, axis=1).astype(f32)
    waves = jnp.concatenate([held[k].astype(bf16) for k in range(N_LAT // 2)], axis=1)
    out_ref[...] = dot_nt(table_ref[...], waves).astype(bf16)


def waves_to_grid(rows, table, after):
    return pl.pallas_call(
        waves_kernel,
        in_specs=[VMEM_SPEC, VMEM_SPEC, pl.BlockSpec(memory_space=pl.ANY)],
        out_shape=[pltpu.VMEM((NLON, JL), bf16), pltpu.HBM((8, LANES), f32)],
        out_specs=[VMEM_SPEC, VMEM_SPEC],
        scratch_shapes=[pltpu.VMEM((N_LAT // 2, JL, LANES), f32)],
        compiler_params=params(12),
        name="waves",
    )(rows, table, in_hbm(after))


def waves_adjoint_kernel(grid_ref, table_ref, out_ref, held):
    value = dot_tn(grid_ref[...], table_ref[...])
    for k in range(N_LAT // 2):
        held[k] = value[:, k * LANES : (k + 1) * LANES]
    for pair in range(N_LAT // 2):
        for lp in range(LL // 2):
            two = [held[pair, pl.ds(2 * lp + k, CLAT, stride=LL), :] for k in (0, 1)]
            for k in (0, 1):
                piece = jnp.concatenate([v[:, k * 64 : (k + 1) * 64] for v in two], axis=1)
                first = (2 * pair + k) * CLAT
                out_ref[first : first + CLAT, lp * LANES : (lp + 1) * LANES] = piece.astype(bf16)


def grid_to_waves(grid, table):
    return pl.pallas_call(
        waves_adjoint_kernel,
        in_specs=[VMEM_SPEC, VMEM_SPEC],
        out_shape=pltpu.VMEM((NLAT, ROWS), bf16),
        out_specs=VMEM_SPEC,
        scratch_shapes=[pltpu.VMEM((N_LAT // 2, JL, LANES), f32)],
        compiler_params=params(12),
        name="waves_adjoint",
    )(grid, table)


GROUP = 256
GROUPS = CELLS // GROUP
TILE = 240
SUM_TILE = 2 * TILE
QUARTER = CAP // 4
ROW_TILES = -(-(CAP + 7 * GROUPS) // SUM_TILE)
MAX_ROWS = ROW_TILES * SUM_TILE


def assign_rows(count, columns):
    slot = lax.broadcasted_iota(jnp.int32, (1, CAP), 1)
    valid = slot < count
    group = jnp.where(valid, lax.shift_right_logical(columns, 8), -1)
    inner = lax.broadcasted_iota(jnp.int32, (GROUP, CAP), 0) == (columns & (GROUP - 1))
    inner = jnp.where(inner, 1.0, 0.0).astype(bf16)
    in_group = lax.broadcasted_iota(jnp.int32, (16, CAP), 0) == group
    seen = dot_nt(jnp.where(in_group, 1.0, 0.0).astype(bf16), inner)
    used = jnp.where(seen > 0.5, 1.0, 0.0)
    before = lax.broadcasted_iota(jnp.int32, (GROUP, GROUP), 0) < lax.broadcasted_iota(
        jnp.int32, (GROUP, GROUP), 1
    )
    rank = dot_nn(used.astype(bf16), jnp.where(before, 1.0, 0.0).astype(bf16))
    padded = jnp.floor((jnp.sum(used, axis=1, keepdims=True) + 7.0) * 0.125) * 8.0
    padded = jnp.broadcast_to(padded, (16, LANES))
    sub = lax.broadcasted_iota(jnp.int32, (16, LANES), 0)
    first = jnp.zeros((16, LANES), f32)
    for g in range(GROUPS):
        first = first + jnp.where(sub > g, padded[g : g + 1, :], 0.0)
    of_slot = dot_nn(rank.astype(bf16), inner) + first[:, 0:1]
    row = jnp.sum(jnp.where(in_group, of_slot, 0.0), axis=0, keepdims=True)
    row = jnp.where(valid, row, -1.0).astype(jnp.int32)
    return row, jnp.where(used > 0.5, rank, -1.0), first


def write_sums(total, row_of_slot, masked, tile_buf, out_hbm, sems):
    tiles = (total + (SUM_TILE - 1)) // SUM_TILE

    def store(t):
        slot = lax.rem(t, 2)
        r = pl.ds(pl.multiple_of(t * SUM_TILE, 8), SUM_TILE)
        return pltpu.make_async_copy(tile_buf.at[slot], out_hbm.at[r, :], sems.at[slot])

    def one_tile(t, _):
        @pl.when(t >= 2)
        def _():
            store(t - 2).wait()

        row = lax.broadcasted_iota(jnp.int32, (SUM_TILE, CAP), 0) + t * SUM_TILE
        hit = jnp.where(row == row_of_slot[...], 1.0, 0.0).astype(bf16)
        tile_buf[lax.rem(t, 2)] = dot_nn(hit, masked[...])
        store(t).start()
        return 0

    lax.fori_loop(0, tiles, one_tile, 0)

    @pl.when(tiles >= 2)
    def _():
        store(tiles - 2).wait()

    store(tiles - 1).wait()


def active_channels(part, pairs_ref, value, masked):
    channel = lax.broadcasted_iota(jnp.int32, (LANES, LANES), 1)
    for i in range(part * QUARTER // LANES, (part + 1) * QUARTER // LANES):
        r = slice(i * LANES, (i + 1) * LANES)
        used = jnp.transpose(jnp.broadcast_to(2 * pairs_ref[:, r], (LANES, LANES)))
        for c in range(CHAN // LANES):
            lanes = slice(c * LANES, (c + 1) * LANES)
            masked[r, lanes] = jnp.where(
                channel + c * LANES < used, value(r, lanes), 0.0
            ).astype(bf16)


def sums_kernel(
    count_ref,
    columns_ref,
    pairs_ref,
    obs_hbm,
    after_ref,
    sum_hbm,
    row_ref,
    rank_ref,
    first_ref,
    obs,
    masked,
    tile_buf,
    sems,
    obs_sems,
):
    del after_ref

    def fetch(part):
        r = pl.ds(part * QUARTER, QUARTER)
        return pltpu.make_async_copy(obs_hbm.at[r, :], obs.at[r, :], obs_sems.at[part])

    for part in range(4):
        fetch(part).start()
    row, rank, first = assign_rows(count_ref[0], columns_ref[...])
    row_ref[...] = row
    rank_ref[...] = rank
    first_ref[...] = first.astype(jnp.int32)
    for part in range(4):
        fetch(part).wait()
        active_channels(part, pairs_ref, lambda r, lanes: obs[r, lanes].astype(f32), masked)
    write_sums(jnp.max(first).astype(jnp.int32), row_ref, masked, tile_buf, sum_hbm, sems)


def seen_kernel(first_ref, pairs_ref, row_ref, after_ref, sum_hbm, masked, tile_buf, sems):
    del after_ref
    for part in range(4):
        active_channels(part, pairs_ref, lambda r, lanes: 1.0, masked)
    write_sums(first_ref[GROUPS, 0], row_ref, masked, tile_buf, sum_hbm, sems)


ROW_COST = pl.CostEstimate(
    flops=2 * MAX_ROWS * CAP * CHAN, transcendentals=0, bytes_accessed=MAX_ROWS * CHAN * 4
)


SUM_SCRATCH = [
    pltpu.VMEM((CAP, CHAN), bf16),
    pltpu.VMEM((2, SUM_TILE, CHAN), f32),
    pltpu.SemaphoreType.DMA((2,)),
]


def row_sums(counts, columns, pairs, obs, after):
    anywhere = pl.BlockSpec(memory_space=pl.ANY)
    return pl.pallas_call(
        sums_kernel,
        in_specs=[
            pl.BlockSpec(memory_space=pltpu.SMEM),
            VMEM_SPEC,
            VMEM_SPEC,
            anywhere,
            anywhere,
        ],
        out_specs=[anywhere, VMEM_SPEC, VMEM_SPEC, VMEM_SPEC],
        scratch_shapes=[pltpu.VMEM((CAP, CHAN), bf16)]
        + SUM_SCRATCH
        + [pltpu.SemaphoreType.DMA((4,))],
        out_shape=[
            pltpu.HBM((MAX_ROWS, CHAN), f32),
            pltpu.HBM((1, CAP), jnp.int32),
            pltpu.HBM((16, GROUP), f32),
            pltpu.HBM((16, LANES), jnp.int32),
        ],
        compiler_params=params(24),
        cost_estimate=ROW_COST,
        name="row_sums",
    )(counts, in_hbm(columns), in_hbm(pairs), in_hbm(obs), in_hbm(after))


def row_seen(first, pairs, row, after):
    anywhere = pl.BlockSpec(memory_space=pl.ANY)
    return pl.pallas_call(
        seen_kernel,
        in_specs=[pl.BlockSpec(memory_space=pltpu.SMEM), VMEM_SPEC, VMEM_SPEC, anywhere],
        out_specs=anywhere,
        scratch_shapes=SUM_SCRATCH,
        out_shape=pltpu.HBM((MAX_ROWS, CHAN), f32),
        compiler_params=params(24),
        cost_estimate=ROW_COST,
        name="row_seen",
    )(in_hbm(first), in_hbm(pairs), in_hbm(row), in_hbm(after))


J_STEP = 16
X_ROWS = 16
PART = J_STEP * CLON


def silu_and_slope(v):
    half = 0.5 * v
    sig = 0.5 * jnp.tanh(half) + 0.5
    act = v * sig
    return act, sig + act - act * sig


def swap_blocks(v):
    lane = lax.broadcasted_iota(jnp.int32, v[0].shape, 1)
    v = list(v)
    for bit in range(4):
        gap = 1 << bit
        upper = (lane & (8 * gap)) != 0
        for s in range(N_LEV):
            if s & gap:
                continue
            a, b = v[s], v[s + gap]
            v[s] = jnp.where(upper, pltpu.roll(b, 8 * gap, 1), a)
            v[s + gap] = jnp.where(upper, b, pltpu.roll(a, LANES - 8 * gap, 1))
    return v


def network_kernel(
    first_ref,
    inc_ref,
    back_hbm,
    rank_ref,
    sum_hbm,
    seen_hbm,
    chan_ref,
    w_in_hbm,
    w_mid,
    w_out_hbm,
    grad_hbm,
    send_ref,
    state,
    picks,
    packed,
    packed_grad,
    w_twice,
    w_last,
    back_buf,
    grads,
    sum_buf,
    seen_buf,
    sems,
    part_sems,
):
    total = first_ref[GROUPS, 0]
    tiles = (total + (TILE - 1)) // TILE

    def fetches(t, slot):
        r = pl.ds(pl.multiple_of(t * TILE, 8), TILE)
        return (
            pltpu.make_async_copy(sum_hbm.at[r, :], sum_buf.at[slot], sems.at[0, slot]),
            pltpu.make_async_copy(seen_hbm.at[r, :], seen_buf.at[slot], sems.at[1, slot]),
        )

    def part_copy(k, src, dst, jc):
        r = pl.ds(pl.multiple_of(jc * PART, PART), PART)
        return pltpu.make_async_copy(src.at[r, :], dst.at[r, :], part_sems.at[k, jc])

    for jc in range(CLAT // J_STEP):
        part_copy(0, back_hbm, back_buf, jc).start()
    weights = [
        pltpu.make_async_copy(w_in_hbm, w_twice.at[pl.ds(0, LEV), :], part_sems.at[2, 0]),
        pltpu.make_async_copy(w_in_hbm, w_twice.at[pl.ds(LEV, LEV), :], part_sems.at[2, 1]),
        pltpu.make_async_copy(w_out_hbm, w_last, part_sems.at[2, 2]),
    ]
    for fetch in weights:
        fetch.start()
    for fetch in fetches(0, 0):
        fetch.start()

    row = lax.broadcasted_iota(jnp.int32, (GROUP, GROUP), 0).astype(f32)
    for g in range(GROUPS):
        picks[g] = jnp.where(row == rank_ref[g : g + 1, :], 1.0, 0.0).astype(bf16)

    def to_state(jc, _):
        part_copy(0, back_hbm, back_buf, jc).wait()
        lanes = pl.ds(pl.multiple_of(jc * LANES, LANES), LANES)
        for part in range(CLON // X_ROWS):
            x0 = part * X_ROWS
            v = [
                inc_ref[s * CLON + x0 : s * CLON + x0 + X_ROWS, lanes].astype(f32)
                for s in range(N_LEV)
            ]
            v = swap_blocks(v)
            for j in range(J_STEP):
                r = pl.ds(pl.multiple_of((jc * J_STEP + j) * CLON + x0, 16), X_ROWS)
                grid_state = back_buf[r, :].astype(f32) + v[j]
                high = grid_state.astype(bf16)
                state[r, :LEV] = high
                state[r, LEV:] = (grid_state - high.astype(f32)).astype(bf16)
        return 0

    lax.fori_loop(0, CLAT // J_STEP, to_state, 0)

    def group_rows(g):
        first = pl.ds(pl.multiple_of(first_ref[g, 0], 8), GROUP)
        return first, slice(g * GROUP, (g + 1) * GROUP), picks[g]

    for g in range(GROUPS):
        rows, cells, pick = group_rows(g)
        packed[rows, :] = dot_nn(pick, state[cells, :])
    packed[pl.ds(pl.multiple_of(total, 8), TILE), :] = jnp.zeros((TILE, 2 * LEV), f32)

    for fetch in weights:
        fetch.wait()

    def one_tile(t, _):
        slot = lax.rem(t, 2)
        for fetch in fetches(t, slot):
            fetch.wait()

        @pl.when(t + 1 < tiles)
        def _():
            for fetch in fetches(t + 1, 1 - slot):
                fetch.start()

        r = pl.ds(pl.multiple_of(t * TILE, 8), TILE)
        act1, slope1 = silu_and_slope(dot_nn(packed[r, :].astype(bf16), w_twice[...]))
        act2, slope2 = silu_and_slope(dot_nn(act1.astype(bf16), w_mid[...]))
        evolved = dot_nn(act2.astype(bf16), w_last[...])
        misfit = (chan_ref[...] * (seen_buf[slot] * evolved - sum_buf[slot])).astype(bf16)
        back2 = (dot_nt(misfit, w_last[...]) * slope2).astype(bf16)
        back1 = (dot_nt(back2, w_mid[...]) * slope1).astype(bf16)
        packed_grad[r, :] = dot_nt(back1, w_twice[:LEV])
        return 0

    lax.fori_loop(0, tiles, one_tile, 0)
    packed_grad[pl.ds(pl.multiple_of(tiles * TILE, 8), GROUP), :] = jnp.zeros((GROUP, LEV), f32)
    for g in range(GROUPS):
        rows, cells, pick = group_rows(g)
        value = packed_grad[rows, :]
        high = value.astype(bf16)
        low = (value - high.astype(f32)).astype(bf16)
        value = dot_tn(pick, jnp.concatenate([high, low], axis=1))
        grads[cells, :] = value[:, :LEV] + value[:, LEV:]
        if (g + 1) * GROUP % PART == 0:
            part_copy(1, grads, grad_hbm, g * GROUP // PART).start()

    def to_send(jc, _):
        lanes = pl.ds(pl.multiple_of(jc * LANES, LANES), LANES)
        for part in range(CLON // X_ROWS):
            x0 = part * X_ROWS
            v = [
                grads[pl.ds(pl.multiple_of((jc * J_STEP + j) * CLON + x0, 16), X_ROWS), :]
                for j in range(J_STEP)
            ]
            v = swap_blocks(v)
            for s in range(N_LEV):
                send_ref[s * CLON + x0 : s * CLON + x0 + X_ROWS, lanes] = v[s].astype(bf16)
        return 0

    lax.fori_loop(0, CLAT // J_STEP, to_send, 0)
    for jc in range(CLAT // J_STEP):
        part_copy(1, grads, grad_hbm, jc).wait()


def network(first, inc, background, rank, sums, seen, channel_weight, w_in, w_mid, w_out):
    anywhere = pl.BlockSpec(memory_space=pl.ANY)
    grad, send = pl.pallas_call(
        network_kernel,
        in_specs=[
            pl.BlockSpec(memory_space=pltpu.SMEM),
            VMEM_SPEC,
            anywhere,
            VMEM_SPEC,
            anywhere,
            anywhere,
            VMEM_SPEC,
            anywhere,
            VMEM_SPEC,
            anywhere,
        ],
        out_specs=[anywhere, VMEM_SPEC],
        out_shape=[
            pltpu.HBM((CELLS, LEV), f32),
            pltpu.VMEM((NLON, JL), bf16),
        ],
        scratch_shapes=[
            pltpu.VMEM((CELLS, 2 * LEV), bf16),
            pltpu.VMEM((GROUPS, GROUP, GROUP), bf16),
            pltpu.VMEM((MAX_ROWS + GROUP, 2 * LEV), f32),
            pltpu.VMEM((MAX_ROWS + GROUP, LEV), f32),
            pltpu.VMEM((2 * LEV, w_in.shape[1]), bf16),
            pltpu.VMEM(w_out.shape, bf16),
            pltpu.VMEM((CELLS, LEV), bf16),
            pltpu.VMEM((CELLS, LEV), f32),
            pltpu.VMEM((2, TILE, CHAN), f32),
            pltpu.VMEM((2, TILE, CHAN), f32),
            pltpu.SemaphoreType.DMA((2, 2)),
            pltpu.SemaphoreType.DMA((3, 3)),
        ],
        compiler_params=params(30),
        name="network",
    )(
        in_hbm(first),
        inc,
        in_hbm(background),
        in_hbm(rank),
        in_hbm(sums),
        in_hbm(seen),
        channel_weight,
        in_hbm(w_in),
        on_chip(w_mid),
        in_hbm(w_out),
    )
    return grad.reshape(CLAT, CLON, LEV), send


def exchange(rows, axis):
    return on_chip(lax.all_to_all(rows, axis, split_axis=0, concat_axis=0, tiled=True))


def per_device(
    spectral,
    background,
    columns,
    counts,
    radiances,
    used_pairs,
    channel_weight,
    weight_in,
    weight_mid,
    weight_out,
):
    table = on_chip(wave_table())
    lat_index = lax.axis_index("lat").astype(jnp.int32).reshape(1)
    legendre, fourier = legendre_transform(lat_index, spectral)
    sums, row, rank, first = row_sums(counts, columns, used_pairs, radiances[0], legendre)
    waves, token = waves_to_grid(exchange(fourier, "lat"), table, first)
    seen = row_seen(first, used_pairs, row, token)
    increment = exchange(waves, "lev")
    grid_grad, send = network(
        first,
        increment,
        background.reshape(CELLS, LEV),
        rank,
        sums,
        seen,
        channel_weight.reshape(1, CHAN),
        weight_in,
        weight_mid,
        weight_out,
    )
    coeff = exchange(grid_to_waves(exchange(send, "lev"), table), "lat")
    return (legendre_adjoint(legendre, coeff), grid_grad)


def solution(mesh):
    in_specs = (
        P(None, "lev", "lat", None),
        P("lat", "lev", None),
        P(("lat", "lev"), None),
        P(("lat", "lev")),
        P(("lat", "lev"), None, None),
        P(("lat", "lev"), None),
        P(),
        P(),
        P(),
        P(),
    )
    out_specs = (P(None, "lev", "lat", None), P("lat", "lev", None))
    return jax.shard_map(
        per_device, mesh=mesh, in_specs=in_specs, out_specs=out_specs, check_vma=False
    )
```

```python
import functools
import math

import jax
import jax.numpy as jnp
import numpy as np
from jax import lax
from jax.experimental import pallas as pl
from jax.experimental.pallas import tpu as pltpu
from jax.sharding import PartitionSpec as P

LEV = 128
M = 256
N = 256
NLAT = 384
NLON = 768
HALF = NLAT // 2
LANES = 128
N_LAT = 8
N_LEV = 16
ML = M // N_LAT
LL = LEV // N_LEV
CLAT = NLAT // N_LAT
CLON = NLON // N_LEV
CELLS = CLAT * CLON
CAP = 2048
CHAN = 512
JL = CLAT * LL
KM = 2 * M
M_PITCH = ML + 8
L_PITCH = 2 * ML + 8
ROWS = 2 * LL * ML

RESCALE_TOP = 2.0**30
RESCALE_BY = 2.0 ** (-60)
RESCALE_LOG = 60.0 * math.log(2.0)
HALF_LOG = 0.5 * math.log(0.5)

bf16 = jnp.bfloat16
f32 = jnp.float32


def params(mib):
    return pltpu.CompilerParams(vmem_limit_bytes=mib << 20)


def on_chip(array):
    return pltpu.with_memory_space_constraint(array, pltpu.VMEM)


def in_hbm(array):
    return pltpu.with_memory_space_constraint(array, pltpu.HBM)


VMEM_SPEC = pl.BlockSpec(memory_space=pltpu.VMEM)


def dot_nt(a, b):
    return lax.dot_general(a, b, (((1,), (1,)), ((), ())), preferred_element_type=f32)


def dot_tn(a, b):
    return lax.dot_general(a, b, (((0,), (0,)), ((), ())), preferred_element_type=f32)


def dot_nn(a, b):
    return jnp.dot(a, b, preferred_element_type=f32)


def wave_table():
    m = np.arange(M)
    phase = (np.arange(NLON)[:, None] * m[None, :] % NLON) * (2.0 * np.pi / NLON)
    weight = np.where(m == 0, 1.0, 2.0) / M
    pair = np.stack([weight * np.cos(phase), -weight * np.sin(phase)])
    table = pair.reshape(2, NLON, N_LAT, ML).transpose(1, 2, 0, 3).reshape(NLON, KM)
    return jnp.asarray(table, f32).astype(bf16)


M_STEP = 8
ADJOINT_STEP = 32


def legendre_kernel(
    spec_hbm, p_hbm, four_ref, spec_ref, table, waves, halves, p_buf, sems, spec_sem
):
    groups = range(ML // 8)

    fetch = pltpu.make_async_copy(spec_hbm, spec_ref, spec_sem)
    fetch.start()
    m0 = lax.axis_index("lat").astype(jnp.int32) * ML
    sub = lax.broadcasted_iota(jnp.int32, (8, LANES), 0)
    mf = [(sub + (m0 + 8 * g)).astype(f32) for g in groups]
    m2 = [v * v for v in mf]
    zero = jnp.zeros((8, LANES), f32)
    lanes = [lax.broadcasted_iota(jnp.int32, (8, LANES), 1) + h * LANES for h in (0, 1)]
    valid = [jnp.where(lanes[h] < HALF, 1.0, 0.0) for h in (0, 1)]
    colat = [
        (jnp.minimum(lanes[h], HALF - 1).astype(f32) + 0.5) * (math.pi / NLAT) for h in (0, 1)
    ]
    x = [jnp.cos(colat[h]) * valid[h] for h in (0, 1)]
    log_cos = [jnp.log(jnp.sin(colat[h])) for h in (0, 1)]
    k_ids = lax.broadcasted_iota(jnp.int32, (8, M), 1).astype(f32) + 1.0
    half_logs = 0.5 * jnp.log((2.0 * k_ids + 1.0) / (2.0 * k_ids))
    norm = [
        jnp.sum(jnp.where(k_ids <= mf[g][:, 0:1], half_logs, 0.0), axis=1, keepdims=True)
        for g in groups
    ]
    logs = [[HALF_LOG + norm[g] + mf[g] * log_cos[h] for h in (0, 1)] for g in groups]

    def block(i, carry):
        prev, earlier, logs, eps_prev, nf = carry
        big = [
            [jnp.maximum(jnp.abs(prev[g][h]), jnp.abs(earlier[g][h])) > RESCALE_TOP for h in (0, 1)]
            for g in groups
        ]
        shrink = [[jnp.where(big[g][h], RESCALE_BY, 1.0) for h in (0, 1)] for g in groups]
        prev = [[prev[g][h] * shrink[g][h] for h in (0, 1)] for g in groups]
        earlier = [[earlier[g][h] * shrink[g][h] for h in (0, 1)] for g in groups]
        logs = [
            [jnp.where(big[g][h], logs[g][h] + RESCALE_LOG, logs[g][h]) for h in (0, 1)]
            for g in groups
        ]
        scale = [[jnp.exp(logs[g][h]) * valid[h] for h in (0, 1)] for g in groups]
        for k in range(8):
            n2 = nf * nf
            inv = 1.0 / jnp.maximum(4.0 * n2 - 1.0, 1.0)
            at = pl.multiple_of((i * 8 + k) * M_PITCH, 8)
            new = []
            eps = []
            for g in groups:
                t = n2 - m2[g]
                q = jnp.maximum(t, 1.0) * inv
                a = lax.rsqrt(q)
                eps.append(jnp.where(t > 0.0, q * a, 0.0))
                diag = nf == mf[g]
                row = []
                for h in (0, 1):
                    cur = (x[h] * prev[g][h] - eps_prev[g] * earlier[g][h]) * a
                    cur = jnp.where(diag, 1.0, cur)
                    table[h, pl.ds(at + 8 * g, 8), :] = cur * scale[g][h]
                    row.append(cur)
                new.append(row)
            prev, earlier, eps_prev = new, prev, eps
            nf = nf + 1.0
        return prev, earlier, logs, eps_prev, nf

    empty = [[zero, zero] for _ in groups]
    lax.fori_loop(0, N // 8, block, (empty, empty, logs, [zero for _ in groups], zero))

    fetch.wait()
    for h in (0, 1):
        for k in range(2 * LL):
            halves[h, k * M_PITCH : k * M_PITCH + ML, :] = spec_ref[
                k * ML : (k + 1) * ML, h * LANES : (h + 1) * LANES
            ]
    lane = lax.broadcasted_iota(jnp.int32, (1, N), 1)
    alternate = jnp.where(lane % 2 == 0, 1.0, -1.0)
    def store(step):
        slot = lax.rem(step, 2)
        m = pl.ds(step * M_STEP, M_STEP)
        return pltpu.make_async_copy(p_buf.at[slot], p_hbm.at[m], sems.at[slot])

    def transform(step, _):
        slot = lax.rem(step, 2)

        @pl.when(step >= 2)
        def _():
            store(step - 2).wait()

        for k in range(M_STEP):
            m = step * M_STEP + k
            p_m = jnp.concatenate(
                [table[h, pl.ds(m, N, stride=M_PITCH), :].astype(bf16) for h in (0, 1)], axis=1
            )
            p_buf[slot, k] = p_m
            s = jnp.concatenate([halves[h, pl.ds(m, 2 * LL, stride=M_PITCH), :] for h in (0, 1)], axis=1)
            s = jnp.concatenate([s, s * (alternate if k % 2 == 0 else -alternate)], axis=0)
            high = s.astype(bf16)
            low = (s - high.astype(f32)).astype(bf16)
            out = dot_nn(jnp.concatenate([high, low], axis=0), p_m)
            out = out[: 4 * LL] + out[4 * LL :]
            for hemi in (0, 1):
                for c in (0, 1):
                    first = (hemi * 2 + c) * LL
                    for h in (0, 1):
                        waves[hemi, h, pl.ds(c * ML + m, LL, stride=L_PITCH), :] = out[
                            first : first + LL, h * LANES : (h + 1) * LANES
                        ]
        store(step).start()
        return 0

    steps = ML // M_STEP
    lax.fori_loop(0, steps, transform, 0)
    row = lax.broadcasted_iota(jnp.int32, (HALF, 256), 0)
    col = lax.broadcasted_iota(jnp.int32, (HALF, 256), 1)
    for hemi in (0, 1):
        pick = jnp.where(col == (row if hemi == 0 else HALF - 1 - row), 1.0, 0.0).astype(bf16)
        values = jnp.concatenate(
            [
                jnp.concatenate(
                    [
                        waves[hemi, h, l * L_PITCH : l * L_PITCH + 2 * ML, :].astype(bf16)
                        for h in (0, 1)
                    ],
                    axis=1,
                )
                for l in range(LL)
            ],
            axis=0,
        )
        four_ref[hemi * HALF : (hemi + 1) * HALF, :] = dot_nt(pick, values).astype(bf16)
    store(steps - 2).wait()
    store(steps - 1).wait()


def legendre_transform(spectral):
    return pl.pallas_call(
        legendre_kernel,
        in_specs=[pl.BlockSpec(memory_space=pl.ANY)],
        out_specs=[pl.BlockSpec(memory_space=pl.ANY), VMEM_SPEC],
        scratch_shapes=[
            pltpu.VMEM((ROWS, N), f32),
            pltpu.VMEM((2, N * M_PITCH, LANES), f32),
            pltpu.VMEM((2, 2, LL * L_PITCH, LANES), f32),
            pltpu.VMEM((2, 2 * LL * M_PITCH, LANES), f32),
            pltpu.VMEM((2, M_STEP, N, 256), bf16),
            pltpu.SemaphoreType.DMA((2,)),
            pltpu.SemaphoreType.DMA,
        ],
        out_shape=[
            pltpu.HBM((ML, N, 256), bf16),
            pltpu.VMEM((NLAT, ROWS), bf16),
        ],
        compiler_params=params(24),
        name="legendre",
    )(in_hbm(spectral.reshape(ROWS, N)))


def adjoint_kernel(p_ref, rows_ref, out_ref, folded, held):
    step = pl.program_id(0)

    @pl.when(step == 0)
    def _():
        j = lax.broadcasted_iota(jnp.int32, (NLAT, 256), 0)
        col = lax.broadcasted_iota(jnp.int32, (NLAT, 256), 1)
        north = jnp.where(col == j, 1.0, 0.0)
        south = jnp.where((j >= HALF) & (col == NLAT - 1 - j), 1.0, 0.0)
        north = jnp.where(col < HALF, north, 0.0)
        for part, pick in ((0, north + south), (1, north - south)):
            value = dot_tn(rows_ref[...], pick.astype(bf16))
            for h in (0, 1):
                for l in range(LL):
                    folded[part, h, l * L_PITCH : l * L_PITCH + 2 * ML, :] = value[
                        l * 2 * ML : (l + 1) * 2 * ML, h * LANES : (h + 1) * LANES
                    ]

    lane = lax.broadcasted_iota(jnp.int32, (2 * LL, N), 1)
    for k in range(ADJOINT_STEP):
        m = step * ADJOINT_STEP + k
        pieces = []
        for part in (0, 1):
            for c in (0, 1):
                pieces.append(
                    jnp.concatenate(
                        [
                            folded[part, h, pl.ds(c * ML + m, LL, stride=L_PITCH), :]
                            for h in (0, 1)
                        ],
                        axis=1,
                    )
                )
        value = dot_nt(jnp.concatenate(pieces, axis=0).astype(bf16), p_ref[m])
        picked = jnp.where(lane % 2 == k % 2, value[: 2 * LL], value[2 * LL :])
        for h in (0, 1):
            held[h, pl.ds(m, 2 * LL, stride=M_PITCH), :] = picked[:, h * LANES : (h + 1) * LANES]

    @pl.when(step == pl.num_programs(0) - 1)
    def _():
        for h in (0, 1):
            for k in range(2 * LL):
                out_ref[k * ML : (k + 1) * ML, h * LANES : (h + 1) * LANES] = held[
                    h, k * M_PITCH : k * M_PITCH + ML, :
                ]


def legendre_adjoint(table, rows):
    whole = lambda shape: pl.BlockSpec(shape, lambda i: (0,) * len(shape))
    out = pl.pallas_call(
        adjoint_kernel,
        grid=(ML // ADJOINT_STEP,),
        in_specs=[
            VMEM_SPEC,
            VMEM_SPEC,
        ],
        out_specs=whole((ROWS, N)),
        scratch_shapes=[
            pltpu.VMEM((2, 2, LL * L_PITCH, LANES), f32),
            pltpu.VMEM((2, 2 * LL * M_PITCH, LANES), f32),
        ],
        out_shape=jax.ShapeDtypeStruct((ROWS, N), f32),
        compiler_params=params(12),
        name="legendre_adjoint",
    )(on_chip(table), rows)
    return out.reshape(2, LL, ML, N)


def waves_kernel(rows_ref, table_ref, after_ref, out_ref, token_ref, held):
    del after_ref
    token_ref[...] = jnp.zeros_like(token_ref)
    for pair in range(N_LAT // 2):
        for l in range(LL):
            pieces = [
                rows_ref[(2 * pair + k) * CLAT : (2 * pair + k + 1) * CLAT, l * 64 : (l + 1) * 64]
                for k in (0, 1)
            ]
            held[pair, pl.ds(l, CLAT, stride=LL), :] = jnp.concatenate(pieces, axis=1).astype(f32)
    waves = jnp.concatenate([held[k].astype(bf16) for k in range(N_LAT // 2)], axis=1)
    out_ref[...] = dot_nt(table_ref[...], waves).astype(bf16)


def waves_to_grid(rows, table, after):
    return pl.pallas_call(
        waves_kernel,
        in_specs=[VMEM_SPEC, VMEM_SPEC, pl.BlockSpec(memory_space=pl.ANY)],
        out_shape=[pltpu.VMEM((NLON, JL), bf16), pltpu.HBM((8, LANES), f32)],
        out_specs=[VMEM_SPEC, VMEM_SPEC],
        scratch_shapes=[pltpu.VMEM((N_LAT // 2, JL, LANES), f32)],
        compiler_params=params(12),
        name="waves",
    )(rows, table, in_hbm(after))


def waves_adjoint_kernel(grid_ref, table_ref, out_ref, held):
    value = dot_tn(grid_ref[...], table_ref[...])
    for k in range(N_LAT // 2):
        held[k] = value[:, k * LANES : (k + 1) * LANES]
    for pair in range(N_LAT // 2):
        for lp in range(LL // 2):
            two = [held[pair, pl.ds(2 * lp + k, CLAT, stride=LL), :] for k in (0, 1)]
            for k in (0, 1):
                piece = jnp.concatenate([v[:, k * 64 : (k + 1) * 64] for v in two], axis=1)
                first = (2 * pair + k) * CLAT
                out_ref[first : first + CLAT, lp * LANES : (lp + 1) * LANES] = piece.astype(bf16)


def grid_to_waves(grid, table):
    return pl.pallas_call(
        waves_adjoint_kernel,
        in_specs=[VMEM_SPEC, VMEM_SPEC],
        out_shape=pltpu.VMEM((NLAT, ROWS), bf16),
        out_specs=VMEM_SPEC,
        scratch_shapes=[pltpu.VMEM((N_LAT // 2, JL, LANES), f32)],
        compiler_params=params(12),
        name="waves_adjoint",
    )(grid, table)


GROUP = 256
GROUPS = CELLS // GROUP
TILE = 240
SUM_TILE = 2 * TILE
QUARTER = CAP // 4
ROW_TILES = -(-(CAP + 7 * GROUPS) // SUM_TILE)
MAX_ROWS = ROW_TILES * SUM_TILE


def assign_rows(count, columns):
    slot = lax.broadcasted_iota(jnp.int32, (1, CAP), 1)
    valid = slot < count
    group = jnp.where(valid, lax.shift_right_logical(columns, 8), -1)
    inner = lax.broadcasted_iota(jnp.int32, (GROUP, CAP), 0) == (columns & (GROUP - 1))
    inner = jnp.where(inner, 1.0, 0.0).astype(bf16)
    in_group = lax.broadcasted_iota(jnp.int32, (16, CAP), 0) == group
    seen = dot_nt(jnp.where(in_group, 1.0, 0.0).astype(bf16), inner)
    used = jnp.where(seen > 0.5, 1.0, 0.0)
    before = lax.broadcasted_iota(jnp.int32, (GROUP, GROUP), 0) < lax.broadcasted_iota(
        jnp.int32, (GROUP, GROUP), 1
    )
    rank = dot_nn(used.astype(bf16), jnp.where(before, 1.0, 0.0).astype(bf16))
    padded = jnp.floor((jnp.sum(used, axis=1, keepdims=True) + 7.0) * 0.125) * 8.0
    padded = jnp.broadcast_to(padded, (16, LANES))
    sub = lax.broadcasted_iota(jnp.int32, (16, LANES), 0)
    first = jnp.zeros((16, LANES), f32)
    for g in range(GROUPS):
        first = first + jnp.where(sub > g, padded[g : g + 1, :], 0.0)
    of_slot = dot_nn(rank.astype(bf16), inner) + first[:, 0:1]
    row = jnp.sum(jnp.where(in_group, of_slot, 0.0), axis=0, keepdims=True)
    row = jnp.where(valid, row, -1.0).astype(jnp.int32)
    return row, jnp.where(used > 0.5, rank, -1.0), first


def write_sums(total, row_of_slot, masked, tile_buf, out_hbm, sems):
    tiles = (total + (SUM_TILE - 1)) // SUM_TILE

    def store(t):
        slot = lax.rem(t, 2)
        r = pl.ds(pl.multiple_of(t * SUM_TILE, 8), SUM_TILE)
        return pltpu.make_async_copy(tile_buf.at[slot], out_hbm.at[r, :], sems.at[slot])

    def one_tile(t, _):
        @pl.when(t >= 2)
        def _():
            store(t - 2).wait()

        row = lax.broadcasted_iota(jnp.int32, (SUM_TILE, CAP), 0) + t * SUM_TILE
        hit = jnp.where(row == row_of_slot[...], 1.0, 0.0).astype(bf16)
        tile_buf[lax.rem(t, 2)] = dot_nn(hit, masked[...])
        store(t).start()
        return 0

    lax.fori_loop(0, tiles, one_tile, 0)

    @pl.when(tiles >= 2)
    def _():
        store(tiles - 2).wait()

    store(tiles - 1).wait()


def active_channels(part, pairs_ref, value, masked):
    channel = lax.broadcasted_iota(jnp.int32, (LANES, LANES), 1)
    for i in range(part * QUARTER // LANES, (part + 1) * QUARTER // LANES):
        r = slice(i * LANES, (i + 1) * LANES)
        used = jnp.transpose(jnp.broadcast_to(2 * pairs_ref[:, r], (LANES, LANES)))
        for c in range(CHAN // LANES):
            lanes = slice(c * LANES, (c + 1) * LANES)
            masked[r, lanes] = jnp.where(
                channel + c * LANES < used, value(r, lanes), 0.0
            ).astype(bf16)


def sums_kernel(
    count_ref,
    columns_ref,
    pairs_ref,
    obs_hbm,
    after_ref,
    sum_hbm,
    row_ref,
    rank_ref,
    first_ref,
    obs,
    masked,
    tile_buf,
    sems,
    obs_sems,
):
    del after_ref

    def fetch(part):
        r = pl.ds(part * QUARTER, QUARTER)
        return pltpu.make_async_copy(obs_hbm.at[r, :], obs.at[r, :], obs_sems.at[part])

    for part in range(4):
        fetch(part).start()
    row, rank, first = assign_rows(count_ref[0], columns_ref[...])
    row_ref[...] = row
    rank_ref[...] = rank
    first_ref[...] = first.astype(jnp.int32)
    for part in range(4):
        fetch(part).wait()
        active_channels(part, pairs_ref, lambda r, lanes: obs[r, lanes].astype(f32), masked)
    write_sums(jnp.max(first).astype(jnp.int32), row_ref, masked, tile_buf, sum_hbm, sems)


def seen_kernel(first_ref, pairs_ref, row_ref, after_ref, sum_hbm, masked, tile_buf, sems):
    del after_ref
    for part in range(4):
        active_channels(part, pairs_ref, lambda r, lanes: 1.0, masked)
    write_sums(first_ref[GROUPS, 0], row_ref, masked, tile_buf, sum_hbm, sems)


ROW_COST = pl.CostEstimate(
    flops=2 * MAX_ROWS * CAP * CHAN, transcendentals=0, bytes_accessed=MAX_ROWS * CHAN * 4
)


SUM_SCRATCH = [
    pltpu.VMEM((CAP, CHAN), bf16),
    pltpu.VMEM((2, SUM_TILE, CHAN), f32),
    pltpu.SemaphoreType.DMA((2,)),
]


def row_sums(counts, columns, pairs, obs, after):
    anywhere = pl.BlockSpec(memory_space=pl.ANY)
    return pl.pallas_call(
        sums_kernel,
        in_specs=[
            pl.BlockSpec(memory_space=pltpu.SMEM),
            VMEM_SPEC,
            VMEM_SPEC,
            anywhere,
            anywhere,
        ],
        out_specs=[anywhere, VMEM_SPEC, VMEM_SPEC, VMEM_SPEC],
        scratch_shapes=[pltpu.VMEM((CAP, CHAN), bf16)]
        + SUM_SCRATCH
        + [pltpu.SemaphoreType.DMA((4,))],
        out_shape=[
            pltpu.HBM((MAX_ROWS, CHAN), f32),
            pltpu.HBM((1, CAP), jnp.int32),
            pltpu.HBM((16, GROUP), f32),
            pltpu.HBM((16, LANES), jnp.int32),
        ],
        compiler_params=params(24),
        cost_estimate=ROW_COST,
        name="row_sums",
    )(counts, in_hbm(columns), in_hbm(pairs), in_hbm(obs), in_hbm(after))


def row_seen(first, pairs, row, after):
    anywhere = pl.BlockSpec(memory_space=pl.ANY)
    return pl.pallas_call(
        seen_kernel,
        in_specs=[pl.BlockSpec(memory_space=pltpu.SMEM), VMEM_SPEC, VMEM_SPEC, anywhere],
        out_specs=anywhere,
        scratch_shapes=SUM_SCRATCH,
        out_shape=pltpu.HBM((MAX_ROWS, CHAN), f32),
        compiler_params=params(24),
        cost_estimate=ROW_COST,
        name="row_seen",
    )(in_hbm(first), in_hbm(pairs), in_hbm(row), in_hbm(after))


J_STEP = 16
X_ROWS = 16
PART = J_STEP * CLON


def silu_and_slope(v):
    half = 0.5 * v
    sig = 0.5 * jnp.tanh(half) + 0.5
    act = v * sig
    return act, sig + act - act * sig


def swap_blocks(v):
    lane = lax.broadcasted_iota(jnp.int32, v[0].shape, 1)
    v = list(v)
    for bit in range(4):
        gap = 1 << bit
        upper = (lane & (8 * gap)) != 0
        for s in range(N_LEV):
            if s & gap:
                continue
            a, b = v[s], v[s + gap]
            v[s] = jnp.where(upper, pltpu.roll(b, 8 * gap, 1), a)
            v[s + gap] = jnp.where(upper, b, pltpu.roll(a, LANES - 8 * gap, 1))
    return v


def network_kernel(
    first_hbm,
    inc_ref,
    back_hbm,
    rank_hbm,
    sum_hbm,
    seen_hbm,
    chan_ref,
    w_in_hbm,
    w_mid,
    w_out_hbm,
    grad_hbm,
    send_ref,
    first_ref,
    rank_ref,
    state,
    picks,
    packed,
    packed_grad,
    w_twice,
    w_last,
    back_buf,
    grads,
    sum_buf,
    seen_buf,
    sems,
    part_sems,
):
    def fetches(t, slot):
        r = pl.ds(pl.multiple_of(t * TILE, 8), TILE)
        return (
            pltpu.make_async_copy(sum_hbm.at[r, :], sum_buf.at[slot], sems.at[0, slot]),
            pltpu.make_async_copy(seen_hbm.at[r, :], seen_buf.at[slot], sems.at[1, slot]),
        )

    def part_copy(k, src, dst, jc):
        r = pl.ds(pl.multiple_of(jc * PART, PART), PART)
        return pltpu.make_async_copy(src.at[r, :], dst.at[r, :], part_sems.at[k, jc])

    ranks = [
        pltpu.make_async_copy(rank_hbm, rank_ref, part_sems.at[3, 0]),
        pltpu.make_async_copy(first_hbm, first_ref, part_sems.at[3, 1]),
    ]
    for fetch in ranks:
        fetch.start()
    for jc in range(CLAT // J_STEP):
        part_copy(0, back_hbm, back_buf, jc).start()
    weights = [
        pltpu.make_async_copy(w_in_hbm, w_twice.at[pl.ds(0, LEV), :], part_sems.at[2, 0]),
        pltpu.make_async_copy(w_in_hbm, w_twice.at[pl.ds(LEV, LEV), :], part_sems.at[2, 1]),
        pltpu.make_async_copy(w_out_hbm, w_last, part_sems.at[2, 2]),
    ]
    for fetch in weights:
        fetch.start()
    for fetch in fetches(0, 0):
        fetch.start()

    def to_state(jc, _):
        part_copy(0, back_hbm, back_buf, jc).wait()
        lanes = pl.ds(pl.multiple_of(jc * LANES, LANES), LANES)
        for part in range(CLON // X_ROWS):
            x0 = part * X_ROWS
            v = [
                inc_ref[s * CLON + x0 : s * CLON + x0 + X_ROWS, lanes].astype(f32)
                for s in range(N_LEV)
            ]
            v = swap_blocks(v)
            for j in range(J_STEP):
                r = pl.ds(pl.multiple_of((jc * J_STEP + j) * CLON + x0, 16), X_ROWS)
                grid_state = back_buf[r, :].astype(f32) + v[j]
                high = grid_state.astype(bf16)
                state[r, :LEV] = high
                state[r, LEV:] = (grid_state - high.astype(f32)).astype(bf16)
        return 0

    lax.fori_loop(0, CLAT // J_STEP, to_state, 0)
    for fetch in ranks:
        fetch.wait()
    total = first_ref[GROUPS, 0]
    tiles = (total + (TILE - 1)) // TILE
    row = lax.broadcasted_iota(jnp.int32, (GROUP, GROUP), 0).astype(f32)
    for g in range(GROUPS):
        picks[g] = jnp.where(row == rank_ref[g : g + 1, :], 1.0, 0.0).astype(bf16)


    def group_rows(g):
        first = pl.ds(pl.multiple_of(first_ref[g, 0], 8), GROUP)
        return first, slice(g * GROUP, (g + 1) * GROUP), picks[g]

    for g in range(GROUPS):
        rows, cells, pick = group_rows(g)
        packed[rows, :] = dot_nn(pick, state[cells, :])
    packed[pl.ds(pl.multiple_of(total, 8), TILE), :] = jnp.zeros((TILE, 2 * LEV), f32)

    for fetch in weights:
        fetch.wait()

    def one_tile(t, _):
        slot = lax.rem(t, 2)
        for fetch in fetches(t, slot):
            fetch.wait()

        @pl.when(t + 1 < tiles)
        def _():
            for fetch in fetches(t + 1, 1 - slot):
                fetch.start()

        r = pl.ds(pl.multiple_of(t * TILE, 8), TILE)
        act1, slope1 = silu_and_slope(dot_nn(packed[r, :].astype(bf16), w_twice[...]))
        act2, slope2 = silu_and_slope(dot_nn(act1.astype(bf16), w_mid[...]))
        evolved = dot_nn(act2.astype(bf16), w_last[...])
        misfit = (chan_ref[...] * (seen_buf[slot] * evolved - sum_buf[slot])).astype(bf16)
        back2 = (dot_nt(misfit, w_last[...]) * slope2).astype(bf16)
        back1 = (dot_nt(back2, w_mid[...]) * slope1).astype(bf16)
        packed_grad[r, :] = dot_nt(back1, w_twice[:LEV])
        return 0

    lax.fori_loop(0, tiles, one_tile, 0)
    packed_grad[pl.ds(pl.multiple_of(tiles * TILE, 8), GROUP), :] = jnp.zeros((GROUP, LEV), f32)
    for g in range(GROUPS):
        rows, cells, pick = group_rows(g)
        value = packed_grad[rows, :]
        high = value.astype(bf16)
        low = (value - high.astype(f32)).astype(bf16)
        value = dot_tn(pick, jnp.concatenate([high, low], axis=1))
        grads[cells, :] = value[:, :LEV] + value[:, LEV:]
        if (g + 1) * GROUP % PART == 0:
            part_copy(1, grads, grad_hbm, g * GROUP // PART).start()

    def to_send(jc, _):
        lanes = pl.ds(pl.multiple_of(jc * LANES, LANES), LANES)
        for part in range(CLON // X_ROWS):
            x0 = part * X_ROWS
            v = [
                grads[pl.ds(pl.multiple_of((jc * J_STEP + j) * CLON + x0, 16), X_ROWS), :]
                for j in range(J_STEP)
            ]
            v = swap_blocks(v)
            for s in range(N_LEV):
                send_ref[s * CLON + x0 : s * CLON + x0 + X_ROWS, lanes] = v[s].astype(bf16)
        return 0

    lax.fori_loop(0, CLAT // J_STEP, to_send, 0)
    for jc in range(CLAT // J_STEP):
        part_copy(1, grads, grad_hbm, jc).wait()


def network(first, inc, background, rank, sums, seen, channel_weight, w_in, w_mid, w_out):
    anywhere = pl.BlockSpec(memory_space=pl.ANY)
    grad, send = pl.pallas_call(
        network_kernel,
        in_specs=[
            anywhere,
            VMEM_SPEC,
            anywhere,
            anywhere,
            anywhere,
            anywhere,
            VMEM_SPEC,
            anywhere,
            VMEM_SPEC,
            anywhere,
        ],
        out_specs=[anywhere, VMEM_SPEC],
        out_shape=[
            pltpu.HBM((CELLS, LEV), f32),
            pltpu.VMEM((NLON, JL), bf16),
        ],
        scratch_shapes=[
            pltpu.SMEM((16, LANES), jnp.int32),
            pltpu.VMEM((16, GROUP), f32),
            pltpu.VMEM((CELLS, 2 * LEV), bf16),
            pltpu.VMEM((GROUPS, GROUP, GROUP), bf16),
            pltpu.VMEM((MAX_ROWS + GROUP, 2 * LEV), f32),
            pltpu.VMEM((MAX_ROWS + GROUP, LEV), f32),
            pltpu.VMEM((2 * LEV, w_in.shape[1]), bf16),
            pltpu.VMEM(w_out.shape, bf16),
            pltpu.VMEM((CELLS, LEV), bf16),
            pltpu.VMEM((CELLS, LEV), f32),
            pltpu.VMEM((2, TILE, CHAN), f32),
            pltpu.VMEM((2, TILE, CHAN), f32),
            pltpu.SemaphoreType.DMA((2, 2)),
            pltpu.SemaphoreType.DMA((4, 3)),
        ],
        compiler_params=params(30),
        name="network",
    )(
        in_hbm(first),
        inc,
        in_hbm(background),
        in_hbm(rank),
        in_hbm(sums),
        in_hbm(seen),
        channel_weight,
        in_hbm(w_in),
        on_chip(w_mid),
        in_hbm(w_out),
    )
    return grad.reshape(CLAT, CLON, LEV), send


def exchange(rows, axis):
    return on_chip(lax.all_to_all(rows, axis, split_axis=0, concat_axis=0, tiled=True))


def per_device(
    spectral,
    background,
    columns,
    counts,
    radiances,
    used_pairs,
    channel_weight,
    weight_in,
    weight_mid,
    weight_out,
):
    table = on_chip(wave_table())
    legendre, fourier = legendre_transform(spectral)
    sums, row, rank, first = row_sums(counts, columns, used_pairs, radiances[0], legendre)
    waves, token = waves_to_grid(exchange(fourier, "lat"), table, first)
    seen = row_seen(first, used_pairs, row, token)
    increment = exchange(waves, "lev")
    grid_grad, send = network(
        first,
        increment,
        background.reshape(CELLS, LEV),
        rank,
        sums,
        seen,
        channel_weight.reshape(1, CHAN),
        weight_in,
        weight_mid,
        weight_out,
    )
    coeff = exchange(grid_to_waves(exchange(send, "lev"), table), "lat")
    return (legendre_adjoint(legendre, coeff), grid_grad)


def solution(mesh):
    in_specs = (
        P(None, "lev", "lat", None),
        P("lat", "lev", None),
        P(("lat", "lev"), None),
        P(("lat", "lev")),
        P(("lat", "lev"), None, None),
        P(("lat", "lev"), None),
        P(),
        P(),
        P(),
        P(),
    )
    out_specs = (P(None, "lev", "lat", None), P("lat", "lev", None))
    return jax.shard_map(
        per_device, mesh=mesh, in_specs=in_specs, out_specs=out_specs, check_vma=False
    )
```

```python
import functools
import math

import jax
import jax.numpy as jnp
import numpy as np
from jax import lax
from jax.experimental import pallas as pl
from jax.experimental.pallas import tpu as pltpu
from jax.sharding import PartitionSpec as P

LEV = 128
M = 256
N = 256
NLAT = 384
NLON = 768
HALF = NLAT // 2
LANES = 128
N_LAT = 8
N_LEV = 16
ML = M // N_LAT
LL = LEV // N_LEV
CLAT = NLAT // N_LAT
CLON = NLON // N_LEV
CELLS = CLAT * CLON
CAP = 2048
CHAN = 512
JL = CLAT * LL
KM = 2 * M
M_PITCH = ML + 8
L_PITCH = 2 * ML + 8
ROWS = 2 * LL * ML

RESCALE_TOP = 2.0**30
RESCALE_BY = 2.0 ** (-60)
RESCALE_LOG = 60.0 * math.log(2.0)
HALF_LOG = 0.5 * math.log(0.5)

bf16 = jnp.bfloat16
f32 = jnp.float32


def params(mib):
    return pltpu.CompilerParams(vmem_limit_bytes=mib << 20)


def on_chip(array):
    return pltpu.with_memory_space_constraint(array, pltpu.VMEM)


def in_hbm(array):
    return pltpu.with_memory_space_constraint(array, pltpu.HBM)


VMEM_SPEC = pl.BlockSpec(memory_space=pltpu.VMEM)


def dot_nt(a, b):
    return lax.dot_general(a, b, (((1,), (1,)), ((), ())), preferred_element_type=f32)


def dot_tn(a, b):
    return lax.dot_general(a, b, (((0,), (0,)), ((), ())), preferred_element_type=f32)


def dot_nn(a, b):
    return jnp.dot(a, b, preferred_element_type=f32)


def wave_table():
    m = np.arange(M)
    phase = (np.arange(NLON)[:, None] * m[None, :] % NLON) * (2.0 * np.pi / NLON)
    weight = np.where(m == 0, 1.0, 2.0) / M
    pair = np.stack([weight * np.cos(phase), -weight * np.sin(phase)])
    table = pair.reshape(2, NLON, N_LAT, ML).transpose(1, 2, 0, 3).reshape(NLON, KM)
    return jnp.asarray(table, f32).astype(bf16)


M_STEP = 8
ADJOINT_STEP = 32


def legendre_kernel(
    spec_hbm, p_hbm, four_ref, spec_ref, table, waves, halves, p_buf, sems, spec_sem
):
    groups = range(ML // 8)

    fetch = pltpu.make_async_copy(spec_hbm, spec_ref, spec_sem)
    fetch.start()
    m0 = lax.axis_index("lat").astype(jnp.int32) * ML
    sub = lax.broadcasted_iota(jnp.int32, (8, LANES), 0)
    mf = [(sub + (m0 + 8 * g)).astype(f32) for g in groups]
    m2 = [v * v for v in mf]
    zero = jnp.zeros((8, LANES), f32)
    lanes = [lax.broadcasted_iota(jnp.int32, (8, LANES), 1) + h * LANES for h in (0, 1)]
    valid = [jnp.where(lanes[h] < HALF, 1.0, 0.0) for h in (0, 1)]
    colat = [
        (jnp.minimum(lanes[h], HALF - 1).astype(f32) + 0.5) * (math.pi / NLAT) for h in (0, 1)
    ]
    x = [jnp.cos(colat[h]) * valid[h] for h in (0, 1)]
    log_cos = [jnp.log(jnp.sin(colat[h])) for h in (0, 1)]
    k_ids = lax.broadcasted_iota(jnp.int32, (8, M), 1).astype(f32) + 1.0
    half_logs = 0.5 * jnp.log((2.0 * k_ids + 1.0) / (2.0 * k_ids))
    norm = [
        jnp.sum(jnp.where(k_ids <= mf[g][:, 0:1], half_logs, 0.0), axis=1, keepdims=True)
        for g in groups
    ]
    logs = [[HALF_LOG + norm[g] + mf[g] * log_cos[h] for h in (0, 1)] for g in groups]

    def block(i, carry):
        prev, earlier, logs, eps_prev, nf = carry
        big = [
            [jnp.maximum(jnp.abs(prev[g][h]), jnp.abs(earlier[g][h])) > RESCALE_TOP for h in (0, 1)]
            for g in groups
        ]
        shrink = [[jnp.where(big[g][h], RESCALE_BY, 1.0) for h in (0, 1)] for g in groups]
        prev = [[prev[g][h] * shrink[g][h] for h in (0, 1)] for g in groups]
        earlier = [[earlier[g][h] * shrink[g][h] for h in (0, 1)] for g in groups]
        logs = [
            [jnp.where(big[g][h], logs[g][h] + RESCALE_LOG, logs[g][h]) for h in (0, 1)]
            for g in groups
        ]
        scale = [[jnp.exp(logs[g][h]) * valid[h] for h in (0, 1)] for g in groups]
        for k in range(8):
            n2 = nf * nf
            inv = 1.0 / jnp.maximum(4.0 * n2 - 1.0, 1.0)
            at = pl.multiple_of((i * 8 + k) * M_PITCH, 8)
            new = []
            eps = []
            for g in groups:
                t = n2 - m2[g]
                q = jnp.maximum(t, 1.0) * inv
                a = lax.rsqrt(q)
                eps.append(jnp.where(t > 0.0, q * a, 0.0))
                diag = nf == mf[g]
                row = []
                for h in (0, 1):
                    cur = (x[h] * prev[g][h] - eps_prev[g] * earlier[g][h]) * a
                    cur = jnp.where(diag, 1.0, cur)
                    table[h, pl.ds(at + 8 * g, 8), :] = cur * scale[g][h]
                    row.append(cur)
                new.append(row)
            prev, earlier, eps_prev = new, prev, eps
            nf = nf + 1.0
        return prev, earlier, logs, eps_prev, nf

    empty = [[zero, zero] for _ in groups]
    lax.fori_loop(0, N // 8, block, (empty, empty, logs, [zero for _ in groups], zero))

    fetch.wait()
    for h in (0, 1):
        for k in range(2 * LL):
            halves[h, k * M_PITCH : k * M_PITCH + ML, :] = spec_ref[
                k * ML : (k + 1) * ML, h * LANES : (h + 1) * LANES
            ]
    lane = lax.broadcasted_iota(jnp.int32, (1, N), 1)
    alternate = jnp.where(lane % 2 == 0, 1.0, -1.0)
    def store(step):
        slot = lax.rem(step, 2)
        m = pl.ds(step * M_STEP, M_STEP)
        return pltpu.make_async_copy(p_buf.at[slot], p_hbm.at[m], sems.at[slot])

    def transform(step, _):
        slot = lax.rem(step, 2)

        @pl.when(step >= 2)
        def _():
            store(step - 2).wait()

        for k in range(M_STEP):
            m = step * M_STEP + k
            p_m = jnp.concatenate(
                [table[h, pl.ds(m, N, stride=M_PITCH), :].astype(bf16) for h in (0, 1)], axis=1
            )
            p_buf[slot, k] = p_m
            s = jnp.concatenate([halves[h, pl.ds(m, 2 * LL, stride=M_PITCH), :] for h in (0, 1)], axis=1)
            s = jnp.concatenate([s, s * (alternate if k % 2 == 0 else -alternate)], axis=0)
            high = s.astype(bf16)
            low = (s - high.astype(f32)).astype(bf16)
            out = dot_nn(jnp.concatenate([high, low], axis=0), p_m)
            out = out[: 4 * LL] + out[4 * LL :]
            for hemi in (0, 1):
                for c in (0, 1):
                    first = (hemi * 2 + c) * LL
                    for h in (0, 1):
                        waves[hemi, h, pl.ds(c * ML + m, LL, stride=L_PITCH), :] = out[
                            first : first + LL, h * LANES : (h + 1) * LANES
                        ]
        store(step).start()
        return 0

    steps = ML // M_STEP
    lax.fori_loop(0, steps, transform, 0)
    row = lax.broadcasted_iota(jnp.int32, (HALF, 256), 0)
    col = lax.broadcasted_iota(jnp.int32, (HALF, 256), 1)
    for hemi in (0, 1):
        pick = jnp.where(col == (row if hemi == 0 else HALF - 1 - row), 1.0, 0.0).astype(bf16)
        values = jnp.concatenate(
            [
                jnp.concatenate(
                    [
                        waves[hemi, h, l * L_PITCH : l * L_PITCH + 2 * ML, :].astype(bf16)
                        for h in (0, 1)
                    ],
                    axis=1,
                )
                for l in range(LL)
            ],
            axis=0,
        )
        four_ref[hemi * HALF : (hemi + 1) * HALF, :] = dot_nt(pick, values).astype(bf16)
    store(steps - 2).wait()
    store(steps - 1).wait()


def legendre_transform(spectral):
    return pl.pallas_call(
        legendre_kernel,
        in_specs=[pl.BlockSpec(memory_space=pl.ANY)],
        out_specs=[pl.BlockSpec(memory_space=pl.ANY), VMEM_SPEC],
        scratch_shapes=[
            pltpu.VMEM((ROWS, N), f32),
            pltpu.VMEM((2, N * M_PITCH, LANES), f32),
            pltpu.VMEM((2, 2, LL * L_PITCH, LANES), f32),
            pltpu.VMEM((2, 2 * LL * M_PITCH, LANES), f32),
            pltpu.VMEM((2, M_STEP, N, 256), bf16),
            pltpu.SemaphoreType.DMA((2,)),
            pltpu.SemaphoreType.DMA,
        ],
        out_shape=[
            pltpu.HBM((ML, N, 256), bf16),
            pltpu.VMEM((NLAT, ROWS), bf16),
        ],
        compiler_params=params(24),
        name="legendre",
    )(in_hbm(spectral.reshape(ROWS, N)))


def adjoint_kernel(p_ref, rows_ref, out_ref, folded, held):
    step = pl.program_id(0)

    @pl.when(step == 0)
    def _():
        j = lax.broadcasted_iota(jnp.int32, (NLAT, 256), 0)
        col = lax.broadcasted_iota(jnp.int32, (NLAT, 256), 1)
        north = jnp.where(col == j, 1.0, 0.0)
        south = jnp.where((j >= HALF) & (col == NLAT - 1 - j), 1.0, 0.0)
        north = jnp.where(col < HALF, north, 0.0)
        for part, pick in ((0, north + south), (1, north - south)):
            value = dot_tn(rows_ref[...], pick.astype(bf16))
            for h in (0, 1):
                for l in range(LL):
                    folded[part, h, l * L_PITCH : l * L_PITCH + 2 * ML, :] = value[
                        l * 2 * ML : (l + 1) * 2 * ML, h * LANES : (h + 1) * LANES
                    ]

    lane = lax.broadcasted_iota(jnp.int32, (2 * LL, N), 1)
    for k in range(ADJOINT_STEP):
        m = step * ADJOINT_STEP + k
        pieces = []
        for part in (0, 1):
            for c in (0, 1):
                pieces.append(
                    jnp.concatenate(
                        [
                            folded[part, h, pl.ds(c * ML + m, LL, stride=L_PITCH), :]
                            for h in (0, 1)
                        ],
                        axis=1,
                    )
                )
        value = dot_nt(jnp.concatenate(pieces, axis=0).astype(bf16), p_ref[m])
        picked = jnp.where(lane % 2 == k % 2, value[: 2 * LL], value[2 * LL :])
        for h in (0, 1):
            held[h, pl.ds(m, 2 * LL, stride=M_PITCH), :] = picked[:, h * LANES : (h + 1) * LANES]

    @pl.when(step == pl.num_programs(0) - 1)
    def _():
        for h in (0, 1):
            for k in range(2 * LL):
                out_ref[k * ML : (k + 1) * ML, h * LANES : (h + 1) * LANES] = held[
                    h, k * M_PITCH : k * M_PITCH + ML, :
                ]


def legendre_adjoint(table, rows):
    whole = lambda shape: pl.BlockSpec(shape, lambda i: (0,) * len(shape))
    out = pl.pallas_call(
        adjoint_kernel,
        grid=(ML // ADJOINT_STEP,),
        in_specs=[
            VMEM_SPEC,
            VMEM_SPEC,
        ],
        out_specs=whole((ROWS, N)),
        scratch_shapes=[
            pltpu.VMEM((2, 2, LL * L_PITCH, LANES), f32),
            pltpu.VMEM((2, 2 * LL * M_PITCH, LANES), f32),
        ],
        out_shape=jax.ShapeDtypeStruct((ROWS, N), f32),
        compiler_params=params(12),
        name="legendre_adjoint",
    )(on_chip(table), rows)
    return out.reshape(2, LL, ML, N)


def waves_kernel(rows_ref, table_ref, after_ref, out_ref, token_ref, held):
    del after_ref
    token_ref[...] = jnp.zeros_like(token_ref)
    for pair in range(N_LAT // 2):
        for l in range(LL):
            pieces = [
                rows_ref[(2 * pair + k) * CLAT : (2 * pair + k + 1) * CLAT, l * 64 : (l + 1) * 64]
                for k in (0, 1)
            ]
            held[pair, pl.ds(l, CLAT, stride=LL), :] = jnp.concatenate(pieces, axis=1).astype(f32)
    waves = jnp.concatenate([held[k].astype(bf16) for k in range(N_LAT // 2)], axis=1)
    out_ref[...] = dot_nt(table_ref[...], waves).astype(bf16)


def waves_to_grid(rows, table, after):
    return pl.pallas_call(
        waves_kernel,
        in_specs=[VMEM_SPEC, VMEM_SPEC, pl.BlockSpec(memory_space=pl.ANY)],
        out_shape=[pltpu.VMEM((NLON, JL), bf16), pltpu.HBM((8, LANES), f32)],
        out_specs=[VMEM_SPEC, VMEM_SPEC],
        scratch_shapes=[pltpu.VMEM((N_LAT // 2, JL, LANES), f32)],
        compiler_params=params(12),
        name="waves",
    )(rows, table, in_hbm(after))


def waves_adjoint_kernel(grid_ref, table_ref, out_ref, held):
    value = dot_tn(grid_ref[...], table_ref[...])
    for k in range(N_LAT // 2):
        held[k] = value[:, k * LANES : (k + 1) * LANES]
    for pair in range(N_LAT // 2):
        for lp in range(LL // 2):
            two = [held[pair, pl.ds(2 * lp + k, CLAT, stride=LL), :] for k in (0, 1)]
            for k in (0, 1):
                piece = jnp.concatenate([v[:, k * 64 : (k + 1) * 64] for v in two], axis=1)
                first = (2 * pair + k) * CLAT
                out_ref[first : first + CLAT, lp * LANES : (lp + 1) * LANES] = piece.astype(bf16)


def grid_to_waves(grid, table):
    return pl.pallas_call(
        waves_adjoint_kernel,
        in_specs=[VMEM_SPEC, VMEM_SPEC],
        out_shape=pltpu.VMEM((NLAT, ROWS), bf16),
        out_specs=VMEM_SPEC,
        scratch_shapes=[pltpu.VMEM((N_LAT // 2, JL, LANES), f32)],
        compiler_params=params(12),
        name="waves_adjoint",
    )(grid, table)


GROUP = 256
GROUPS = CELLS // GROUP
TILE = 240
SUM_TILE = 2 * TILE
QUARTER = CAP // 4
ROW_TILES = -(-(CAP + 7 * GROUPS) // SUM_TILE)
MAX_ROWS = ROW_TILES * SUM_TILE


def assign_rows(count, columns):
    slot = lax.broadcasted_iota(jnp.int32, (1, CAP), 1)
    valid = slot < count
    group = jnp.where(valid, lax.shift_right_logical(columns, 8), -1)
    inner = lax.broadcasted_iota(jnp.int32, (GROUP, CAP), 0) == (columns & (GROUP - 1))
    inner = jnp.where(inner, 1.0, 0.0).astype(bf16)
    in_group = lax.broadcasted_iota(jnp.int32, (16, CAP), 0) == group
    seen = dot_nt(jnp.where(in_group, 1.0, 0.0).astype(bf16), inner)
    used = jnp.where(seen > 0.5, 1.0, 0.0)
    before = lax.broadcasted_iota(jnp.int32, (GROUP, GROUP), 0) < lax.broadcasted_iota(
        jnp.int32, (GROUP, GROUP), 1
    )
    rank = dot_nn(used.astype(bf16), jnp.where(before, 1.0, 0.0).astype(bf16))
    padded = jnp.floor((jnp.sum(used, axis=1, keepdims=True) + 7.0) * 0.125) * 8.0
    padded = jnp.broadcast_to(padded, (16, LANES))
    sub = lax.broadcasted_iota(jnp.int32, (16, LANES), 0)
    first = jnp.zeros((16, LANES), f32)
    for g in range(GROUPS):
        first = first + jnp.where(sub > g, padded[g : g + 1, :], 0.0)
    of_slot = dot_nn(rank.astype(bf16), inner) + first[:, 0:1]
    row = jnp.sum(jnp.where(in_group, of_slot, 0.0), axis=0, keepdims=True)
    row = jnp.where(valid, row, -1.0).astype(jnp.int32)
    return row, jnp.where(used > 0.5, rank, -1.0), first


def write_sums(total, row_of_slot, masked, tile_buf, out_hbm, sems):
    tiles = (total + (SUM_TILE - 1)) // SUM_TILE

    def store(t):
        slot = lax.rem(t, 2)
        r = pl.ds(pl.multiple_of(t * SUM_TILE, 8), SUM_TILE)
        return pltpu.make_async_copy(tile_buf.at[slot], out_hbm.at[r, :], sems.at[slot])

    def one_tile(t, _):
        @pl.when(t >= 2)
        def _():
            store(t - 2).wait()

        row = lax.broadcasted_iota(jnp.int32, (SUM_TILE, CAP), 0) + t * SUM_TILE
        hit = jnp.where(row == row_of_slot[...], 1.0, 0.0).astype(bf16)
        tile_buf[lax.rem(t, 2)] = dot_nn(hit, masked[...])
        store(t).start()
        return 0

    lax.fori_loop(0, tiles, one_tile, 0)

    @pl.when(tiles >= 2)
    def _():
        store(tiles - 2).wait()

    store(tiles - 1).wait()


def active_channels(part, pairs_ref, value, masked):
    channel = lax.broadcasted_iota(jnp.int32, (LANES, LANES), 1)
    for i in range(part * QUARTER // LANES, (part + 1) * QUARTER // LANES):
        r = slice(i * LANES, (i + 1) * LANES)
        used = jnp.transpose(jnp.broadcast_to(2 * pairs_ref[:, r], (LANES, LANES)))
        for c in range(CHAN // LANES):
            lanes = slice(c * LANES, (c + 1) * LANES)
            masked[r, lanes] = jnp.where(
                channel + c * LANES < used, value(r, lanes), 0.0
            ).astype(bf16)


def sums_kernel(
    count_ref,
    columns_ref,
    pairs_ref,
    obs_hbm,
    after_ref,
    sum_hbm,
    row_ref,
    rank_ref,
    first_ref,
    obs,
    masked,
    tile_buf,
    sems,
    obs_sems,
):
    del after_ref

    def fetch(part):
        r = pl.ds(part * QUARTER, QUARTER)
        return pltpu.make_async_copy(obs_hbm.at[r, :], obs.at[r, :], obs_sems.at[part])

    for part in range(4):
        fetch(part).start()
    row, rank, first = assign_rows(count_ref[0], columns_ref[...])
    row_ref[...] = row
    rank_ref[...] = rank
    first_ref[...] = first.astype(jnp.int32)
    for part in range(4):
        fetch(part).wait()
        active_channels(part, pairs_ref, lambda r, lanes: obs[r, lanes].astype(f32), masked)
    write_sums(jnp.max(first).astype(jnp.int32), row_ref, masked, tile_buf, sum_hbm, sems)


def seen_kernel(first_ref, pairs_ref, row_ref, after_ref, sum_hbm, masked, tile_buf, sems):
    del after_ref
    for part in range(4):
        active_channels(part, pairs_ref, lambda r, lanes: 1.0, masked)
    write_sums(first_ref[GROUPS, 0], row_ref, masked, tile_buf, sum_hbm, sems)


ROW_COST = pl.CostEstimate(
    flops=2 * MAX_ROWS * CAP * CHAN, transcendentals=0, bytes_accessed=MAX_ROWS * CHAN * 4
)


SUM_SCRATCH = [
    pltpu.VMEM((CAP, CHAN), bf16),
    pltpu.VMEM((2, SUM_TILE, CHAN), f32),
    pltpu.SemaphoreType.DMA((2,)),
]


def row_sums(counts, columns, pairs, obs, after):
    anywhere = pl.BlockSpec(memory_space=pl.ANY)
    return pl.pallas_call(
        sums_kernel,
        in_specs=[
            pl.BlockSpec(memory_space=pltpu.SMEM),
            VMEM_SPEC,
            VMEM_SPEC,
            anywhere,
            anywhere,
        ],
        out_specs=[anywhere, VMEM_SPEC, VMEM_SPEC, VMEM_SPEC],
        scratch_shapes=[pltpu.VMEM((CAP, CHAN), bf16)]
        + SUM_SCRATCH
        + [pltpu.SemaphoreType.DMA((4,))],
        out_shape=[
            pltpu.HBM((MAX_ROWS, CHAN), f32),
            pltpu.HBM((1, CAP), jnp.int32),
            pltpu.HBM((16, GROUP), f32),
            pltpu.HBM((16, LANES), jnp.int32),
        ],
        compiler_params=params(24),
        cost_estimate=ROW_COST,
        name="row_sums",
    )(counts, in_hbm(columns), in_hbm(pairs), in_hbm(obs), in_hbm(after))


def row_seen(first, pairs, row, after):
    anywhere = pl.BlockSpec(memory_space=pl.ANY)
    return pl.pallas_call(
        seen_kernel,
        in_specs=[pl.BlockSpec(memory_space=pltpu.SMEM), VMEM_SPEC, VMEM_SPEC, anywhere],
        out_specs=anywhere,
        scratch_shapes=SUM_SCRATCH,
        out_shape=pltpu.HBM((MAX_ROWS, CHAN), f32),
        compiler_params=params(24),
        cost_estimate=ROW_COST,
        name="row_seen",
    )(in_hbm(first), in_hbm(pairs), in_hbm(row), in_hbm(after))


J_STEP = 16
X_ROWS = 16
PART = J_STEP * CLON


def silu_and_slope(v):
    half = 0.5 * v
    sig = 0.5 * jnp.tanh(half) + 0.5
    act = v * sig
    return act, sig + act - act * sig


def swap_blocks(v):
    lane = lax.broadcasted_iota(jnp.int32, v[0].shape, 1)
    v = list(v)
    for bit in range(4):
        gap = 1 << bit
        upper = (lane & (8 * gap)) != 0
        for s in range(N_LEV):
            if s & gap:
                continue
            a, b = v[s], v[s + gap]
            v[s] = jnp.where(upper, pltpu.roll(b, 8 * gap, 1), a)
            v[s + gap] = jnp.where(upper, b, pltpu.roll(a, LANES - 8 * gap, 1))
    return v


def network_kernel(
    first_hbm,
    inc_ref,
    back_hbm,
    rank_hbm,
    sum_hbm,
    seen_hbm,
    chan_ref,
    w_in_hbm,
    w_mid,
    w_out_hbm,
    grad_hbm,
    send_ref,
    first_ref,
    rank_ref,
    state,
    picks,
    packed,
    packed_grad,
    w_twice,
    w_last,
    back_buf,
    grads,
    sum_buf,
    seen_buf,
    sems,
    part_sems,
):
    def fetches(t, slot):
        r = pl.ds(pl.multiple_of(t * TILE, 8), TILE)
        return (
            pltpu.make_async_copy(sum_hbm.at[r, :], sum_buf.at[slot], sems.at[0, slot]),
            pltpu.make_async_copy(seen_hbm.at[r, :], seen_buf.at[slot], sems.at[1, slot]),
        )

    def part_copy(k, src, dst, jc):
        r = pl.ds(pl.multiple_of(jc * PART, PART), PART)
        return pltpu.make_async_copy(src.at[r, :], dst.at[r, :], part_sems.at[k, jc])

    ranks = [
        pltpu.make_async_copy(rank_hbm, rank_ref, part_sems.at[3, 0]),
        pltpu.make_async_copy(first_hbm, first_ref, part_sems.at[3, 1]),
    ]
    for fetch in ranks:
        fetch.start()
    for jc in range(CLAT // J_STEP):
        part_copy(0, back_hbm, back_buf, jc).start()
    weights = [
        pltpu.make_async_copy(w_in_hbm, w_twice.at[pl.ds(0, LEV), :], part_sems.at[2, 0]),
        pltpu.make_async_copy(w_in_hbm, w_twice.at[pl.ds(LEV, LEV), :], part_sems.at[2, 1]),
        pltpu.make_async_copy(w_out_hbm, w_last, part_sems.at[2, 2]),
    ]
    for fetch in weights:
        fetch.start()
    for fetch in fetches(0, 0):
        fetch.start()

    def turn(jc, _):
        lanes = pl.ds(pl.multiple_of(jc * LANES, LANES), LANES)
        for part in range(CLON // X_ROWS):
            x0 = part * X_ROWS
            v = [
                inc_ref[s * CLON + x0 : s * CLON + x0 + X_ROWS, lanes].astype(f32)
                for s in range(N_LEV)
            ]
            v = swap_blocks(v)
            for j in range(J_STEP):
                r = pl.ds(pl.multiple_of((jc * J_STEP + j) * CLON + x0, 16), X_ROWS)
                grads[r, :] = v[j]
        return 0

    lax.fori_loop(0, CLAT // J_STEP, turn, 0)
    for fetch in ranks:
        fetch.wait()
    total = first_ref[GROUPS, 0]
    tiles = (total + (TILE - 1)) // TILE
    row = lax.broadcasted_iota(jnp.int32, (GROUP, GROUP), 0).astype(f32)
    for g in range(GROUPS):
        picks[g] = jnp.where(row == rank_ref[g : g + 1, :], 1.0, 0.0).astype(bf16)
    for jc in range(CLAT // J_STEP):
        part_copy(0, back_hbm, back_buf, jc).wait()

    def to_state(i, _):
        r = pl.ds(pl.multiple_of(i * GROUP, GROUP), GROUP)
        grid_state = back_buf[r, :].astype(f32) + grads[r, :]
        high = grid_state.astype(bf16)
        state[r, :LEV] = high
        state[r, LEV:] = (grid_state - high.astype(f32)).astype(bf16)
        return 0

    lax.fori_loop(0, GROUPS, to_state, 0)

    def group_rows(g):
        first = pl.ds(pl.multiple_of(first_ref[g, 0], 8), GROUP)
        return first, slice(g * GROUP, (g + 1) * GROUP), picks[g]

    for g in range(GROUPS):
        rows, cells, pick = group_rows(g)
        packed[rows, :] = dot_nn(pick, state[cells, :])
    packed[pl.ds(pl.multiple_of(total, 8), TILE), :] = jnp.zeros((TILE, 2 * LEV), f32)

    for fetch in weights:
        fetch.wait()

    def one_tile(t, _):
        slot = lax.rem(t, 2)
        for fetch in fetches(t, slot):
            fetch.wait()

        @pl.when(t + 1 < tiles)
        def _():
            for fetch in fetches(t + 1, 1 - slot):
                fetch.start()

        r = pl.ds(pl.multiple_of(t * TILE, 8), TILE)
        act1, slope1 = silu_and_slope(dot_nn(packed[r, :].astype(bf16), w_twice[...]))
        act2, slope2 = silu_and_slope(dot_nn(act1.astype(bf16), w_mid[...]))
        evolved = dot_nn(act2.astype(bf16), w_last[...])
        misfit = (chan_ref[...] * (seen_buf[slot] * evolved - sum_buf[slot])).astype(bf16)
        back2 = (dot_nt(misfit, w_last[...]) * slope2).astype(bf16)
        back1 = (dot_nt(back2, w_mid[...]) * slope1).astype(bf16)
        packed_grad[r, :] = dot_nt(back1, w_twice[:LEV])
        return 0

    lax.fori_loop(0, tiles, one_tile, 0)
    packed_grad[pl.ds(pl.multiple_of(tiles * TILE, 8), GROUP), :] = jnp.zeros((GROUP, LEV), f32)
    for g in range(GROUPS):
        rows, cells, pick = group_rows(g)
        value = packed_grad[rows, :]
        high = value.astype(bf16)
        low = (value - high.astype(f32)).astype(bf16)
        value = dot_tn(pick, jnp.concatenate([high, low], axis=1))
        grads[cells, :] = value[:, :LEV] + value[:, LEV:]
        if (g + 1) * GROUP % PART == 0:
            part_copy(1, grads, grad_hbm, g * GROUP // PART).start()

    def to_send(jc, _):
        lanes = pl.ds(pl.multiple_of(jc * LANES, LANES), LANES)
        for part in range(CLON // X_ROWS):
            x0 = part * X_ROWS
            v = [
                grads[pl.ds(pl.multiple_of((jc * J_STEP + j) * CLON + x0, 16), X_ROWS), :]
                for j in range(J_STEP)
            ]
            v = swap_blocks(v)
            for s in range(N_LEV):
                send_ref[s * CLON + x0 : s * CLON + x0 + X_ROWS, lanes] = v[s].astype(bf16)
        return 0

    lax.fori_loop(0, CLAT // J_STEP, to_send, 0)
    for jc in range(CLAT // J_STEP):
        part_copy(1, grads, grad_hbm, jc).wait()


def network(first, inc, background, rank, sums, seen, channel_weight, w_in, w_mid, w_out):
    anywhere = pl.BlockSpec(memory_space=pl.ANY)
    grad, send = pl.pallas_call(
        network_kernel,
        in_specs=[
            anywhere,
            VMEM_SPEC,
            anywhere,
            anywhere,
            anywhere,
            anywhere,
            VMEM_SPEC,
            anywhere,
            VMEM_SPEC,
            anywhere,
        ],
        out_specs=[anywhere, VMEM_SPEC],
        out_shape=[
            pltpu.HBM((CELLS, LEV), f32),
            pltpu.VMEM((NLON, JL), bf16),
        ],
        scratch_shapes=[
            pltpu.SMEM((16, LANES), jnp.int32),
            pltpu.VMEM((16, GROUP), f32),
            pltpu.VMEM((CELLS, 2 * LEV), bf16),
            pltpu.VMEM((GROUPS, GROUP, GROUP), bf16),
            pltpu.VMEM((MAX_ROWS + GROUP, 2 * LEV), f32),
            pltpu.VMEM((MAX_ROWS + GROUP, LEV), f32),
            pltpu.VMEM((2 * LEV, w_in.shape[1]), bf16),
            pltpu.VMEM(w_out.shape, bf16),
            pltpu.VMEM((CELLS, LEV), bf16),
            pltpu.VMEM((CELLS, LEV), f32),
            pltpu.VMEM((2, TILE, CHAN), f32),
            pltpu.VMEM((2, TILE, CHAN), f32),
            pltpu.SemaphoreType.DMA((2, 2)),
            pltpu.SemaphoreType.DMA((4, 3)),
        ],
        compiler_params=params(30),
        name="network",
    )(
        in_hbm(first),
        inc,
        in_hbm(background),
        in_hbm(rank),
        in_hbm(sums),
        in_hbm(seen),
        channel_weight,
        in_hbm(w_in),
        on_chip(w_mid),
        in_hbm(w_out),
    )
    return grad.reshape(CLAT, CLON, LEV), send


def exchange(rows, axis):
    return on_chip(lax.all_to_all(rows, axis, split_axis=0, concat_axis=0, tiled=True))


def per_device(
    spectral,
    background,
    columns,
    counts,
    radiances,
    used_pairs,
    channel_weight,
    weight_in,
    weight_mid,
    weight_out,
):
    table = on_chip(wave_table())
    legendre, fourier = legendre_transform(spectral)
    sums, row, rank, first = row_sums(counts, columns, used_pairs, radiances[0], legendre)
    waves, token = waves_to_grid(exchange(fourier, "lat"), table, first)
    seen = row_seen(first, used_pairs, row, token)
    increment = exchange(waves, "lev")
    grid_grad, send = network(
        first,
        increment,
        background.reshape(CELLS, LEV),
        rank,
        sums,
        seen,
        channel_weight.reshape(1, CHAN),
        weight_in,
        weight_mid,
        weight_out,
    )
    coeff = exchange(grid_to_waves(exchange(send, "lev"), table), "lat")
    return (legendre_adjoint(legendre, coeff), grid_grad)


def solution(mesh):
    in_specs = (
        P(None, "lev", "lat", None),
        P("lat", "lev", None),
        P(("lat", "lev"), None),
        P(("lat", "lev")),
        P(("lat", "lev"), None, None),
        P(("lat", "lev"), None),
        P(),
        P(),
        P(),
        P(),
    )
    out_specs = (P(None, "lev", "lat", None), P("lat", "lev", None))
    return jax.shard_map(
        per_device, mesh=mesh, in_specs=in_specs, out_specs=out_specs, check_vma=False
    )
```

```python
import functools
import math

import jax
import jax.numpy as jnp
import numpy as np
from jax import lax
from jax.experimental import pallas as pl
from jax.experimental.pallas import tpu as pltpu
from jax.sharding import PartitionSpec as P

LEV = 128
M = 256
N = 256
NLAT = 384
NLON = 768
HALF = NLAT // 2
LANES = 128
N_LAT = 8
N_LEV = 16
ML = M // N_LAT
LL = LEV // N_LEV
CLAT = NLAT // N_LAT
CLON = NLON // N_LEV
CELLS = CLAT * CLON
CAP = 2048
CHAN = 512
JL = CLAT * LL
KM = 2 * M
M_PITCH = ML + 8
L_PITCH = 2 * ML + 8
ROWS = 2 * LL * ML

RESCALE_TOP = 2.0**30
RESCALE_BY = 2.0 ** (-60)
RESCALE_LOG = 60.0 * math.log(2.0)
HALF_LOG = 0.5 * math.log(0.5)

bf16 = jnp.bfloat16
f32 = jnp.float32


def params(mib):
    return pltpu.CompilerParams(vmem_limit_bytes=mib << 20)


def on_chip(array):
    return pltpu.with_memory_space_constraint(array, pltpu.VMEM)


def in_hbm(array):
    return pltpu.with_memory_space_constraint(array, pltpu.HBM)


VMEM_SPEC = pl.BlockSpec(memory_space=pltpu.VMEM)


def dot_nt(a, b):
    return lax.dot_general(a, b, (((1,), (1,)), ((), ())), preferred_element_type=f32)


def dot_tn(a, b):
    return lax.dot_general(a, b, (((0,), (0,)), ((), ())), preferred_element_type=f32)


def dot_nn(a, b):
    return jnp.dot(a, b, preferred_element_type=f32)


def wave_table():
    m = np.arange(M)
    phase = (np.arange(NLON)[:, None] * m[None, :] % NLON) * (2.0 * np.pi / NLON)
    weight = np.where(m == 0, 1.0, 2.0) / M
    pair = np.stack([weight * np.cos(phase), -weight * np.sin(phase)])
    table = pair.reshape(2, NLON, N_LAT, ML).transpose(1, 2, 0, 3).reshape(NLON, KM)
    return jnp.asarray(table, f32).astype(bf16)


M_STEP = 8
ADJOINT_STEP = 32


def legendre_kernel(
    spec_hbm, p_hbm, four_ref, spec_ref, table, waves, halves, p_buf, sems, spec_sem
):
    groups = range(ML // 8)

    fetch = pltpu.make_async_copy(spec_hbm, spec_ref, spec_sem)
    fetch.start()
    m0 = lax.axis_index("lat").astype(jnp.int32) * ML
    sub = lax.broadcasted_iota(jnp.int32, (8, LANES), 0)
    mf = [(sub + (m0 + 8 * g)).astype(f32) for g in groups]
    m2 = [v * v for v in mf]
    zero = jnp.zeros((8, LANES), f32)
    lanes = [lax.broadcasted_iota(jnp.int32, (8, LANES), 1) + h * LANES for h in (0, 1)]
    valid = [jnp.where(lanes[h] < HALF, 1.0, 0.0) for h in (0, 1)]
    colat = [
        (jnp.minimum(lanes[h], HALF - 1).astype(f32) + 0.5) * (math.pi / NLAT) for h in (0, 1)
    ]
    x = [jnp.cos(colat[h]) * valid[h] for h in (0, 1)]
    log_cos = [jnp.log(jnp.sin(colat[h])) for h in (0, 1)]
    k_ids = lax.broadcasted_iota(jnp.int32, (8, M), 1).astype(f32) + 1.0
    half_logs = 0.5 * jnp.log((2.0 * k_ids + 1.0) / (2.0 * k_ids))
    norm = [
        jnp.sum(jnp.where(k_ids <= mf[g][:, 0:1], half_logs, 0.0), axis=1, keepdims=True)
        for g in groups
    ]
    logs = [[HALF_LOG + norm[g] + mf[g] * log_cos[h] for h in (0, 1)] for g in groups]

    def block(i, carry):
        prev, earlier, logs, eps_prev, nf = carry
        big = [
            [jnp.maximum(jnp.abs(prev[g][h]), jnp.abs(earlier[g][h])) > RESCALE_TOP for h in (0, 1)]
            for g in groups
        ]
        shrink = [[jnp.where(big[g][h], RESCALE_BY, 1.0) for h in (0, 1)] for g in groups]
        prev = [[prev[g][h] * shrink[g][h] for h in (0, 1)] for g in groups]
        earlier = [[earlier[g][h] * shrink[g][h] for h in (0, 1)] for g in groups]
        logs = [
            [jnp.where(big[g][h], logs[g][h] + RESCALE_LOG, logs[g][h]) for h in (0, 1)]
            for g in groups
        ]
        scale = [[jnp.exp(logs[g][h]) * valid[h] for h in (0, 1)] for g in groups]
        for k in range(8):
            n2 = nf * nf
            inv = 1.0 / jnp.maximum(4.0 * n2 - 1.0, 1.0)
            at = pl.multiple_of((i * 8 + k) * M_PITCH, 8)
            new = []
            eps = []
            for g in groups:
                t = n2 - m2[g]
                q = jnp.maximum(t, 1.0) * inv
                a = lax.rsqrt(q)
                eps.append(jnp.where(t > 0.0, q * a, 0.0))
                diag = nf == mf[g]
                row = []
                for h in (0, 1):
                    cur = (x[h] * prev[g][h] - eps_prev[g] * earlier[g][h]) * a
                    cur = jnp.where(diag, 1.0, cur)
                    table[h, pl.ds(at + 8 * g, 8), :] = cur * scale[g][h]
                    row.append(cur)
                new.append(row)
            prev, earlier, eps_prev = new, prev, eps
            nf = nf + 1.0
        return prev, earlier, logs, eps_prev, nf

    empty = [[zero, zero] for _ in groups]
    lax.fori_loop(0, N // 8, block, (empty, empty, logs, [zero for _ in groups], zero))

    fetch.wait()
    for h in (0, 1):
        for k in range(2 * LL):
            halves[h, k * M_PITCH : k * M_PITCH + ML, :] = spec_ref[
                k * ML : (k + 1) * ML, h * LANES : (h + 1) * LANES
            ]
    lane = lax.broadcasted_iota(jnp.int32, (1, N), 1)
    alternate = jnp.where(lane % 2 == 0, 1.0, -1.0)
    def store(step):
        slot = lax.rem(step, 2)
        m = pl.ds(step * M_STEP, M_STEP)
        return pltpu.make_async_copy(p_buf.at[slot], p_hbm.at[m], sems.at[slot])

    def transform(step, _):
        slot = lax.rem(step, 2)

        @pl.when(step >= 2)
        def _():
            store(step - 2).wait()

        for k in range(M_STEP):
            m = step * M_STEP + k
            p_m = jnp.concatenate(
                [table[h, pl.ds(m, N, stride=M_PITCH), :].astype(bf16) for h in (0, 1)], axis=1
            )
            p_buf[slot, k] = p_m
            s = jnp.concatenate([halves[h, pl.ds(m, 2 * LL, stride=M_PITCH), :] for h in (0, 1)], axis=1)
            s = jnp.concatenate([s, s * (alternate if k % 2 == 0 else -alternate)], axis=0)
            high = s.astype(bf16)
            low = (s - high.astype(f32)).astype(bf16)
            out = dot_nn(jnp.concatenate([high, low], axis=0), p_m)
            out = out[: 4 * LL] + out[4 * LL :]
            for hemi in (0, 1):
                for c in (0, 1):
                    first = (hemi * 2 + c) * LL
                    for h in (0, 1):
                        waves[hemi, h, pl.ds(c * ML + m, LL, stride=L_PITCH), :] = out[
                            first : first + LL, h * LANES : (h + 1) * LANES
                        ]
        store(step).start()
        return 0

    steps = ML // M_STEP
    lax.fori_loop(0, steps, transform, 0)
    row = lax.broadcasted_iota(jnp.int32, (HALF, 256), 0)
    col = lax.broadcasted_iota(jnp.int32, (HALF, 256), 1)
    for hemi in (0, 1):
        pick = jnp.where(col == (row if hemi == 0 else HALF - 1 - row), 1.0, 0.0).astype(bf16)
        values = jnp.concatenate(
            [
                jnp.concatenate(
                    [
                        waves[hemi, h, l * L_PITCH : l * L_PITCH + 2 * ML, :].astype(bf16)
                        for h in (0, 1)
                    ],
                    axis=1,
                )
                for l in range(LL)
            ],
            axis=0,
        )
        four_ref[hemi * HALF : (hemi + 1) * HALF, :] = dot_nt(pick, values).astype(bf16)
    store(steps - 2).wait()
    store(steps - 1).wait()


def legendre_transform(spectral):
    return pl.pallas_call(
        legendre_kernel,
        in_specs=[pl.BlockSpec(memory_space=pl.ANY)],
        out_specs=[pl.BlockSpec(memory_space=pl.ANY), VMEM_SPEC],
        scratch_shapes=[
            pltpu.VMEM((ROWS, N), f32),
            pltpu.VMEM((2, N * M_PITCH, LANES), f32),
            pltpu.VMEM((2, 2, LL * L_PITCH, LANES), f32),
            pltpu.VMEM((2, 2 * LL * M_PITCH, LANES), f32),
            pltpu.VMEM((2, M_STEP, N, 256), bf16),
            pltpu.SemaphoreType.DMA((2,)),
            pltpu.SemaphoreType.DMA,
        ],
        out_shape=[
            pltpu.HBM((ML, N, 256), bf16),
            pltpu.VMEM((NLAT, ROWS), bf16),
        ],
        compiler_params=params(24),
        name="legendre",
    )(in_hbm(spectral.reshape(ROWS, N)))


def adjoint_kernel(p_ref, rows_ref, out_ref, folded, held):
    step = pl.program_id(0)

    @pl.when(step == 0)
    def _():
        j = lax.broadcasted_iota(jnp.int32, (NLAT, 256), 0)
        col = lax.broadcasted_iota(jnp.int32, (NLAT, 256), 1)
        north = jnp.where(col == j, 1.0, 0.0)
        south = jnp.where((j >= HALF) & (col == NLAT - 1 - j), 1.0, 0.0)
        north = jnp.where(col < HALF, north, 0.0)
        for part, pick in ((0, north + south), (1, north - south)):
            value = dot_tn(rows_ref[...], pick.astype(bf16))
            for h in (0, 1):
                for l in range(LL):
                    folded[part, h, l * L_PITCH : l * L_PITCH + 2 * ML, :] = value[
                        l * 2 * ML : (l + 1) * 2 * ML, h * LANES : (h + 1) * LANES
                    ]

    lane = lax.broadcasted_iota(jnp.int32, (2 * LL, N), 1)
    for k in range(ADJOINT_STEP):
        m = step * ADJOINT_STEP + k
        pieces = []
        for part in (0, 1):
            for c in (0, 1):
                pieces.append(
                    jnp.concatenate(
                        [
                            folded[part, h, pl.ds(c * ML + m, LL, stride=L_PITCH), :]
                            for h in (0, 1)
                        ],
                        axis=1,
                    )
                )
        value = dot_nt(jnp.concatenate(pieces, axis=0).astype(bf16), p_ref[m])
        picked = jnp.where(lane % 2 == k % 2, value[: 2 * LL], value[2 * LL :])
        for h in (0, 1):
            held[h, pl.ds(m, 2 * LL, stride=M_PITCH), :] = picked[:, h * LANES : (h + 1) * LANES]

    @pl.when(step == pl.num_programs(0) - 1)
    def _():
        for h in (0, 1):
            for k in range(2 * LL):
                out_ref[k * ML : (k + 1) * ML, h * LANES : (h + 1) * LANES] = held[
                    h, k * M_PITCH : k * M_PITCH + ML, :
                ]


def legendre_adjoint(table, rows):
    whole = lambda shape: pl.BlockSpec(shape, lambda i: (0,) * len(shape))
    out = pl.pallas_call(
        adjoint_kernel,
        grid=(ML // ADJOINT_STEP,),
        in_specs=[
            VMEM_SPEC,
            VMEM_SPEC,
        ],
        out_specs=whole((ROWS, N)),
        scratch_shapes=[
            pltpu.VMEM((2, 2, LL * L_PITCH, LANES), f32),
            pltpu.VMEM((2, 2 * LL * M_PITCH, LANES), f32),
        ],
        out_shape=jax.ShapeDtypeStruct((ROWS, N), f32),
        compiler_params=params(12),
        name="legendre_adjoint",
    )(on_chip(table), rows)
    return out.reshape(2, LL, ML, N)


def waves_kernel(rows_ref, table_ref, after_ref, out_ref, token_ref, held):
    del after_ref
    token_ref[...] = jnp.zeros_like(token_ref)
    for pair in range(N_LAT // 2):
        for l in range(LL):
            pieces = [
                rows_ref[(2 * pair + k) * CLAT : (2 * pair + k + 1) * CLAT, l * 64 : (l + 1) * 64]
                for k in (0, 1)
            ]
            held[pair, pl.ds(l, CLAT, stride=LL), :] = jnp.concatenate(pieces, axis=1).astype(f32)
    waves = jnp.concatenate([held[k].astype(bf16) for k in range(N_LAT // 2)], axis=1)
    out_ref[...] = dot_nt(table_ref[...], waves).astype(bf16)


def waves_to_grid(rows, table, after):
    return pl.pallas_call(
        waves_kernel,
        in_specs=[VMEM_SPEC, VMEM_SPEC, pl.BlockSpec(memory_space=pl.ANY)],
        out_shape=[pltpu.VMEM((NLON, JL), bf16), pltpu.HBM((8, LANES), f32)],
        out_specs=[VMEM_SPEC, VMEM_SPEC],
        scratch_shapes=[pltpu.VMEM((N_LAT // 2, JL, LANES), f32)],
        compiler_params=params(12),
        name="waves",
    )(rows, table, in_hbm(after))


def waves_adjoint_kernel(grid_ref, table_ref, out_ref, held):
    value = dot_tn(grid_ref[...], table_ref[...])
    for k in range(N_LAT // 2):
        held[k] = value[:, k * LANES : (k + 1) * LANES]
    for pair in range(N_LAT // 2):
        for lp in range(LL // 2):
            two = [held[pair, pl.ds(2 * lp + k, CLAT, stride=LL), :] for k in (0, 1)]
            for k in (0, 1):
                piece = jnp.concatenate([v[:, k * 64 : (k + 1) * 64] for v in two], axis=1)
                first = (2 * pair + k) * CLAT
                out_ref[first : first + CLAT, lp * LANES : (lp + 1) * LANES] = piece.astype(bf16)


def grid_to_waves(grid, table):
    return pl.pallas_call(
        waves_adjoint_kernel,
        in_specs=[VMEM_SPEC, VMEM_SPEC],
        out_shape=pltpu.VMEM((NLAT, ROWS), bf16),
        out_specs=VMEM_SPEC,
        scratch_shapes=[pltpu.VMEM((N_LAT // 2, JL, LANES), f32)],
        compiler_params=params(12),
        name="waves_adjoint",
    )(grid, table)


GROUP = 256
GROUPS = CELLS // GROUP
TILE = 240
SUM_TILE = 2 * TILE
QUARTER = CAP // 4
ROW_TILES = -(-(CAP + 7 * GROUPS) // SUM_TILE)
MAX_ROWS = ROW_TILES * SUM_TILE


def assign_rows(count, columns):
    slot = lax.broadcasted_iota(jnp.int32, (1, CAP), 1)
    valid = slot < count
    group = jnp.where(valid, lax.shift_right_logical(columns, 8), -1)
    inner = lax.broadcasted_iota(jnp.int32, (GROUP, CAP), 0) == (columns & (GROUP - 1))
    inner = jnp.where(inner, 1.0, 0.0).astype(bf16)
    in_group = lax.broadcasted_iota(jnp.int32, (16, CAP), 0) == group
    seen = dot_nt(jnp.where(in_group, 1.0, 0.0).astype(bf16), inner)
    used = jnp.where(seen > 0.5, 1.0, 0.0)
    before = lax.broadcasted_iota(jnp.int32, (GROUP, GROUP), 0) < lax.broadcasted_iota(
        jnp.int32, (GROUP, GROUP), 1
    )
    rank = dot_nn(used.astype(bf16), jnp.where(before, 1.0, 0.0).astype(bf16))
    padded = jnp.floor((jnp.sum(used, axis=1, keepdims=True) + 7.0) * 0.125) * 8.0
    padded = jnp.broadcast_to(padded, (16, LANES))
    sub = lax.broadcasted_iota(jnp.int32, (16, LANES), 0)
    first = jnp.zeros((16, LANES), f32)
    for g in range(GROUPS):
        first = first + jnp.where(sub > g, padded[g : g + 1, :], 0.0)
    of_slot = dot_nn(rank.astype(bf16), inner) + first[:, 0:1]
    row = jnp.sum(jnp.where(in_group, of_slot, 0.0), axis=0, keepdims=True)
    row = jnp.where(valid, row, -1.0).astype(jnp.int32)
    return row, jnp.where(used > 0.5, rank, -1.0), first


def write_sums(total, row_of_slot, masked, tile_buf, out_hbm, sems):
    tiles = (total + (SUM_TILE - 1)) // SUM_TILE

    def store(t):
        slot = lax.rem(t, 2)
        r = pl.ds(pl.multiple_of(t * SUM_TILE, 8), SUM_TILE)
        return pltpu.make_async_copy(tile_buf.at[slot], out_hbm.at[r, :], sems.at[slot])

    def one_tile(t, _):
        @pl.when(t >= 2)
        def _():
            store(t - 2).wait()

        row = lax.broadcasted_iota(jnp.int32, (SUM_TILE, CAP), 0) + t * SUM_TILE
        hit = jnp.where(row == row_of_slot[...], 1.0, 0.0).astype(bf16)
        tile_buf[lax.rem(t, 2)] = dot_nn(hit, masked[...])
        store(t).start()
        return 0

    lax.fori_loop(0, tiles, one_tile, 0)

    @pl.when(tiles >= 2)
    def _():
        store(tiles - 2).wait()

    store(tiles - 1).wait()


def active_channels(part, pairs_ref, value, masked):
    channel = lax.broadcasted_iota(jnp.int32, (LANES, LANES), 1)
    for i in range(part * QUARTER // LANES, (part + 1) * QUARTER // LANES):
        r = slice(i * LANES, (i + 1) * LANES)
        used = jnp.transpose(jnp.broadcast_to(2 * pairs_ref[:, r], (LANES, LANES)))
        for c in range(CHAN // LANES):
            lanes = slice(c * LANES, (c + 1) * LANES)
            masked[r, lanes] = jnp.where(
                channel + c * LANES < used, value(r, lanes), 0.0
            ).astype(bf16)


def sums_kernel(
    count_ref,
    columns_ref,
    pairs_ref,
    obs_hbm,
    after_ref,
    sum_hbm,
    row_hbm,
    rank_hbm,
    first_hbm,
    row_ref,
    rank_ref,
    first_ref,
    obs,
    masked,
    tile_buf,
    sems,
    obs_sems,
    small_sems,
):
    del after_ref

    def fetch(part):
        r = pl.ds(part * QUARTER, QUARTER)
        return pltpu.make_async_copy(obs_hbm.at[r, :], obs.at[r, :], obs_sems.at[part])

    for part in range(4):
        fetch(part).start()
    row, rank, first = assign_rows(count_ref[0], columns_ref[...])
    row_ref[...] = row
    rank_ref[...] = rank
    first_ref[...] = first.astype(jnp.int32)
    small = [
        pltpu.make_async_copy(row_ref, row_hbm, small_sems.at[0]),
        pltpu.make_async_copy(rank_ref, rank_hbm, small_sems.at[1]),
        pltpu.make_async_copy(first_ref, first_hbm, small_sems.at[2]),
    ]
    for store in small:
        store.start()
    for part in range(4):
        fetch(part).wait()
        active_channels(part, pairs_ref, lambda r, lanes: obs[r, lanes].astype(f32), masked)
    write_sums(jnp.max(first).astype(jnp.int32), row_ref, masked, tile_buf, sum_hbm, sems)
    for store in small:
        store.wait()


def seen_kernel(first_ref, pairs_ref, row_ref, after_ref, sum_hbm, masked, tile_buf, sems):
    del after_ref
    for part in range(4):
        active_channels(part, pairs_ref, lambda r, lanes: 1.0, masked)
    write_sums(first_ref[GROUPS, 0], row_ref, masked, tile_buf, sum_hbm, sems)


ROW_COST = pl.CostEstimate(
    flops=2 * MAX_ROWS * CAP * CHAN, transcendentals=0, bytes_accessed=MAX_ROWS * CHAN * 4
)


SUM_SCRATCH = [
    pltpu.VMEM((CAP, CHAN), bf16),
    pltpu.VMEM((2, SUM_TILE, CHAN), f32),
    pltpu.SemaphoreType.DMA((2,)),
]


def row_sums(counts, columns, pairs, obs, after):
    anywhere = pl.BlockSpec(memory_space=pl.ANY)
    return pl.pallas_call(
        sums_kernel,
        in_specs=[
            pl.BlockSpec(memory_space=pltpu.SMEM),
            VMEM_SPEC,
            VMEM_SPEC,
            anywhere,
            anywhere,
        ],
        out_specs=[anywhere] * 4,
        scratch_shapes=[
            pltpu.VMEM((1, CAP), jnp.int32),
            pltpu.VMEM((16, GROUP), f32),
            pltpu.VMEM((16, LANES), jnp.int32),
            pltpu.VMEM((CAP, CHAN), bf16),
        ]
        + SUM_SCRATCH
        + [pltpu.SemaphoreType.DMA((4,)), pltpu.SemaphoreType.DMA((3,))],
        out_shape=[
            pltpu.HBM((MAX_ROWS, CHAN), f32),
            pltpu.HBM((1, CAP), jnp.int32),
            pltpu.HBM((16, GROUP), f32),
            pltpu.HBM((16, LANES), jnp.int32),
        ],
        compiler_params=params(24),
        cost_estimate=ROW_COST,
        name="row_sums",
    )(counts, in_hbm(columns), in_hbm(pairs), in_hbm(obs), in_hbm(after))


def row_seen(first, pairs, row, after):
    anywhere = pl.BlockSpec(memory_space=pl.ANY)
    return pl.pallas_call(
        seen_kernel,
        in_specs=[pl.BlockSpec(memory_space=pltpu.SMEM), VMEM_SPEC, VMEM_SPEC, anywhere],
        out_specs=anywhere,
        scratch_shapes=SUM_SCRATCH,
        out_shape=pltpu.HBM((MAX_ROWS, CHAN), f32),
        compiler_params=params(24),
        cost_estimate=ROW_COST,
        name="row_seen",
    )(in_hbm(first), in_hbm(pairs), in_hbm(row), in_hbm(after))


J_STEP = 16
X_ROWS = 16
PART = J_STEP * CLON


def silu_and_slope(v):
    half = 0.5 * v
    sig = 0.5 * jnp.tanh(half) + 0.5
    act = v * sig
    return act, sig + act - act * sig


def swap_blocks(v):
    lane = lax.broadcasted_iota(jnp.int32, v[0].shape, 1)
    v = list(v)
    for bit in range(4):
        gap = 1 << bit
        upper = (lane & (8 * gap)) != 0
        for s in range(N_LEV):
            if s & gap:
                continue
            a, b = v[s], v[s + gap]
            v[s] = jnp.where(upper, pltpu.roll(b, 8 * gap, 1), a)
            v[s + gap] = jnp.where(upper, b, pltpu.roll(a, LANES - 8 * gap, 1))
    return v


def network_kernel(
    first_hbm,
    inc_ref,
    back_hbm,
    rank_hbm,
    sum_hbm,
    seen_hbm,
    chan_ref,
    w_in_hbm,
    w_mid,
    w_out_hbm,
    grad_hbm,
    send_ref,
    first_ref,
    rank_ref,
    state,
    picks,
    packed,
    packed_grad,
    w_twice,
    w_last,
    back_buf,
    grads,
    sum_buf,
    seen_buf,
    sems,
    part_sems,
):
    def fetches(t, slot):
        r = pl.ds(pl.multiple_of(t * TILE, 8), TILE)
        return (
            pltpu.make_async_copy(sum_hbm.at[r, :], sum_buf.at[slot], sems.at[0, slot]),
            pltpu.make_async_copy(seen_hbm.at[r, :], seen_buf.at[slot], sems.at[1, slot]),
        )

    def part_copy(k, src, dst, jc):
        r = pl.ds(pl.multiple_of(jc * PART, PART), PART)
        return pltpu.make_async_copy(src.at[r, :], dst.at[r, :], part_sems.at[k, jc])

    ranks = [
        pltpu.make_async_copy(rank_hbm, rank_ref, part_sems.at[3, 0]),
        pltpu.make_async_copy(first_hbm, first_ref, part_sems.at[3, 1]),
    ]
    for fetch in ranks:
        fetch.start()
    for jc in range(CLAT // J_STEP):
        part_copy(0, back_hbm, back_buf, jc).start()
    weights = [
        pltpu.make_async_copy(w_in_hbm, w_twice.at[pl.ds(0, LEV), :], part_sems.at[2, 0]),
        pltpu.make_async_copy(w_in_hbm, w_twice.at[pl.ds(LEV, LEV), :], part_sems.at[2, 1]),
        pltpu.make_async_copy(w_out_hbm, w_last, part_sems.at[2, 2]),
    ]
    for fetch in weights:
        fetch.start()
    for fetch in fetches(0, 0):
        fetch.start()

    def turn(jc, _):
        lanes = pl.ds(pl.multiple_of(jc * LANES, LANES), LANES)
        for part in range(CLON // X_ROWS):
            x0 = part * X_ROWS
            v = [
                inc_ref[s * CLON + x0 : s * CLON + x0 + X_ROWS, lanes].astype(f32)
                for s in range(N_LEV)
            ]
            v = swap_blocks(v)
            for j in range(J_STEP):
                r = pl.ds(pl.multiple_of((jc * J_STEP + j) * CLON + x0, 16), X_ROWS)
                grads[r, :] = v[j]
        return 0

    lax.fori_loop(0, CLAT // J_STEP, turn, 0)
    for fetch in ranks:
        fetch.wait()
    total = first_ref[GROUPS, 0]
    tiles = (total + (TILE - 1)) // TILE
    row = lax.broadcasted_iota(jnp.int32, (GROUP, GROUP), 0).astype(f32)
    for g in range(GROUPS):
        picks[g] = jnp.where(row == rank_ref[g : g + 1, :], 1.0, 0.0).astype(bf16)
    for jc in range(CLAT // J_STEP):
        part_copy(0, back_hbm, back_buf, jc).wait()

    def to_state(i, _):
        r = pl.ds(pl.multiple_of(i * GROUP, GROUP), GROUP)
        grid_state = back_buf[r, :].astype(f32) + grads[r, :]
        high = grid_state.astype(bf16)
        state[r, :LEV] = high
        state[r, LEV:] = (grid_state - high.astype(f32)).astype(bf16)
        return 0

    lax.fori_loop(0, GROUPS, to_state, 0)

    def group_rows(g):
        first = pl.ds(pl.multiple_of(first_ref[g, 0], 8), GROUP)
        return first, slice(g * GROUP, (g + 1) * GROUP), picks[g]

    for g in range(GROUPS):
        rows, cells, pick = group_rows(g)
        packed[rows, :] = dot_nn(pick, state[cells, :])
    packed[pl.ds(pl.multiple_of(total, 8), TILE), :] = jnp.zeros((TILE, 2 * LEV), f32)

    for fetch in weights:
        fetch.wait()

    def one_tile(t, _):
        slot = lax.rem(t, 2)
        for fetch in fetches(t, slot):
            fetch.wait()

        @pl.when(t + 1 < tiles)
        def _():
            for fetch in fetches(t + 1, 1 - slot):
                fetch.start()

        r = pl.ds(pl.multiple_of(t * TILE, 8), TILE)
        act1, slope1 = silu_and_slope(dot_nn(packed[r, :].astype(bf16), w_twice[...]))
        act2, slope2 = silu_and_slope(dot_nn(act1.astype(bf16), w_mid[...]))
        evolved = dot_nn(act2.astype(bf16), w_last[...])
        misfit = (chan_ref[...] * (seen_buf[slot] * evolved - sum_buf[slot])).astype(bf16)
        back2 = (dot_nt(misfit, w_last[...]) * slope2).astype(bf16)
        back1 = (dot_nt(back2, w_mid[...]) * slope1).astype(bf16)
        packed_grad[r, :] = dot_nt(back1, w_twice[:LEV])
        return 0

    lax.fori_loop(0, tiles, one_tile, 0)
    packed_grad[pl.ds(pl.multiple_of(tiles * TILE, 8), GROUP), :] = jnp.zeros((GROUP, LEV), f32)
    for g in range(GROUPS):
        rows, cells, pick = group_rows(g)
        value = packed_grad[rows, :]
        high = value.astype(bf16)
        low = (value - high.astype(f32)).astype(bf16)
        value = dot_tn(pick, jnp.concatenate([high, low], axis=1))
        grads[cells, :] = value[:, :LEV] + value[:, LEV:]
        if (g + 1) * GROUP % PART == 0:
            part_copy(1, grads, grad_hbm, g * GROUP // PART).start()

    def to_send(jc, _):
        lanes = pl.ds(pl.multiple_of(jc * LANES, LANES), LANES)
        for part in range(CLON // X_ROWS):
            x0 = part * X_ROWS
            v = [
                grads[pl.ds(pl.multiple_of((jc * J_STEP + j) * CLON + x0, 16), X_ROWS), :]
                for j in range(J_STEP)
            ]
            v = swap_blocks(v)
            for s in range(N_LEV):
                send_ref[s * CLON + x0 : s * CLON + x0 + X_ROWS, lanes] = v[s].astype(bf16)
        return 0

    lax.fori_loop(0, CLAT // J_STEP, to_send, 0)
    for jc in range(CLAT // J_STEP):
        part_copy(1, grads, grad_hbm, jc).wait()


def network(first, inc, background, rank, sums, seen, channel_weight, w_in, w_mid, w_out):
    anywhere = pl.BlockSpec(memory_space=pl.ANY)
    grad, send = pl.pallas_call(
        network_kernel,
        in_specs=[
            anywhere,
            VMEM_SPEC,
            anywhere,
            anywhere,
            anywhere,
            anywhere,
            VMEM_SPEC,
            anywhere,
            VMEM_SPEC,
            anywhere,
        ],
        out_specs=[anywhere, VMEM_SPEC],
        out_shape=[
            pltpu.HBM((CELLS, LEV), f32),
            pltpu.VMEM((NLON, JL), bf16),
        ],
        scratch_shapes=[
            pltpu.SMEM((16, LANES), jnp.int32),
            pltpu.VMEM((16, GROUP), f32),
            pltpu.VMEM((CELLS, 2 * LEV), bf16),
            pltpu.VMEM((GROUPS, GROUP, GROUP), bf16),
            pltpu.VMEM((MAX_ROWS + GROUP, 2 * LEV), f32),
            pltpu.VMEM((MAX_ROWS + GROUP, LEV), f32),
            pltpu.VMEM((2 * LEV, w_in.shape[1]), bf16),
            pltpu.VMEM(w_out.shape, bf16),
            pltpu.VMEM((CELLS, LEV), bf16),
            pltpu.VMEM((CELLS, LEV), f32),
            pltpu.VMEM((2, TILE, CHAN), f32),
            pltpu.VMEM((2, TILE, CHAN), f32),
            pltpu.SemaphoreType.DMA((2, 2)),
            pltpu.SemaphoreType.DMA((4, 3)),
        ],
        compiler_params=params(30),
        name="network",
    )(
        in_hbm(first),
        inc,
        in_hbm(background),
        in_hbm(rank),
        in_hbm(sums),
        in_hbm(seen),
        channel_weight,
        in_hbm(w_in),
        on_chip(w_mid),
        in_hbm(w_out),
    )
    return grad.reshape(CLAT, CLON, LEV), send


def exchange(rows, axis):
    return on_chip(lax.all_to_all(rows, axis, split_axis=0, concat_axis=0, tiled=True))


def per_device(
    spectral,
    background,
    columns,
    counts,
    radiances,
    used_pairs,
    channel_weight,
    weight_in,
    weight_mid,
    weight_out,
):
    table = on_chip(wave_table())
    legendre, fourier = legendre_transform(spectral)
    sums, row, rank, first = row_sums(counts, columns, used_pairs, radiances[0], legendre)
    waves, token = waves_to_grid(exchange(fourier, "lat"), table, first)
    seen = row_seen(first, used_pairs, row, token)
    increment = exchange(waves, "lev")
    grid_grad, send = network(
        first,
        increment,
        background.reshape(CELLS, LEV),
        rank,
        sums,
        seen,
        channel_weight.reshape(1, CHAN),
        weight_in,
        weight_mid,
        weight_out,
    )
    coeff = exchange(grid_to_waves(exchange(send, "lev"), table), "lat")
    return (legendre_adjoint(legendre, coeff), grid_grad)


def solution(mesh):
    in_specs = (
        P(None, "lev", "lat", None),
        P("lat", "lev", None),
        P(("lat", "lev"), None),
        P(("lat", "lev")),
        P(("lat", "lev"), None, None),
        P(("lat", "lev"), None),
        P(),
        P(),
        P(),
        P(),
    )
    out_specs = (P(None, "lev", "lat", None), P("lat", "lev", None))
    return jax.shard_map(
        per_device, mesh=mesh, in_specs=in_specs, out_specs=out_specs, check_vma=False
    )
```
